32 devices in a mesh: fsdp: 4 (over x, core), context: 2 (over y), tensor: 4 (over z).
Axes of the slice: x: 2, y: 2, z: 4, core: 2. Of those that a mesh axis runs over, the one named last changes fastest.
Arguments:
- tokens: bfloat16 [8192, 1024], P(('fsdp', 'context')), may hold values from -6 to 6
- cotangent: bfloat16 [8192, 1024], P(('fsdp', 'context')), may hold values from -6 to 6
- segments: int32 [8192], P(('fsdp', 'context')), may hold values from 0 to 3, as said below
- positions: int32 [8192], P(('fsdp', 'context')), may hold values from 0 to 1535, as said below
- parents: int32 [4, 4], P('fsdp'), may hold values from 0 to 3, as said below
- block_lists: int32 [16, 3], P(('fsdp', 'context')), may hold values from -1 to 3, as said below
- project_weight: bfloat16 [1024, 3, 1024], P('fsdp', None, 'tensor'), may hold values from -0.1875 to 0.1875
- project_bias: float32 [3, 1024], P(None, 'tensor'), may hold values from -3 to 3
- dense_weight: bfloat16 [1024, 1024], P('tensor', 'fsdp'), may hold values from -3 to 3
- dense_bias: float32 [1024], replicated, may hold values from -3 to 3
- up_weight: bfloat16 [1024, 4096], P('fsdp', 'tensor'), may hold values from -0.1875 to 0.1875
- up_bias: float32 [4096], P('tensor'), may hold values from -3 to 3
- down_weight: bfloat16 [4096, 1024], P('tensor', 'fsdp'), may hold values from -0.09375 to 0.09375
- down_bias: float32 [1024], replicated, may hold values from -3 to 3
- first_gain: float32 [1024], replicated, may hold values from 0.1 to 1.9
- first_shift: float32 [1024], replicated, may hold values from -3 to 3
- second_gain: float32 [1024], replicated, may hold values from 0.1 to 1.9
- second_shift: float32 [1024], replicated, may hold values from -3 to 3
Outputs:
- layer_out: bfloat16 [8192, 1024], P(('fsdp', 'context'))
- tokens_grad: bfloat16 [8192, 1024], P(('fsdp', 'context'))
- project_weight_grad: float32 [1024, 3, 1024], P('fsdp', None, 'tensor')
- project_bias_grad: float32 [3, 1024], P(None, 'tensor')
- dense_weight_grad: float32 [1024, 1024], P('tensor', 'fsdp')
- dense_bias_grad: float32 [1024], replicated
- up_weight_grad: float32 [1024, 4096], P('fsdp', 'tensor')
- up_bias_grad: float32 [4096], P('tensor')
- down_weight_grad: float32 [4096, 1024], P('tensor', 'fsdp')
- down_bias_grad: float32 [1024], replicated
- first_gain_grad: float32 [1024], replicated
- first_shift_grad: float32 [1024], replicated
- second_gain_grad: float32 [1024], replicated
- second_shift_grad: float32 [1024], replicated
The draws below stay inside these ranges and needn't reach their ends.
Inputs may be any that keep to these rules, and one draw needn't show every extreme that they name: `segments`: every aligned block of 512 tokens lies in one segment; a tree has one trunk of 1 block, 1 branches and 2 leaves of one block each, its blocks in any order. The trunk's blocks hold positions 0 to 511, a branch's block starts at 512, a leaf's at 1024; within a block positions rise by one. `parents`: the trunk is its own parent, each branch's parent is the trunk, each leaf's parent a branch, each branch the parent of two leaves. `block_lists`: each row holds its own block and every block of the segments above it on its path, each once in some order, then -1 to the end; a listed block other than its own lies wholly in an ancestor segment with smaller positions.
All inputs are finite; a program needn't handle non-finite values.
Results may differ from the reference program's by a relative error of at most 0.012.
The reference program's roundings to bfloat16 on the way count: a program that leaves them out, or rounds other values in their place, can miss the bound.
Values may be sent and summed in bfloat16 or wider, within the bound.
No kernel may reach another device: no remote copies, remote signals or barrier semaphores. Data moves between devices by JAX's collectives and lax.ppermute only.
A program may use at most 128 MiB of HBM per device.

```python
import jax
import jax.numpy as jnp
from jax import lax

D = 1024
HEADS = 16
HD = 64
FF = 4096
ROT = 16
BLK = 512
NB = 4
TREE = 2048
TREES = 4
TOKENS = 8192
BRANCHES = 1
NSEG = 4
TRUNK = 1
MAXK = 3


def tree_layout(key):
    base_key = jax.random.fold_in(key, 7)

    def one_tree(tree_index):
        tree_key = jax.random.fold_in(base_key, tree_index)
        order_key, label_key = jax.random.split(tree_key)
        canon_of_slot = jax.random.permutation(order_key, NB).astype(jnp.int32)
        labels = jax.random.permutation(label_key, NSEG).astype(jnp.int32)
        slot_of_canon = jnp.argsort(canon_of_slot).astype(jnp.int32)
        canonical = jnp.arange(NB, dtype=jnp.int32)
        in_trunk = canonical < TRUNK
        in_branch = (canonical >= TRUNK) & (canonical < TRUNK + BRANCHES)
        branch_of = jnp.where(in_branch, canonical - TRUNK, (canonical - TRUNK - BRANCHES) // 2)
        branch_of = jnp.clip(branch_of, 0, BRANCHES - 1)
        seg_index = jnp.where(in_trunk, 0, jnp.where(in_branch, 1 + branch_of, 1 + canonical - TRUNK))
        start_pos = jnp.where(in_trunk, canonical * BLK, jnp.where(in_branch, TRUNK * BLK, (TRUNK + 1) * BLK))
        column = jnp.arange(MAXK, dtype=jnp.int32)[None, :]
        canon_col = canonical[:, None]
        entry_trunk = jnp.where(column <= canon_col, column, -1)
        second_entry = jnp.where(in_branch[:, None], canon_col, TRUNK + branch_of[:, None])
        third_entry = jnp.where(in_branch[:, None], -1, canon_col)
        entry_other = jnp.where(column < TRUNK, column, jnp.where(column == TRUNK, second_entry, jnp.where(column == TRUNK + 1, third_entry, -1)))
        entries = jnp.where(in_trunk[:, None], entry_trunk, entry_other)
        listed = jnp.where(entries >= 0, slot_of_canon[jnp.maximum(entries, 0)], -1)
        seg_slot = labels[seg_index][canon_of_slot]
        start_slot = start_pos[canon_of_slot]
        lists_slot = listed[canon_of_slot]
        seg_ids = jnp.arange(NSEG, dtype=jnp.int32)
        parent_index = jnp.where(seg_ids <= BRANCHES, 0, 1 + (seg_ids - 1 - BRANCHES) // 2)
        parent_ids = jnp.zeros((NSEG,), jnp.int32).at[labels].set(labels[parent_index])
        token_segs = jnp.repeat(seg_slot, BLK)
        token_pos = (start_slot[:, None] + jnp.arange(BLK, dtype=jnp.int32)[None, :]).reshape(-1)
        return (token_segs, token_pos, parent_ids, lists_slot)
    return jax.vmap(one_tree)(jnp.arange(TREES, dtype=jnp.int32))


def draw_segments(key, part):
    return tree_layout(key)[0].reshape(TOKENS).astype(jnp.int32)


def draw_positions(key, part):
    return tree_layout(key)[1].reshape(TOKENS).astype(jnp.int32)


def draw_parents(key, part):
    return tree_layout(key)[2].reshape(TREES, NSEG).astype(jnp.int32)


def draw_block_lists(key, part):
    return tree_layout(key)[3].reshape(TREES * NB, MAXK).astype(jnp.int32)


def level_of(stream_key, shape, pieces, low, largest):
    gain = 1.0
    for position, blocks in pieces:
        heights = jax.random.uniform(jax.random.fold_in(jax.random.fold_in(stream_key, 6), position), (blocks,), jnp.float32, low / len(pieces), largest / len(pieces))
        gain = gain * jnp.repeat(jnp.exp(heights), shape[position] // blocks).reshape((-1,) + (1,) * (len(shape) - 1 - position))
    return gain


def noise(key, extent, spread, bound, cuts=(), held_as=jnp.bfloat16):
    values = spread * jax.random.normal(key, extent, jnp.float32)
    if cuts:
        values = values * level_of(key, extent, cuts, -0.22, 0.18)
    return jnp.clip(values, -bound, bound).astype(held_as)


def setup_inputs(seed: int = 0) -> dict:
    seeds = jax.random.split(jax.random.key(seed), 19)
    return {
        "tokens": noise(seeds[0], (TOKENS, D), 1.0, 6.0, ((0, 8),)),
        "cotangent": noise(seeds[1], (TOKENS, D), 1.0, 6.0, ((0, 8),)),
        "segments": draw_segments(jax.random.fold_in(seeds[18], 71), 0),
        "positions": draw_positions(jax.random.fold_in(seeds[18], 71), 0),
        "parents": draw_parents(jax.random.fold_in(seeds[18], 71), 0),
        "block_lists": draw_block_lists(jax.random.fold_in(seeds[18], 71), 0),
        "project_weight": noise(seeds[6], (D, 3, D), D ** -0.5, 0.1875, ((0, 4), (2, 4))),
        "project_bias": noise(seeds[7], (3, D), 0.5, 3.0, ((1, 4),), jnp.float32),
        "dense_weight": noise(seeds[8], (D, D), 4 ** -0.5, 3.0, ((0, 4), (1, 4))),
        "dense_bias": noise(seeds[9], (D,), 0.5, 3.0, (), jnp.float32),
        "up_weight": noise(seeds[10], (D, FF), D ** -0.5, 0.1875, ((0, 4), (1, 4))),
        "up_bias": noise(seeds[11], (FF,), 0.5, 3.0, ((0, 4),), jnp.float32),
        "down_weight": noise(seeds[12], (FF, D), FF ** -0.5, 0.09375, ((0, 4), (1, 4))),
        "down_bias": noise(seeds[13], (D,), 0.5, 3.0, (), jnp.float32),
        "first_gain": jnp.clip(1.0 + 0.18 * jax.random.normal(seeds[14], (D,), jnp.float32), 0.1, 1.9),
        "first_shift": noise(seeds[15], (D,), 0.5, 3.0, (), jnp.float32),
        "second_gain": jnp.clip(1.0 + 0.18 * jax.random.normal(seeds[16], (D,), jnp.float32), 0.1, 1.9),
        "second_shift": noise(seeds[17], (D,), 0.5, 3.0, (), jnp.float32),
    }


@jax.custom_vjp
def low(v):
    return lax.optimization_barrier(v.astype(jnp.bfloat16)).astype(jnp.float32)

@jax.custom_vjp
def low_back(v):
    return v

def low_keep(v):
    return (low(v), None)

def low_pass(kept, grad):
    return (grad,)

def back_keep(v):
    return (v, None)

def back_low(kept, grad):
    return (low(grad),)
low.defvjp(low_keep, low_pass)
low_back.defvjp(back_keep, back_low)
epsilon = 1e-05
masked = -1e+30
highest = lax.Precision.HIGHEST

def norm_layer(values_in, gain_row, shift_row):
    row_mean = lax.optimization_barrier(jnp.mean(values_in, axis=-1, keepdims=True))
    centered = values_in - row_mean
    variance = lax.optimization_barrier(jnp.mean(centered * centered, axis=-1, keepdims=True))
    return centered * lax.rsqrt(variance + epsilon) * gain_row + shift_row

def angles(path_pos):
    frequency = jnp.exp(-jnp.log(10000.0) * jnp.arange(ROT // 2, dtype=jnp.float32) * 2.0 / ROT)
    angle_rows = path_pos.astype(jnp.float32)[:, None] * frequency[None, :]
    return (jnp.cos(angle_rows), jnp.sin(angle_rows))

def rotate(values_in, cos_rows, sin_rows):
    rot_half = ROT // 2
    lower_part = values_in[..., :rot_half]
    upper_part = values_in[..., rot_half:ROT]
    cos_part = cos_rows[:, None, :]
    sin_part = sin_rows[:, None, :]
    return jnp.concatenate([lower_part * cos_part - upper_part * sin_part, upper_part * cos_part + lower_part * sin_part, values_in[..., ROT:]], axis=-1)

def attend_tree(inputs):
    queries, key_rows, value_rows, segment_ids, path_pos, parent_ids, listing = inputs
    key_block_ids = jnp.arange(TREE, dtype=jnp.int32) // BLK

    def attend_block(block_inputs):
        query_block, query_segs, query_pos, allowed = block_inputs
        scores = jnp.einsum('qhd,khd->hqk', query_block, key_rows, precision=highest) * HD ** (-0.5)
        scores = low_back(scores)
        listed = jnp.any(allowed[:, None] == key_block_ids[None, :], axis=0)
        parent_one = parent_ids[query_segs]
        parent_two = parent_ids[parent_one]
        ancestor = (segment_ids[None, :] == query_segs[:, None]) | (segment_ids[None, :] == parent_one[:, None]) | (segment_ids[None, :] == parent_two[:, None])
        visible = listed[None, :] & ancestor & (path_pos[None, :] <= query_pos[:, None])
        scores = jnp.where(visible[None], scores, masked)
        row_top = lax.optimization_barrier(jnp.max(scores, axis=-1, keepdims=True))
        exponent = jnp.exp(scores - row_top)
        probability = low(exponent / lax.optimization_barrier(jnp.sum(exponent, axis=-1, keepdims=True)))
        return jnp.einsum('hqk,khd->qhd', probability, value_rows, precision=highest)
    blocks = lax.map(jax.checkpoint(attend_block), (queries.reshape(NB, BLK, HEADS, HD), segment_ids.reshape(NB, BLK), path_pos.reshape(NB, BLK), listing))
    return blocks.reshape(TREE, HEADS, HD)

def forward(inputs, project_weight, project_bias, dense_weight, dense_bias, up_weight, up_bias, down_weight, down_bias, first_gain, first_shift, second_gain, second_shift, integers):
    segments, positions, parents, block_lists = integers
    normed_one = low(norm_layer(inputs, first_gain, first_shift))
    normed_two = low(norm_layer(inputs, second_gain, second_shift))
    projected = low_back(jnp.einsum('td,dcj->tcj', normed_one, project_weight, precision=highest) + project_bias[None])
    cos_rows, sin_rows = angles(positions)
    queries = low(rotate(projected[:, 0].reshape(TOKENS, HEADS, HD), cos_rows, sin_rows))
    key_rows = low(rotate(projected[:, 1].reshape(TOKENS, HEADS, HD), cos_rows, sin_rows))
    value_rows = low(projected[:, 2].reshape(TOKENS, HEADS, HD))
    context_rows = lax.map(attend_tree, (queries.reshape(TREES, TREE, HEADS, HD), key_rows.reshape(TREES, TREE, HEADS, HD), value_rows.reshape(TREES, TREE, HEADS, HD), segments.reshape(TREES, TREE), positions.reshape(TREES, TREE), parents, block_lists.reshape(TREES, NB, MAXK)))
    context_rows = low(low_back(context_rows.reshape(TOKENS, D)))
    attention_out = jnp.dot(context_rows, dense_weight, precision=highest) + dense_bias
    hidden = low_back(jnp.dot(normed_two, up_weight, precision=highest) + up_bias)
    activated = low(jax.nn.gelu(hidden, approximate=False))
    mlp_out = jnp.dot(activated, down_weight, precision=highest) + down_bias
    return inputs + attention_out + mlp_out

def reference(tokens, cotangent, segments, positions, parents, block_lists, project_weight, project_bias, dense_weight, dense_bias, up_weight, up_bias, down_weight, down_bias, first_gain, first_shift, second_gain, second_shift):
    integers = (segments, positions, parents, block_lists)
    floats = [tokens, project_weight, project_bias, dense_weight, dense_bias, up_weight, up_bias, down_weight, down_bias, first_gain, first_shift, second_gain, second_shift]
    floats = [item.astype(jnp.float32) for item in floats]

    def layer(*params):
        return forward(*params, integers)
    result, pull_back = jax.vjp(layer, *floats)
    gradients = pull_back(cotangent.astype(jnp.float32))
    return (result.astype(jnp.bfloat16), gradients[0].astype(jnp.bfloat16), gradients[1], gradients[2], gradients[3], gradients[4], gradients[5], gradients[6], gradients[7], gradients[8], gradients[9], gradients[10], gradients[11], gradients[12])
```

```python
from functools import partial

import jax
import jax.numpy as jnp
from jax import lax
from jax.experimental import pallas as pl
from jax.experimental.pallas import tpu as pltpu
from jax.sharding import PartitionSpec as P

HD = 64
ROT = 16
BLK = 512
PAIR = 2 * HD

epsilon = 1e-05
masked = -1e30
bf16 = jnp.bfloat16
f32 = jnp.float32
scale2 = HD ** (-0.5) * 1.4426950408889634
NT = (((1,), (1,)), ((), ()))
NN = (((1,), (0,)), ((), ()))
TN = (((0,), (0,)), ((), ()))


def dot(a, b, dims):
    return lax.dot_general(a, b, dims, preferred_element_type=f32)


def params(**kw):
    return pltpu.CompilerParams(vmem_limit_bytes=56 * 1024 * 1024, **kw)


def whole(shape):
    return pl.BlockSpec(shape, lambda *_: (0,) * len(shape))


smem = pl.BlockSpec(memory_space=pltpu.SMEM)


def norm_rows(x):
    mean = jnp.mean(x, axis=-1, keepdims=True)
    centered = x - mean
    variance = jnp.mean(centered * centered, axis=-1, keepdims=True)
    factor = lax.rsqrt(variance + epsilon)
    return centered * factor, factor


def rotate_lanes(x, cos, low_sin, high_sin, sign):
    left = pltpu.roll(x, PAIR - ROT // 2, 1)
    right = pltpu.roll(x, ROT // 2, 1)
    return x * cos + sign * (left * low_sin + right * high_sin)


def columns(index, width):
    return pl.ds(pl.multiple_of(index * width, width), width)


def project_kernel(ids, n1, w0, w1, w2, w3, bias, cos, lows, highs, q0, q1, kv0, kv1):
    weights = (w0, w1, w2, w3)
    width = w0.shape[2]
    depth = w0.shape[1]
    outs = ((q0, q1), (kv0, kv1))
    for part in range(3):
        total = bias[part : part + 1, :] + jnp.zeros((n1.shape[0], width), f32)
        for piece in range(4):
            total += dot(n1[:, columns(ids[piece], depth)], weights[piece][part], NN)
        for pair in range(2):
            half = total[:, pair * PAIR : (pair + 1) * PAIR]
            if part < 2:
                half = rotate_lanes(half, cos[...], lows[...], highs[...], 1.0)
            if part == 0:
                outs[0][pair][...] = half.astype(bf16)
            else:
                outs[1][pair][:, (part - 1) * PAIR : part * PAIR] = half.astype(bf16)


def project(ids, n1, weights, bias, tables, tile=256):
    rows = n1.shape[0]
    row = lambda w: pl.BlockSpec((tile, w), lambda i: (i, 0))
    return pl.pallas_call(
        project_kernel,
        grid=(rows // tile,),
        in_specs=[smem, row(n1.shape[1])]
        + [whole(w.shape) for w in weights]
        + [whole(bias.shape)]
        + [row(PAIR)] * 3,
        out_specs=[row(PAIR)] * 2 + [row(2 * PAIR)] * 2,
        out_shape=[jax.ShapeDtypeStruct((rows, PAIR), bf16)] * 2
        + [jax.ShapeDtypeStruct((rows, 2 * PAIR), bf16)] * 2,
        compiler_params=params(),
        name="project",
    )(ids, n1, *weights, bias, *tables)


def head_lanes(shape, head):
    return lax.broadcasted_iota(jnp.int32, shape, 1) // HD == head


def load_keys(kvs, kv_scr):
    start = 0
    for part in kvs:
        count = part.shape[0] // BLK
        for block in range(count):
            kv_scr[start + block] = part[block * BLK : (block + 1) * BLK, :]
        start += count


def attend_forward_kernel(slots, maxk, ids, q, *refs):
    parts = refs[: -6]
    o, lse, kv, turned, state, acc = refs[-6:]
    load_keys(parts, kv)
    for slot in range(slots):
        turned[slot] = kv[slot][:, PAIR:].T
    for block in range(q.shape[0] // BLK):
        own = ids[0] + block
        for head in range(2):
            rows = slice(head * HD, (head + 1) * HD)
            query = q[block * BLK : (block + 1) * BLK, :]
            query = jnp.where(head_lanes(query.shape, head), query, jnp.zeros_like(query))

            scores = dot(kv[own][:, :PAIR], query, NT) * scale2
            keep = lax.broadcasted_iota(jnp.int32, scores.shape, 0) <= lax.broadcasted_iota(
                jnp.int32, scores.shape, 1
            )
            scores = jnp.where(keep, scores, masked)
            top = jnp.max(scores, axis=0, keepdims=True)
            weight = jnp.exp2(scores - top)
            state[0:1, :] = top
            state[1:2, :] = jnp.sum(weight, axis=0, keepdims=True)
            acc[rows, :] = dot(turned[own][rows, :], weight.astype(bf16), NN)

            def entry(step, unused):
                slot = ids[2 + block * maxk + step]

                @pl.when((slot >= 0) & (slot != own))
                def _():
                    scores = dot(kv[slot][:, :PAIR], query, NT) * scale2
                    old = state[0:1, :]
                    top = jnp.maximum(old, jnp.max(scores, axis=0, keepdims=True))
                    weight = jnp.exp2(scores - top)
                    shrink = jnp.exp2(old - top)
                    state[0:1, :] = top
                    state[1:2, :] = state[1:2, :] * shrink + jnp.sum(weight, axis=0, keepdims=True)
                    acc[rows, :] = acc[rows, :] * shrink + dot(
                        turned[slot][rows, :], weight.astype(bf16), NN
                    )

                return unused

            lax.fori_loop(0, maxk, entry, 0)
            line = block * 2 + head
            lse[line : line + 1, :] = state[0:1, :] + jnp.log2(state[1:2, :])
            acc[rows, :] = acc[rows, :] * (1.0 / state[1:2, :])
        o[block * BLK : (block + 1) * BLK, :] = acc[...].T


def attend_forward(ids, maxk, q, kvs):
    slots = sum(part.shape[0] for part in kvs) // BLK
    rows = q.shape[0]
    return pl.pallas_call(
        partial(attend_forward_kernel, slots, maxk),
        grid=(),
        in_specs=[smem] + [pl.BlockSpec(memory_space=pltpu.VMEM)] * (1 + len(kvs)),
        out_specs=[pl.BlockSpec(memory_space=pltpu.VMEM)] * 2,
        out_shape=[
            jax.ShapeDtypeStruct((rows, PAIR), f32),
            jax.ShapeDtypeStruct((8, BLK), f32),
        ],
        scratch_shapes=[
            pltpu.VMEM((slots, BLK, 2 * PAIR), bf16),
            pltpu.VMEM((slots, PAIR, BLK), bf16),
            pltpu.VMEM((8, BLK), f32),
            pltpu.VMEM((PAIR, BLK), f32),
        ],
        compiler_params=params(),
        name="attend_forward",
    )(ids, q, *kvs)


def attend_backward_kernel(slots, maxk, split, ids, q, g, o, lse, cos, lows, highs, *refs):
    outs = 2 if split else 1
    parts = refs[: -5 - outs]
    grads = refs[-5 - outs : -5]
    qg, kv, turned, acc, total = refs[-5:]
    load_keys(parts, kv)
    for slot in range(slots):
        turned[slot] = kv[slot][:, :PAIR].T
    total[...] = jnp.zeros_like(total)
    pick = (
        lax.broadcasted_iota(jnp.int32, (8, PAIR), 1) // HD
        == lax.broadcasted_iota(jnp.int32, (8, PAIR), 0)
    ).astype(f32)
    for block in range(q.shape[0] // BLK):
        own = ids[0] + block
        span = slice(block * BLK, (block + 1) * BLK)
        deltas = lax.dot_general(
            pick,
            o[span, :] * g[span, :].astype(f32),
            NT,
            preferred_element_type=f32,
            precision=lax.Precision.HIGHEST,
        )
        for head in range(2):
            rows = slice(head * HD, (head + 1) * HD)
            lanes = head_lanes((BLK, PAIR), head)
            query = q[span, :]
            query = jnp.where(lanes, query, jnp.zeros_like(query))
            grad = g[span, :]
            grad = jnp.where(lanes, grad, jnp.zeros_like(grad))
            line = block * 2 + head
            log_sum = lse[line : line + 1, :]
            delta = deltas[head : head + 1, :]

            def tile(slot, keep):
                scores = dot(kv[slot][:, :PAIR], query, NT) * scale2
                prob = jnp.exp2(scores - log_sum)
                if keep is not None:
                    prob = jnp.where(keep, prob, 0.0)
                prob_grad = dot(kv[slot][:, PAIR:], grad, NT)
                score_grad = (prob * (prob_grad - delta)).astype(bf16)
                total[slot, :, PAIR:] += dot(prob.astype(bf16), grad, NN)
                total[slot, :, :PAIR] += dot(score_grad, query, NN)
                return dot(turned[slot][rows, :], score_grad, NN)

            keep = lax.broadcasted_iota(jnp.int32, (BLK, BLK), 0) <= lax.broadcasted_iota(
                jnp.int32, (BLK, BLK), 1
            )
            acc[rows, :] = tile(own, keep)

            def entry(step, unused):
                slot = ids[2 + block * maxk + step]

                @pl.when((slot >= 0) & (slot != own))
                def _():
                    acc[rows, :] += tile(slot, None)

                return unused

            lax.fori_loop(0, maxk, entry, 0)
        grad_q = acc[...].T * (HD ** (-0.5))
        qg[span, :] = rotate_lanes(
            grad_q, cos[span, :], lows[span, :], highs[span, :], -1.0
        ).astype(bf16)
    start = 0
    for out in grads:
        count = out.shape[0] // BLK
        for block in range(count):
            out[block * BLK : (block + 1) * BLK, :] = total[start + block].astype(out.dtype)
        start += count


def attend_backward(ids, maxk, q, g, o, lse, tables, kvs):
    slots = sum(part.shape[0] for part in kvs) // BLK
    rows = q.shape[0]
    split = len(kvs) == 2
    shapes = [jax.ShapeDtypeStruct(kvs[0].shape, f32 if split else bf16)]
    if split:
        shapes.append(jax.ShapeDtypeStruct(kvs[1].shape, bf16))
    shapes.append(jax.ShapeDtypeStruct((rows, PAIR), bf16))
    vmem = pl.BlockSpec(memory_space=pltpu.VMEM)
    return pl.pallas_call(
        partial(attend_backward_kernel, slots, maxk, split),
        grid=(),
        in_specs=[smem] + [vmem] * (7 + len(kvs)),
        out_specs=[vmem] * len(shapes),
        out_shape=shapes,
        scratch_shapes=[
            pltpu.VMEM((slots, BLK, 2 * PAIR), bf16),
            pltpu.VMEM((slots, PAIR, BLK), bf16),
            pltpu.VMEM((PAIR, BLK), f32),
            pltpu.VMEM((slots, BLK, 2 * PAIR), f32),
        ],
        compiler_params=params(),
        name="attend_backward",
    )(ids, q, g, o, lse, *tables, *kvs)


def mlp_kernel(
    ids, x, cot, gain, shift, up_bias, u0, u1, u2, u3, d0, d1, d2, d3, c0, c1, c2, c3,
    n2, act, hid_grad, mlp, e2, g0, g1, up_sum, norm_sums,
):
    ups, downs, denses = (u0, u1, u2, u3), (d0, d1, d2, d3), (c0, c1, c2, c3)
    depth = u0.shape[0]
    step = pl.program_id(0)

    @pl.when(step == 0)
    def _():
        up_sum[...] = jnp.zeros_like(up_sum)
        norm_sums[...] = jnp.zeros_like(norm_sums)

    normal, _ = norm_rows(x[...].astype(f32))
    n2[...] = (normal * gain[...] + shift[...]).astype(bf16)
    hidden = up_bias[...] + jnp.zeros((x.shape[0], u0.shape[1]), f32)
    back = jnp.zeros((x.shape[0], u0.shape[1]), f32)
    context_grad = jnp.zeros((x.shape[0], c0.shape[0]), f32)
    for piece in range(4):
        where = columns(ids[piece], depth)
        hidden += dot(n2[:, where], ups[piece][...], NN)
        back += dot(cot[:, where], downs[piece][...], NT)
        context_grad += dot(cot[:, where], denses[piece][...], NT)
    g0[...] = context_grad[:, :PAIR].astype(bf16)
    g1[...] = context_grad[:, PAIR:].astype(bf16)
    cdf = 0.5 + 0.5 * lax.erf(hidden * (2.0 ** -0.5))
    pdf = jnp.exp(hidden * hidden * -0.5) * 0.3989422804014327
    act[...] = (hidden * cdf).astype(bf16)
    low = (back * (cdf + hidden * pdf)).astype(bf16)
    hid_grad[...] = low
    up_sum[...] += jnp.sum(low.astype(f32), axis=0, keepdims=True)
    for piece in range(4):
        where = columns(ids[piece], depth)
        mlp[:, where] = dot(act[...], downs[piece][...], NN)
        e2[:, where] = dot(low, ups[piece][...], NT)
    grad = e2[...]
    norm_sums[0:1, :] += jnp.sum(grad * normal, axis=0, keepdims=True)
    norm_sums[1:2, :] += jnp.sum(grad, axis=0, keepdims=True)
    e2[...] = grad * gain[...]


def mlp_all(ids, x, cot, gain, shift, up_bias, ups, downs, denses, tile=256):
    rows, width = x.shape
    units = up_bias.shape[1]
    row = lambda w: pl.BlockSpec((tile, w), lambda i: (i, 0))
    s = jax.ShapeDtypeStruct
    return pl.pallas_call(
        mlp_kernel,
        grid=(rows // tile,),
        in_specs=[smem, row(width), row(width)]
        + [whole(a.shape) for a in (gain, shift, up_bias, *ups, *downs, *denses)],
        out_specs=[
            row(width), row(units), row(units), row(width), row(width), row(PAIR), row(PAIR),
            whole((1, units)), whole((8, width)),
        ],
        out_shape=[
            s((rows, width), bf16), s((rows, units), bf16), s((rows, units), bf16),
            s((rows, width), f32), s((rows, width), f32), s((rows, PAIR), bf16),
            s((rows, PAIR), bf16), s((1, units), f32), s((8, width), f32),
        ],
        compiler_params=params(),
        name="mlp_all",
    )(ids, x, cot, gain, shift, up_bias, *ups, *downs, *denses)


def output_kernel(ids, o0, o1, mlp, c0, c1, c2, c3, out, ctx):
    width = c0.shape[1]
    ctx[:, :PAIR] = o0[...].astype(bf16)
    ctx[:, PAIR:] = o1[...].astype(bf16)
    for piece, weight in enumerate((c0, c1, c2, c3)):
        where = columns(ids[piece], width)
        out[:, where] = (mlp[:, where] + dot(ctx[...], weight[...], NN)).astype(bf16)


def output_part(ids, o0, o1, mlp, denses, tile=256):
    rows, width = mlp.shape
    row = lambda w: pl.BlockSpec((tile, w), lambda i: (i, 0))
    return pl.pallas_call(
        output_kernel,
        grid=(rows // tile,),
        in_specs=[smem, row(PAIR), row(PAIR), row(width)] + [whole(a.shape) for a in denses],
        out_specs=[row(width), row(2 * PAIR)],
        out_shape=[
            jax.ShapeDtypeStruct((rows, width), bf16),
            jax.ShapeDtypeStruct((rows, 2 * PAIR), bf16),
        ],
        compiler_params=params(),
        name="output_part",
    )(ids, o0, o1, mlp, *denses)


def input_grad_kernel(
    split, ids, x, e2, gain, qg0, qg1, cos, lows, highs, w0, w1, w2, w3, *refs
):
    grads, (pg, e, norm_sums, bias_sum, first) = refs[:-5], refs[-5:]
    weights = (w0, w1, w2, w3)
    depth = w0.shape[1]
    width = w0.shape[2]

    @pl.when(pl.program_id(0) == 0)
    def _():
        norm_sums[...] = jnp.zeros_like(norm_sums)
        bias_sum[...] = jnp.zeros_like(bias_sum)

    pg[:, 0:PAIR] = qg0[...]
    pg[:, PAIR : 2 * PAIR] = qg1[...]
    for pair in range(2):
        if split:
            own, other = grads[2 * pair : 2 * pair + 2]
            grad = own[...] + other[...].astype(f32)
        else:
            grad = grads[pair][...].astype(f32)
        key = rotate_lanes(
            grad[:, :PAIR] * (HD ** (-0.5)), cos[...], lows[...], highs[...], -1.0
        )
        at = width + pair * PAIR
        pg[:, at : at + PAIR] = key.astype(bf16)
        pg[:, at + width : at + width + PAIR] = grad[:, PAIR:].astype(bf16)
    bias_sum[...] += jnp.sum(pg[...].astype(f32), axis=0, keepdims=True)
    normal, _ = norm_rows(x[...].astype(f32))
    for piece in range(4):
        where = columns(ids[piece], depth)
        total = dot(pg[:, :width], weights[piece][0], NT)
        total += dot(pg[:, width : 2 * width], weights[piece][1], NT)
        total += dot(pg[:, 2 * width :], weights[piece][2], NT)
        first[:, where] = total
    grad = first[...]
    e[...] = (grad * gain[...] + e2[...]).astype(bf16)
    norm_sums[0:1, :] += jnp.sum(grad * normal, axis=0, keepdims=True)
    norm_sums[1:2, :] += jnp.sum(grad, axis=0, keepdims=True)


def input_grad(ids, x, e2, gain, qgs, tables, weights, grads, split, tile=256):
    rows, width = x.shape
    row = lambda w: pl.BlockSpec((tile, w), lambda i: (i, 0))
    s = jax.ShapeDtypeStruct
    units = 3 * weights[0].shape[2]
    return pl.pallas_call(
        partial(input_grad_kernel, split),
        grid=(rows // tile,),
        in_specs=[smem, row(width), row(width), whole(gain.shape), row(PAIR), row(PAIR)]
        + [row(PAIR)] * 3
        + [whole(w.shape) for w in weights]
        + [row(2 * PAIR)] * len(grads),
        out_specs=[row(units), row(width), whole((8, width)), whole((1, units))],
        out_shape=[
            s((rows, units), bf16), s((rows, width), bf16), s((8, width), f32),
            s((1, units), f32),
        ],
        scratch_shapes=[pltpu.VMEM((tile, width), f32)],
        compiler_params=params(),
        name="input_grad",
    )(ids, x, e2, gain, *qgs, *tables, *weights, *grads)


def swap(values, axis, size, bit):
    pairs = [(i, i ^ bit) for i in range(size)]
    return jax.tree.map(lambda v: lax.ppermute(v, axis, pairs), values)


def sum_all(value, axes):
    for axis, size in axes:
        bit = 1
        while bit < size:
            value = value + swap(value, axis, size, bit)
            bit *= 2
    return value


def pieces_of(shard):
    first = swap(shard, "fsdp", 4, 2)
    return (shard, swap(shard, "fsdp", 4, 1), first, swap(first, "fsdp", 4, 1))


def shard_of(grad, me, context):
    core, chip = me % 2, me // 2
    grad = grad.reshape((2, 2) + grad.shape[1:])
    pick = lambda a, i, d: lax.dynamic_index_in_dim(a, i, d, keepdims=False)
    kept, sent = pick(grad, core, 1), pick(grad, 1 - core, 1)
    got = swap(sent, "fsdp", 4, 1)
    grad = (kept.astype(f32) + got.astype(f32)).astype(bf16)
    kept, sent = pick(grad, chip, 0), pick(grad, 1 - chip, 0)
    got = swap(sent, "fsdp", 4, 2)
    grad = (kept.astype(f32) + got.astype(f32)).astype(bf16)
    if context == 2:
        return grad.astype(f32) + swap(grad, "context", 2, 1).astype(f32)
    return lax.psum(grad.astype(f32), "context")


def all_sum_rows(value, finish, chunks):
    size = value.shape[0] // chunks
    place = lax.axis_index("tensor")
    middle = (place == 1) | (place == 2)
    done = []
    for index in range(chunks):
        part = value[index * size : (index + 1) * size]
        got = lax.ppermute(part, "tensor", [(0, 1), (3, 2)])
        part = (part.astype(f32) + got.astype(f32)).astype(bf16)
        got = lax.ppermute(part, "tensor", [(1, 2), (2, 1)])
        final = finish(part.astype(f32) + got.astype(f32), index * size, size)
        got = lax.ppermute(final, "tensor", [(1, 0), (2, 3)])
        done.append(jnp.where(middle, final, got))
    return jnp.concatenate(done, axis=0)


def rotation_tables(positions):
    lane = jnp.arange(PAIR, dtype=jnp.int32) % HD
    half = ROT // 2
    frequency = jnp.exp(
        -jnp.log(10000.0) * (lane % half).astype(f32) * 2.0 / ROT
    )
    angle = positions.astype(f32)[:, None] * frequency[None, :]
    cos = jnp.where(lane < ROT, jnp.cos(angle), 1.0)
    sin = jnp.sin(angle)
    return (
        cos,
        jnp.where(lane < half, -sin, 0.0),
        jnp.where((lane >= half) & (lane < ROT), sin, 0.0),
    )


def body(
    contexts,
    tokens,
    cotangent,
    segments,
    positions,
    parents,
    block_lists,
    project_weight,
    project_bias,
    dense_weight,
    dense_bias,
    up_weight,
    up_bias,
    down_weight,
    down_bias,
    first_gain,
    first_shift,
    second_gain,
    second_shift,
):
    rows, width = tokens.shape
    blocks = rows // BLK
    maxk = block_lists.shape[1]
    me = lax.axis_index("fsdp")
    place = lax.axis_index("context")
    order = jnp.stack([me, me ^ 1, me ^ 2, me ^ 3]).astype(jnp.int32)
    split = contexts == 2
    slots = contexts * blocks
    first_slot = place * blocks
    if split:
        lists = jnp.where(block_lists >= 0, (block_lists - first_slot) % slots, -1)
        base = jnp.zeros((), jnp.int32)
    else:
        lists, base = block_lists, first_slot
    ids = jnp.concatenate(
        [jnp.stack([base, base]).astype(jnp.int32), lists.reshape(-1).astype(jnp.int32)]
    )

    projects = pieces_of(jnp.transpose(project_weight, (1, 0, 2)))
    denses = pieces_of(dense_weight)
    ups = pieces_of(up_weight)
    downs = pieces_of(down_weight)

    inputs = tokens.astype(f32)
    normal, factor = norm_rows(inputs)
    normed_one = (normal * first_gain + first_shift).astype(bf16)
    tables = rotation_tables(positions)
    q0, q1, kv0, kv1 = project(order, normed_one, projects, project_bias, tables)
    if split:
        keys = [(kv, swap(kv, "context", 2, 1)) for kv in (kv0, kv1)]
    else:
        keys = [(lax.all_gather(kv, "context", axis=0, tiled=True),) for kv in (kv0, kv1)]

    (
        normed_two, activated, hidden_grad, mlp_out, e2, g0, g1, up_sum, sums_two,
    ) = mlp_all(
        order, tokens, cotangent, second_gain[None], second_shift[None], up_bias[None],
        ups, downs, denses,
    )
    o0, lse0 = attend_forward(ids, maxk, q0, keys[0])
    o1, lse1 = attend_forward(ids, maxk, q1, keys[1])
    partial_out, context_low = output_part(order, o0, o1, mlp_out, denses)
    summed = lax.psum_scatter(partial_out, "tensor", scatter_dimension=0, tiled=True)
    quarter = summed.shape[0]
    mine = lax.dynamic_slice_in_dim(tokens, lax.axis_index("tensor") * quarter, quarter, 0)
    layer_out = (mine.astype(f32) + summed.astype(f32) + dense_bias + down_bias).astype(bf16)
    layer_out = lax.all_gather(layer_out, "tensor", axis=0, tiled=True)

    back0 = attend_backward(ids, maxk, q0, g0, o0, lse0, tables, keys[0])
    back1 = attend_backward(ids, maxk, q1, g1, o1, lse1, tables, keys[1])
    if split:
        grads = []
        for own, other, _ in (back0, back1):
            grads += [own, swap(other, "context", 2, 1)]
    else:
        grads = [
            lax.psum_scatter(whole_grad, "context", scatter_dimension=0, tiled=True)
            for whole_grad, _ in (back0, back1)
        ]
    projected_grad, e, sums_one, project_sum = input_grad(
        order, tokens, e2, first_gain[None], (back0[-1], back1[-1]), tables, projects, grads, split
    )

    upstream = cotangent.astype(f32)

    def finish(total, start, size):
        n = normal[start : start + size]
        r = factor[start : start + size]
        mean_e = jnp.mean(total, axis=-1, keepdims=True)
        mean_en = jnp.mean(total * n, axis=-1, keepdims=True)
        result = upstream[start : start + size] + r * (total - mean_e - n * mean_en)
        return result.astype(bf16)

    tokens_grad = all_sum_rows(e, finish, 4)

    product = lambda a, b: lax.dot_general(a, b, TN, preferred_element_type=f32).astype(bf16)
    up_grad = product(normed_two, hidden_grad).reshape(4, width // 4, -1)
    down_grad = product(activated, cotangent).reshape(-1, 4, width // 4).transpose(1, 0, 2)
    dense_grad = product(context_low, cotangent).reshape(-1, 4, width // 4).transpose(1, 0, 2)
    project_grad = product(normed_one, projected_grad).reshape(4, width // 4, -1)
    up_grad = shard_of(up_grad, me, contexts)
    down_grad = shard_of(down_grad, me, contexts)
    dense_grad = shard_of(dense_grad, me, contexts)
    project_grad = shard_of(project_grad, me, contexts)

    bias_total = jnp.sum(upstream, axis=0, keepdims=True)
    data = (("fsdp", 4), ("context", contexts))
    everything = sum_all(
        jnp.concatenate([up_sum, project_sum, bias_total, sums_one[:1], sums_one[1:2], sums_two[:1], sums_two[1:2]], axis=1),
        data,
    )
    units = up_bias.shape[0]
    third = project_sum.shape[1]
    up_total, project_total, bias_sum, norms = jnp.split(
        everything[0], [units, units + third, units + third + width]
    )
    norms = sum_all(norms.reshape(4, width), (("tensor", 4),))
    return (
        layer_out,
        tokens_grad,
        project_grad.reshape(width // 4, 3, -1),
        project_total.reshape(3, -1),
        dense_grad,
        bias_sum,
        up_grad,
        up_total,
        down_grad,
        bias_sum,
        norms[0],
        norms[1],
        norms[2],
        norms[3],
    )


def solution(mesh):
    tokens = P(("fsdp", "context"), None)
    line = P(("fsdp", "context"))
    in_specs = (
        tokens, tokens, line, line, P("fsdp", None), tokens,
        P("fsdp", None, "tensor"), P(None, "tensor"), P("tensor", "fsdp"), P(),
        P("fsdp", "tensor"), P("tensor"), P("tensor", "fsdp"), P(), P(), P(), P(), P(),
    )
    out_specs = (
        tokens, tokens, P("fsdp", None, "tensor"), P(None, "tensor"), P("tensor", "fsdp"), P(),
        P("fsdp", "tensor"), P("tensor"), P("tensor", "fsdp"), P(), P(), P(), P(), P(),
    )
    run = partial(body, mesh.shape["context"])
    return jax.shard_map(run, mesh=mesh, in_specs=in_specs, out_specs=out_specs, check_vma=False)
```

```python
from functools import partial

import jax
import jax.numpy as jnp
from jax import lax
from jax.experimental import pallas as pl
from jax.experimental.pallas import tpu as pltpu
from jax.sharding import PartitionSpec as P

HD = 64
ROT = 16
BLK = 512
PAIR = 2 * HD
SHARD = 256
EXTRA = 16

epsilon = 1e-05
masked = -1e30
bf16 = jnp.bfloat16
f32 = jnp.float32
scale2 = HD ** (-0.5) * 1.4426950408889634
NT = (((1,), (1,)), ((), ()))
NN = (((1,), (0,)), ((), ()))
TN = (((0,), (0,)), ((), ()))


def dot(a, b, dims):
    return lax.dot_general(a, b, dims, preferred_element_type=f32)


def params(mib):
    return pltpu.CompilerParams(vmem_limit_bytes=mib * 1024 * 1024)


SCALE = 1.0


def cost(micros):
    return pl.CostEstimate(
        flops=int(1.15e9 * micros * SCALE), bytes_accessed=int(3.7e6 * micros * SCALE), transcendentals=0
    )


def whole(shape):
    return pl.BlockSpec(shape, lambda *_: (0,) * len(shape))


smem = pl.BlockSpec(memory_space=pltpu.SMEM)


def norm_rows(x):
    mean = jnp.mean(x, axis=-1, keepdims=True)
    centered = x - mean
    variance = jnp.mean(centered * centered, axis=-1, keepdims=True)
    factor = lax.rsqrt(variance + epsilon)
    return centered * factor, factor


def rotate_lanes(x, cos, sin, sign):
    lane = lax.broadcasted_iota(jnp.int32, x.shape, 1) % HD
    left = pltpu.roll(x, PAIR - ROT // 2, 1)
    right = pltpu.roll(x, ROT // 2, 1)
    return x * cos + jnp.where(lane < ROT // 2, -sign * left, sign * right) * sin


def columns(index, width):
    return pl.ds(pl.multiple_of(index * width, width), width)


def project_kernel(ids, n1, w0, w1, w2, w3, bias, cos, sin, q0, q1, kv0, kv1):
    weights = (w0, w1, w2, w3)
    width = w0.shape[1]
    depth = w0.shape[0] // 3
    outs = ((q0, q1), (kv0, kv1))
    for part in range(3):
        total = bias[part : part + 1, :] + jnp.zeros((n1.shape[0], width), f32)
        for piece in range(4):
            total += dot(n1[:, columns(ids[piece], depth)], weights[piece][part * depth : (part + 1) * depth, :], NN)
        for pair in range(2):
            half = total[:, pair * PAIR : (pair + 1) * PAIR]
            if part < 2:
                half = rotate_lanes(half, cos[...], sin[...], 1.0)
            if part == 0:
                outs[0][pair][...] = half.astype(bf16)
            else:
                outs[1][pair][:, (part - 1) * PAIR : part * PAIR] = half.astype(bf16)


def project(ids, n1, weights, bias, tables, tile=256):
    rows = n1.shape[0]
    row = lambda w: pl.BlockSpec((tile, w), lambda i: (i, 0))
    return pl.pallas_call(
        project_kernel,
        grid=(rows // tile,),
        in_specs=[smem, row(n1.shape[1])]
        + [whole(w.shape) for w in weights]
        + [whole(bias.shape)]
        + [row(PAIR)] * 2,
        out_specs=[row(PAIR)] * 2 + [row(2 * PAIR)] * 2,
        out_shape=[jax.ShapeDtypeStruct((rows, PAIR), bf16)] * 2
        + [jax.ShapeDtypeStruct((rows, 2 * PAIR), bf16)] * 2,
        compiler_params=params(16),
        cost_estimate=cost(4.3),
        name="project",
    )(ids, n1, *weights, bias, *tables)


def head_lanes(shape, head):
    return lax.broadcasted_iota(jnp.int32, shape, 1) // HD == head


def load_keys(kvs, kv_scr):
    start = 0
    for part in kvs:
        count = part.shape[0] // BLK
        for block in range(count):
            kv_scr[start + block] = part[block * BLK : (block + 1) * BLK, :]
        start += count


def attend_forward_kernel(maxk, low, count, first, last, ids, q, kv, *refs):
    if first:
        ins, refs = None, refs
    else:
        ins, refs = refs[:2], refs[2:]
    outs, (turned, state, acc) = refs[:2], refs[2:]
    for slot in range(count):
        turned[slot] = kv[slot * BLK : (slot + 1) * BLK, PAIR:].T
    if not first:
        state[...] = ins[0][...]
        acc[...] = ins[1][...]
    for block in range(q.shape[0] // BLK):
        own = ids[0] + block
        for head in range(2):
            rows = slice(block * PAIR + head * HD, block * PAIR + (head + 1) * HD)
            part = slice(head * HD, (head + 1) * HD)
            line = block * 2 + head
            tops, sums = slice(line, line + 1), slice(8 + line, 9 + line)
            query = q[block * BLK : (block + 1) * BLK, :]
            query = jnp.where(head_lanes(query.shape, head), query, jnp.zeros_like(query))

            if first:
                at = pl.ds(pl.multiple_of((own - low) * BLK, BLK), BLK)
                scores = dot(kv[at, :PAIR], query, NT) * scale2
                keep = lax.broadcasted_iota(jnp.int32, scores.shape, 0) <= lax.broadcasted_iota(
                    jnp.int32, scores.shape, 1
                )
                scores = jnp.where(keep, scores, masked)
                top = jnp.max(scores, axis=0, keepdims=True)
                weight = jnp.exp2(scores - top)
                state[tops, :] = top
                state[sums, :] = jnp.sum(weight, axis=0, keepdims=True)
                acc[rows, :] = dot(turned[own - low][part, :], weight.astype(bf16), NN)

            def entry(step, unused):
                slot = ids[2 + block * maxk + step]

                @pl.when((slot >= low) & (slot < low + count) & (slot != own))
                def _():
                    at = pl.ds(pl.multiple_of((slot - low) * BLK, BLK), BLK)
                    scores = dot(kv[at, :PAIR], query, NT) * scale2
                    old = state[tops, :]
                    top = jnp.maximum(old, jnp.max(scores, axis=0, keepdims=True))
                    weight = jnp.exp2(scores - top)
                    shrink = jnp.exp2(old - top)
                    state[tops, :] = top
                    state[sums, :] = state[sums, :] * shrink + jnp.sum(
                        weight, axis=0, keepdims=True
                    )
                    acc[rows, :] = acc[rows, :] * shrink + dot(
                        turned[slot - low][part, :], weight.astype(bf16), NN
                    )

                return unused

            lax.fori_loop(0, maxk, entry, 0)
            if last:
                outs[1][line : line + 1, :] = state[tops, :] + jnp.log2(state[sums, :])
                acc[rows, :] = acc[rows, :] * (1.0 / state[sums, :])
        if last:
            outs[0][block * BLK : (block + 1) * BLK, :] = acc[
                block * PAIR : (block + 1) * PAIR, :
            ].T
    if not last:
        outs[0][...] = state[...]
        outs[1][...] = acc[...]


def attend_forward(ids, maxk, q, kv, low, carried, last, micros=0):
    count = kv.shape[0] // BLK
    rows = q.shape[0]
    tall = rows // BLK * PAIR
    vmem = pl.BlockSpec(memory_space=pltpu.VMEM)
    s = jax.ShapeDtypeStruct
    shapes = [s((rows, PAIR), f32), s((8, BLK), f32)] if last else [
        s((16, BLK), f32), s((tall, BLK), f32)
    ]
    return pl.pallas_call(
        partial(attend_forward_kernel, maxk, low, count, carried is None, last),
        in_specs=[smem] + [vmem] * (2 + len(carried or ())),
        out_specs=[vmem] * 2,
        out_shape=shapes,
        scratch_shapes=[
            pltpu.VMEM((count, PAIR, BLK), bf16),
            pltpu.VMEM((16, BLK), f32),
            pltpu.VMEM((tall, BLK), f32),
        ],
        compiler_params=params(8 + 2 * count),
        cost_estimate=cost(micros),
        name="attend_forward",
    )(ids, q, kv, *(carried or ()))


def attend_backward_kernel(slots, maxk, split, ids, q, g, o, lse, cos, sin, *refs):
    outs = 2 if split else 1
    parts = refs[: -5 - outs]
    grads = refs[-5 - outs : -5]
    qg, kv, turned, acc, total = refs[-5:]
    load_keys(parts, kv)
    for slot in range(slots):
        turned[slot] = kv[slot][:, :PAIR].T
    total[...] = jnp.zeros_like(total)
    pick = (
        lax.broadcasted_iota(jnp.int32, (8, PAIR), 1) // HD
        == lax.broadcasted_iota(jnp.int32, (8, PAIR), 0)
    ).astype(f32)
    for block in range(q.shape[0] // BLK):
        own = ids[0] + block
        span = slice(block * BLK, (block + 1) * BLK)
        deltas = lax.dot_general(
            pick,
            o[span, :] * g[span, :].astype(f32),
            NT,
            preferred_element_type=f32,
            precision=lax.Precision.HIGHEST,
        )
        for head in range(2):
            rows = slice(head * HD, (head + 1) * HD)
            lanes = head_lanes((BLK, PAIR), head)
            query = q[span, :]
            query = jnp.where(lanes, query, jnp.zeros_like(query))
            grad = g[span, :]
            grad = jnp.where(lanes, grad, jnp.zeros_like(grad))
            line = block * 2 + head
            log_sum = lse[line : line + 1, :]
            delta = deltas[head : head + 1, :]

            def tile(slot, keep):
                scores = dot(kv[slot][:, :PAIR], query, NT) * scale2
                prob = jnp.exp2(scores - log_sum)
                if keep is not None:
                    prob = jnp.where(keep, prob, 0.0)
                prob_grad = dot(kv[slot][:, PAIR:], grad, NT)
                score_grad = (prob * (prob_grad - delta)).astype(bf16)
                total[slot, :, PAIR:] += dot(prob.astype(bf16), grad, NN)
                total[slot, :, :PAIR] += dot(score_grad, query, NN)
                return dot(turned[slot][rows, :], score_grad, NN)

            keep = lax.broadcasted_iota(jnp.int32, (BLK, BLK), 0) <= lax.broadcasted_iota(
                jnp.int32, (BLK, BLK), 1
            )
            acc[rows, :] = tile(own, keep)

            def entry(step, unused):
                slot = ids[2 + block * maxk + step]

                @pl.when((slot >= 0) & (slot != own))
                def _():
                    acc[rows, :] += tile(slot, None)

                return unused

            lax.fori_loop(0, maxk, entry, 0)
        grad_q = acc[...].T * (HD ** (-0.5))
        qg[span, :] = rotate_lanes(
            grad_q, cos[span, :], sin[span, :], -1.0
        ).astype(bf16)
    start = 0
    for out in grads:
        count = out.shape[0] // BLK
        for block in range(count):
            out[block * BLK : (block + 1) * BLK, :] = total[start + block].astype(out.dtype)
        start += count


def attend_backward(ids, maxk, q, g, o, lse, tables, kvs):
    slots = sum(part.shape[0] for part in kvs) // BLK
    rows = q.shape[0]
    split = len(kvs) == 2
    shapes = [jax.ShapeDtypeStruct(kvs[0].shape, bf16)]
    if split:
        shapes.append(jax.ShapeDtypeStruct(kvs[1].shape, bf16))
    shapes.append(jax.ShapeDtypeStruct((rows, PAIR), bf16))
    vmem = pl.BlockSpec(memory_space=pltpu.VMEM)
    return pl.pallas_call(
        partial(attend_backward_kernel, slots, maxk, split),
        grid=(),
        in_specs=[smem] + [vmem] * (6 + len(kvs)),
        out_specs=[vmem] * len(shapes),
        out_shape=shapes,
        scratch_shapes=[
            pltpu.VMEM((slots, BLK, 2 * PAIR), bf16),
            pltpu.VMEM((slots, PAIR, BLK), bf16),
            pltpu.VMEM((PAIR, BLK), f32),
            pltpu.VMEM((slots, BLK, 2 * PAIR), f32),
        ],
        compiler_params=params(14 + slots),
        cost_estimate=cost(0),
        name="attend_backward",
    )(ids, q, g, o, lse, *tables, *kvs)


def unpack(ids, pieces, units, up, down, dense):
    for i, piece in enumerate(pieces):
        where = columns(ids[i], SHARD)
        down[:, where] = piece[:units, :]
        for n in range(units // SHARD):
            up[where, n * SHARD : (n + 1) * SHARD] = piece[
                units + n * SHARD : units + (n + 1) * SHARD, :
            ]
        if dense is not None:
            dense[:, where] = piece[2 * units :, :]


def store_half(bits, keep, send, rows, value):
    tile = value.shape[0]
    per = rows // 2 // tile
    step = pl.program_id(0)
    at = pl.ds(pl.multiple_of(lax.rem(step, per) * tile, tile), tile)
    ours = step // per == bits[0]

    @pl.when(ours)
    def _():
        keep[at, :] = value

    @pl.when(jnp.logical_not(ours))
    def _():
        send[at, :] = value


def mlp_forward_kernel(
    rows, ids, bits, x, cot, gain, shift, up_bias, p0, p1, p2, p3, o0, o1,
    keep, send, n2, act, slope, ctx, g0, g1, up, down, dense,
):
    units = act.shape[1]

    @pl.when(pl.program_id(0) == 0)
    def _():
        unpack(ids, (p0, p1, p2, p3), units, up, down, dense)

    normal, _ = norm_rows(x[...].astype(f32))
    normed = (normal * gain[...] + shift[...]).astype(bf16)
    n2[...] = normed
    hidden = dot(normed, up[...], NN) + up_bias[...]
    cdf = 0.5 + 0.5 * lax.erf(hidden * (2.0 ** -0.5))
    pdf = jnp.exp(hidden * hidden * -0.5) * 0.3989422804014327
    low = (hidden * cdf).astype(bf16)
    act[...] = low
    slope[...] = (cdf + hidden * pdf).astype(bf16)
    context_grad = dot(cot[...], dense[...], NT)
    g0[...] = context_grad[:, :PAIR].astype(bf16)
    g1[...] = context_grad[:, PAIR:].astype(bf16)
    ctx[:, :PAIR] = o0[...].astype(bf16)
    ctx[:, PAIR:] = o1[...].astype(bf16)
    value = dot(ctx[...], dense[...], NN) + dot(low, down[...], NN)
    store_half(bits, keep, send, rows, value.astype(bf16))


def mlp_forward(ids, bits, x, cot, gain, shift, up_bias, pieces, o0, o1, tile=256):
    rows, width = x.shape
    units = up_bias.shape[1]
    row = lambda w: pl.BlockSpec((tile, w), lambda i: (i, 0))
    s = jax.ShapeDtypeStruct
    return pl.pallas_call(
        partial(mlp_forward_kernel, rows),
        grid=(rows // tile,),
        in_specs=[smem, smem, row(width), row(width)]
        + [whole(a.shape) for a in (gain, shift, up_bias, *pieces)]
        + [row(PAIR), row(PAIR)],
        out_specs=[whole((rows // 2, width))] * 2
        + [row(width), row(units), row(units), row(2 * PAIR), row(PAIR), row(PAIR)],
        out_shape=[s((rows // 2, width), bf16)] * 2
        + [
            s((rows, width), bf16), s((rows, units), bf16), s((rows, units), bf16),
            s((rows, 2 * PAIR), bf16), s((rows, PAIR), bf16), s((rows, PAIR), bf16),
        ],
        scratch_shapes=[
            pltpu.VMEM((width, units), bf16),
            pltpu.VMEM((units, width), bf16),
            pltpu.VMEM((2 * PAIR, width), bf16),
        ],
        compiler_params=params(28),
        cost_estimate=cost(1),
        name="mlp_forward",
    )(ids, bits, x, cot, gain, shift, up_bias, *pieces, o0, o1)


def mlp_backward_kernel(
    ids, x, cot, gain, slope, p0, p1, p2, p3, hid, e2, sums, up, down
):
    units = hid.shape[1]

    @pl.when(pl.program_id(0) == 0)
    def _():
        sums[...] = jnp.zeros_like(sums)
        unpack(ids, (p0, p1, p2, p3), units, up, down, None)

    low = (dot(cot[...], down[...], NT) * slope[...].astype(f32)).astype(bf16)
    hid[...] = low
    grad = dot(low, up[...], NT)
    normal, _ = norm_rows(x[...].astype(f32))
    sums[0:1, :] += jnp.sum(grad * normal, axis=0, keepdims=True)
    sums[1:2, :] += jnp.sum(grad, axis=0, keepdims=True)
    sums[2:3, :] += jnp.sum(low.astype(f32), axis=0, keepdims=True)
    sums[3:4, :] += jnp.sum(cot[...].astype(f32), axis=0, keepdims=True)
    e2[...] = (grad * gain[...]).astype(bf16)


def mlp_backward(ids, x, cot, gain, slope, pieces, tile=256):
    rows, width = x.shape
    units = slope.shape[1]
    row = lambda w: pl.BlockSpec((tile, w), lambda i: (i, 0))
    s = jax.ShapeDtypeStruct
    return pl.pallas_call(
        mlp_backward_kernel,
        grid=(rows // tile,),
        in_specs=[smem, row(width), row(width), whole(gain.shape), row(units)]
        + [whole(a.shape) for a in pieces],
        out_specs=[row(units), row(width), whole((8, width))],
        out_shape=[s((rows, units), bf16), s((rows, width), bf16), s((8, width), f32)],
        scratch_shapes=[
            pltpu.VMEM((width, units), bf16),
            pltpu.VMEM((units, width), bf16),
        ],
        compiler_params=params(26),
        cost_estimate=cost(1),
        name="mlp_backward",
    )(ids, x, cot, gain, slope, *pieces)


def mlp_weights_kernel(ids, act, cot, n2, hid, keep, near, far):
    units = act.shape[1]
    step = pl.program_id(0)
    index = ids[step]
    for out, when in ((near, step == 0), (far, step == 1), (keep, step >= 2)):

        @pl.when(when)
        def _():
            out[0, :units, :] = dot(act[...], cot[:, columns(index, SHARD)], TN).astype(bf16)
            lhs = n2[:, columns(index, SHARD)]
            for n in range(units // SHARD):
                at = slice(n * SHARD, (n + 1) * SHARD)
                out[0, units + n * SHARD : units + (n + 1) * SHARD, :] = dot(
                    lhs, hid[:, at], TN
                ).astype(bf16)


def rest_weights_kernel(ids, ctx, cot, n1, pg, keep, near, far):
    width = ctx.shape[1]
    step = pl.program_id(0)
    index = ids[step]
    for out, when in ((near, step == 0), (far, step == 1), (keep, step >= 2)):

        @pl.when(when)
        def _():
            out[0, :width, :] = dot(ctx[...], cot[:, columns(index, SHARD)], TN).astype(bf16)
            lhs = n1[:, columns(index, SHARD)]
            for n in range(3):
                at = slice(n * SHARD, (n + 1) * SHARD)
                out[0, width + n * SHARD : width + (n + 1) * SHARD, :] = dot(
                    lhs, pg[:, at], TN
                ).astype(bf16)


def weight_parts(kernel, name, ids, tall, *args):
    s = lambda n: jax.ShapeDtypeStruct((n, tall, SHARD), bf16)
    return pl.pallas_call(
        kernel,
        grid=(4,),
        in_specs=[smem] + [whole(a.shape) for a in args],
        out_specs=[
            pl.BlockSpec((1, tall, SHARD), lambda i: (jnp.maximum(i - 2, 0), 0, 0)),
            whole((1, tall, SHARD)),
            whole((1, tall, SHARD)),
        ],
        out_shape=[s(2), s(1), s(1)],
        compiler_params=params(20),
        cost_estimate=cost(0),
        name=name,
    )(ids, *args)


def input_grad_kernel(
    split, rows, ids, bits, x, e2, gain, sums_two, qg0, qg1, cos, sin, w0, w1, w2, w3, *refs
):
    count = 4 if split else 2
    grads, (keep, send, pg, sums, first) = refs[:count], refs[count:]
    weights = (w0, w1, w2, w3)
    depth = w0.shape[0] // 3
    width = w0.shape[1]

    @pl.when(pl.program_id(0) == 0)
    def _():
        sums[...] = sums_two[...]

    pg[:, 0:PAIR] = qg0[...]
    pg[:, PAIR : 2 * PAIR] = qg1[...]
    for pair in range(2):
        if split:
            own, other = grads[2 * pair : 2 * pair + 2]
            grad = own[...].astype(f32) + other[...].astype(f32)
        else:
            grad = grads[pair][...].astype(f32)
        key = rotate_lanes(
            grad[:, :PAIR] * (HD ** (-0.5)), cos[...], sin[...], -1.0
        )
        at = width + pair * PAIR
        pg[:, at : at + PAIR] = key.astype(bf16)
        pg[:, at + width : at + width + PAIR] = grad[:, PAIR:].astype(bf16)
    sums[6:7, : 3 * width] += jnp.sum(pg[...].astype(f32), axis=0, keepdims=True)
    normal, _ = norm_rows(x[...].astype(f32))
    for piece in range(4):
        where = columns(ids[piece], depth)
        total = dot(pg[:, :width], weights[piece][:depth, :], NT)
        total += dot(pg[:, width : 2 * width], weights[piece][depth : 2 * depth, :], NT)
        total += dot(pg[:, 2 * width :], weights[piece][2 * depth :, :], NT)
        first[:, where] = total
    grad = first[...]
    store_half(bits, keep, send, rows, (grad * gain[...] + e2[...].astype(f32)).astype(bf16))
    sums[4:5, :] += jnp.sum(grad * normal, axis=0, keepdims=True)
    sums[5:6, :] += jnp.sum(grad, axis=0, keepdims=True)

    @pl.when(pl.program_id(0) == pl.num_programs(0) - 1)
    def _():
        terms = split_terms(jnp.concatenate([sums[0:2, :], sums[4:6, :]], axis=0))
        keep[rows // 2 :, :] = terms
        send[rows // 2 :, :] = terms


def input_grad(ids, bits, x, e2, gain, sums, qgs, tables, weights, grads, split, tile=256):
    rows, width = x.shape
    row = lambda w: pl.BlockSpec((tile, w), lambda i: (i, 0))
    s = jax.ShapeDtypeStruct
    units = 3 * weights[0].shape[1]
    half = (rows // 2 + EXTRA, width)
    return pl.pallas_call(
        partial(input_grad_kernel, split, rows),
        grid=(rows // tile,),
        in_specs=[smem, smem, row(width), row(width), whole(gain.shape), whole(sums.shape)]
        + [row(PAIR), row(PAIR)]
        + [row(PAIR)] * 2
        + [whole(w.shape) for w in weights]
        + [row(2 * PAIR)] * len(grads),
        out_specs=[whole(half)] * 2 + [row(units), whole((8, width))],
        out_shape=[s(half, bf16)] * 2
        + [s((rows, units), bf16), s((8, width), f32)],
        scratch_shapes=[pltpu.VMEM((tile, width), f32)],
        compiler_params=params(24),
        cost_estimate=cost(0),
        name="input_grad",
    )(ids, bits, x, e2, gain, sums, *qgs, *tables, *weights, *grads)


def call(kernel, name, args, shapes, grid=1, in_specs=None, out_specs=None, aliases=None, mib=16):
    s = jax.ShapeDtypeStruct
    many = isinstance(shapes, list)
    shapes = [s(*shape) for shape in (shapes if many else [shapes])]
    out = pl.pallas_call(
        kernel,
        grid=(grid,),
        in_specs=in_specs or [whole(a.shape) for a in args],
        out_specs=out_specs or [whole(shape.shape) for shape in shapes],
        out_shape=shapes,
        input_output_aliases=aliases or {},
        compiler_params=params(mib),
        cost_estimate=cost(0),
        name=name,
    )(*args)
    return out if many else out[0]


def add_kernel(a, b, out):
    out[...] = (a[...].astype(f32) + b[...].astype(f32)).astype(out.dtype)


def add(a, b, dtype=bf16, grid=2):
    grid = grid if a.shape[0] > 8 else 1
    row = pl.BlockSpec((a.shape[0] // grid, a.shape[1]), lambda i: (i, 0))
    return call(add_kernel, "add", (a, b), (a.shape, dtype), grid, [row, row], [row])


def split_terms(value):
    high = value.astype(bf16)
    rest = value - high.astype(f32)
    middle = rest.astype(bf16)
    low = (rest - middle.astype(f32)).astype(bf16)
    return jnp.concatenate([high, middle, low, jnp.zeros_like(low)], axis=0)


def join_terms(terms):
    terms = terms.astype(f32)
    return terms[0:4] + terms[4:8] + terms[8:12]


def quarters_kernel(half, bits, kept, got, keep, send):
    size = half // 2
    for out, index in ((keep, bits[1]), (send, 1 - bits[1])):
        at = pl.ds(pl.multiple_of(index * size, size), size)
        out[:size, :] = (kept[at, :].astype(f32) + got[at, :].astype(f32)).astype(bf16)
    if kept.shape[0] > half:
        terms = split_terms(join_terms(kept[half:, :]) + join_terms(got[half:, :]))
        keep[size:, :] = terms
        send[size:, :] = terms


def quarters(bits, kept, got, half):
    shape = (kept.shape[0] - half // 2, kept.shape[1])
    return call(
        partial(quarters_kernel, half), "quarters", (bits, kept, got),
        [(shape, bf16)] * 2, 1, [smem, whole(kept.shape), whole(got.shape)],
    )


def finish_out_kernel(bits, a, b, x, dense_bias, down_bias, out):
    size = out.shape[0]
    at = pl.ds(pl.multiple_of((bits[0] * 2 + bits[1]) * size, size), size)
    total = a[...].astype(f32) + b[...].astype(f32)
    out[...] = (x[at, :].astype(f32) + total + (dense_bias[...] + down_bias[...])).astype(bf16)


def finish_in_kernel(bits, a, b, x, upstream, out, norms):
    size, tile = out.shape[0], 128
    start = (bits[0] * 2 + bits[1]) * size
    for at in range(0, size, tile):
        here = slice(at, at + tile)
        there = pl.ds(pl.multiple_of(start + at, tile), tile)
        total = a[here, :].astype(f32) + b[here, :].astype(f32)
        normal, factor = norm_rows(x[there, :].astype(f32))
        mean_e = jnp.mean(total, axis=-1, keepdims=True)
        mean_en = jnp.mean(total * normal, axis=-1, keepdims=True)
        result = upstream[there, :].astype(f32) + factor * (total - mean_e - normal * mean_en)
        out[here, :] = result.astype(bf16)
    norms[0:4, :] = join_terms(a[size:, :]) + join_terms(b[size:, :])
    norms[4:8, :] = jnp.zeros((4, norms.shape[1]), f32)


def finish(kernel, name, bits, a, b, arrays, shapes):
    args = (bits, a, b, *arrays)
    return call(kernel, name, args, shapes, 1, [smem] + [whole(v.shape) for v in args[1:]])


def assemble_kernel(bits, a, b, c, d, out):
    size = a.shape[0]
    first, second = bits[0], bits[1]
    places = (
        (a, first, second), (b, first, 1 - second), (c, 1 - first, second),
        (d, 1 - first, 1 - second),
    )
    for part, high, low in places:
        out[pl.ds(pl.multiple_of((high * 2 + low) * size, size), size), :] = part[...]


def assemble(bits, *parts):
    rows, width = parts[0].shape
    return call(
        assemble_kernel, "assemble", (bits, *parts), ((4 * rows, width), parts[0].dtype), 1,
        [smem] + [whole(part.shape) for part in parts],
    )


def halves_kernel(keep, near, far, here, there):
    here[...] = keep[0].astype(f32) + near[0].astype(f32)
    there[...] = (keep[1].astype(f32) + far[0].astype(f32)).astype(bf16)


def halves(keep, got, grid=2):
    tall, width = keep.shape[1:]
    block = lambda n: pl.BlockSpec((n, tall // grid, width), lambda i: (0, i, 0))
    row = pl.BlockSpec((tall // grid, width), lambda i: (i, 0))
    return call(
        halves_kernel, "halves", (keep, *got), [((tall, width), f32), ((tall, width), bf16)],
        grid, [block(2), block(1), block(1)], [row, row],
    )


def mlp_last_kernel(a, b, down, up):
    units = down.shape[0]
    down[...] = a[:units, :].astype(f32) + b[:units, :].astype(f32)
    for n in range(units // SHARD):
        at = slice(units + n * SHARD, units + (n + 1) * SHARD)
        up[:, n * SHARD : (n + 1) * SHARD] = a[at, :].astype(f32) + b[at, :].astype(f32)


def rest_last_kernel(a, b, dense, project):
    dense[...] = a[:SHARD, :].astype(f32) + b[:SHARD, :].astype(f32)
    for n in range(3):
        at = slice((n + 1) * SHARD, (n + 2) * SHARD)
        project[:, n, :] = a[at, :].astype(f32) + b[at, :].astype(f32)


def swap(values, axis, size, bit):
    pairs = [(i, i ^ bit) for i in range(size)]
    return jax.tree.map(lambda v: lax.ppermute(v, axis, pairs), values)


def after(values, *others):
    return lax.optimization_barrier((values, others))[0]


class TensorSum:
    def __init__(self, bits, keep, send, half):
        self.bits, self.kept, self.half = bits, keep, half
        self.got = swap(send, "tensor", 4, 1)

    def quarter(self, mark):
        self.kept, send = quarters(self.bits, self.kept, after(self.got, mark), self.half)
        self.got = swap(send, "tensor", 4, 2)
        return send

    def finish(self, run, mark):
        self.final = run(self.kept, after(self.got, mark))
        self.more = None
        if isinstance(self.final, (list, tuple)):
            self.final, self.more = self.final
        self.far = swap(self.final, "tensor", 4, 2)
        self.near = swap(self.final, "tensor", 4, 1)
        return self.final

    def spread(self, mark):
        self.far, self.near = after((self.far, self.near), mark)
        self.last = swap(self.far, "tensor", 4, 1)
        return self.far

    def result(self, mark):
        last = after(self.last, mark)
        return assemble(self.bits, self.final, self.far, self.near, last)


def rotation_tables(positions):
    lane = jnp.arange(PAIR, dtype=jnp.int32) % HD
    half = ROT // 2
    frequency = jnp.exp(
        -jnp.log(10000.0) * (lane % half).astype(f32) * 2.0 / ROT
    )
    angle = positions.astype(f32)[:, None] * frequency[None, :]
    rotated = lane < ROT
    return jnp.where(rotated, jnp.cos(angle), 1.0), jnp.where(rotated, jnp.sin(angle), 0.0)


def body(
    contexts,
    tokens,
    cotangent,
    segments,
    positions,
    parents,
    block_lists,
    project_weight,
    project_bias,
    dense_weight,
    dense_bias,
    up_weight,
    up_bias,
    down_weight,
    down_bias,
    first_gain,
    first_shift,
    second_gain,
    second_shift,
):
    rows, width = tokens.shape
    blocks = rows // BLK
    maxk = block_lists.shape[1]
    me = lax.axis_index("fsdp")
    place = lax.axis_index("context")
    order = jnp.stack([me, me ^ 1, me ^ 2, me ^ 3]).astype(jnp.int32)
    send_order = jnp.stack([me ^ 1, me ^ 3, me, me ^ 2]).astype(jnp.int32)
    split = contexts == 2
    tensor = lax.axis_index("tensor")
    bits = jnp.stack([tensor % 2, tensor // 2]).astype(jnp.int32)
    slots = contexts * blocks
    first_slot = place * blocks
    if split:
        lists = jnp.where(block_lists >= 0, (block_lists - first_slot) % slots, -1)
        base = jnp.zeros((), jnp.int32)
    else:
        lists, base = block_lists, first_slot
    ids = jnp.concatenate(
        [jnp.stack([base, base]).astype(jnp.int32), lists.reshape(-1).astype(jnp.int32)]
    )

    blocks_of = lambda w: w.reshape(SHARD, -1, SHARD).transpose(1, 0, 2).reshape(-1, SHARD)
    units = up_bias.shape[0]
    wp = blocks_of(project_weight)
    wp1, wp2 = swap(wp, "fsdp", 4, 1), swap(wp, "fsdp", 4, 2)
    wp3 = swap(wp2, "fsdp", 4, 1)
    projects = (wp, wp1, wp2, wp3)
    wr = jnp.concatenate([down_weight, blocks_of(up_weight), dense_weight], axis=0)
    wr = after(wr, wp)
    wr1, wr2 = swap(wr, "fsdp", 4, 1), swap(wr, "fsdp", 4, 2)

    normal, _ = norm_rows(tokens.astype(f32))
    normed_one = (normal * first_gain + first_shift).astype(bf16)
    tables = rotation_tables(positions)
    q0, q1, kv0, kv1 = project(order, normed_one, projects, project_bias, tables)
    if split:
        other0, other1 = swap(kv0, "context", 2, 1), swap(kv1, "context", 2, 1)
        keys = ((kv0, other0), (kv1, other1))
        state0 = attend_forward(ids, maxk, q0, kv0, 0, None, False)
        state1 = attend_forward(ids, maxk, after(q1, state0), kv1, 0, None, False)
        o0, lse0 = attend_forward(
            ids, maxk, after(q0, state1), other0, blocks, state0, True
        )
        wr2 = after(wr2, o0)
        wr3 = swap(wr2, "fsdp", 4, 1)
        o1, lse1 = attend_forward(
            ids, maxk, after(q1, o0), other1, blocks, state1, True, 10
        )
    else:
        keys = [(lax.all_gather(kv, "context", axis=0, tiled=True),) for kv in (kv0, kv1)]
        wr3 = swap(wr2, "fsdp", 4, 1)
        o0, lse0 = attend_forward(ids, maxk, q0, keys[0][0], 0, None, True)
        o1, lse1 = attend_forward(ids, maxk, q1, keys[1][0], 0, None, True)

    keep, send, normed_two, activated, slope, context_low, g0, g1 = mlp_forward(
        order, bits, tokens, cotangent, second_gain[None], second_shift[None], up_bias[None],
        (wr, wr1, wr2, wr3), o0, o1,
    )
    out = TensorSum(bits, keep, send, rows // 2)
    back0 = attend_backward(ids, maxk, q0, g0, o0, lse0, tables, keys[0])
    back1 = attend_backward(ids, maxk, q1, after(g1, back0), o1, lse1, tables, keys[1])
    mark = out.quarter(back1)
    if split:
        grads = []
        for own, other, _ in (back0, back1):
            grads += [own, swap(other, "context", 2, 1)]
    else:
        grads = [
            lax.psum_scatter(whole_grad, "context", scatter_dimension=0, tiled=True)
            for whole_grad, _ in (back0, back1)
        ]
    hidden_grad, e2, sums = mlp_backward(
        order, tokens, after(cotangent, mark, grads[1] if split else mark), second_gain[None], slope, (wr, wr1, wr2, wr3)
    )
    keep, send, projected_grad, sums = input_grad(
        order, bits, tokens, e2, first_gain[None], sums, (back0[-1], back1[-1]),
        tables, projects, grads, split,
    )
    line = TensorSum(bits, keep, send, rows // 2)
    quarter = (rows // 4, width)
    mark = out.finish(
        lambda a, b: finish(
            finish_out_kernel, "finish_out", bits, a, b,
            (tokens, dense_bias[None], down_bias[None]), (quarter, bf16),
        ),
        keep,
    )
    mlp_keep, *mlp_send = weight_parts(
        mlp_weights_kernel, "mlp_weights", send_order, 2 * units,
        activated, cotangent, normed_two, after(hidden_grad, mark),
    )
    mlp_got = swap(mlp_send, "fsdp", 4, 1)
    rest_keep, *rest_send = weight_parts(
        rest_weights_kernel, "rest_weights", send_order, 4 * SHARD,
        context_low, cotangent, normed_one, after(projected_grad, mlp_keep),
    )
    rest_got = swap(rest_send, "fsdp", 4, 1)
    mark = out.spread(rest_keep)
    mark = line.quarter(mark)
    mlp_here, mlp_there = halves(mlp_keep, after(mlp_got, mark))
    mlp_got = swap(mlp_there, "fsdp", 4, 2)
    rest_here, rest_there = halves(rest_keep, after(rest_got, mlp_here))
    rest_got = swap(rest_there, "fsdp", 4, 2)
    mark = rest_here
    mark = line.finish(
        lambda a, b: finish(
            finish_in_kernel, "finish_in", bits, a, b, (tokens, cotangent),
            [(quarter, bf16), ((8, width), f32)],
        ),
        mark,
    )
    layer_out = out.result(mark)
    mlp_part = add(mlp_here, after(mlp_got, layer_out))
    if split:
        mlp_got = swap(mlp_part, "context", 2, 1)
    sums = jnp.concatenate(
        [line.more[0:2], sums[2:4], line.more[2:4], sums[6:8]], axis=0
    )
    mark = mlp_part
    for step in [("fsdp", 4, 1), ("fsdp", 4, 2)]:
        sums = mark = add(sums, swap(after(sums, mark), *step), f32)
    mark = line.spread(mark)
    rest_part = add(rest_here, after(rest_got, mark))
    if split:
        rest_got = swap(rest_part, "context", 2, 1)
    mark = rest_part
    for i in range(contexts.bit_length() - 1):
        sums = mark = add(sums, swap(after(sums, mark), "context", contexts, 1 << i), f32)
    tokens_grad = mark = line.result(mark)
    if split:
        down_grad, up_grad = call(
            mlp_last_kernel, "mlp_last", (mlp_part, after(mlp_got, mark)),
            [((units, SHARD), f32), ((SHARD, units), f32)],
        )
        dense_grad, project_grad = call(
            rest_last_kernel, "rest_last", (rest_part, after(rest_got, down_grad)),
            [((SHARD, SHARD), f32), ((SHARD, 3, SHARD), f32)],
        )
        mark = dense_grad
    else:
        mlp_part, rest_part = lax.psum(
            (mlp_part.astype(f32), rest_part.astype(f32)), "context"
        )
        back_blocks = lambda g: g.reshape(-1, SHARD, SHARD).transpose(1, 0, 2)
        down_grad = mlp_part[:units]
        up_grad = back_blocks(mlp_part[units:]).reshape(SHARD, units)
        dense_grad = rest_part[:SHARD]
        project_grad = back_blocks(rest_part[SHARD:])
    norms = sums
    up_total, bias_sum = sums[2], sums[3]
    project_total = sums[6, : project_bias.size]
    return (
        layer_out,
        tokens_grad,
        project_grad,
        project_total.reshape(3, -1),
        dense_grad,
        bias_sum,
        up_grad,
        up_total,
        down_grad,
        bias_sum,
        norms[4],
        norms[5],
        norms[0],
        norms[1],
    )


def solution(mesh):
    tokens = P(("fsdp", "context"), None)
    line = P(("fsdp", "context"))
    in_specs = (
        tokens, tokens, line, line, P("fsdp", None), tokens,
        P("fsdp", None, "tensor"), P(None, "tensor"), P("tensor", "fsdp"), P(),
        P("fsdp", "tensor"), P("tensor"), P("tensor", "fsdp"), P(), P(), P(), P(), P(),
    )
    out_specs = (
        tokens, tokens, P("fsdp", None, "tensor"), P(None, "tensor"), P("tensor", "fsdp"), P(),
        P("fsdp", "tensor"), P("tensor"), P("tensor", "fsdp"), P(), P(), P(), P(), P(),
    )
    run = partial(body, mesh.shape["context"])
    return jax.shard_map(run, mesh=mesh, in_specs=in_specs, out_specs=out_specs, check_vma=False)
```

```python
from functools import partial

import jax
import jax.numpy as jnp
from jax import lax
from jax.experimental import pallas as pl
from jax.experimental.pallas import tpu as pltpu
from jax.sharding import PartitionSpec as P

HD = 64
ROT = 16
BLK = 512
PAIR = 2 * HD
SHARD = 256
EXTRA = 16

epsilon = 1e-05
masked = -1e30
bf16 = jnp.bfloat16
f32 = jnp.float32
scale2 = HD ** (-0.5) * 1.4426950408889634
NT = (((1,), (1,)), ((), ()))
NN = (((1,), (0,)), ((), ()))
TN = (((0,), (0,)), ((), ()))


def dot(a, b, dims):
    return lax.dot_general(a, b, dims, preferred_element_type=f32)


def params(mib):
    return pltpu.CompilerParams(vmem_limit_bytes=mib * 1024 * 1024)


SCALE = 1.0


def cost(micros):
    return pl.CostEstimate(
        flops=int(1.15e9 * micros * SCALE), bytes_accessed=int(3.7e6 * micros * SCALE), transcendentals=0
    )


def whole(shape):
    return pl.BlockSpec(shape, lambda *_: (0,) * len(shape))


smem = pl.BlockSpec(memory_space=pltpu.SMEM)


def norm_rows(x):
    mean = jnp.mean(x, axis=-1, keepdims=True)
    centered = x - mean
    variance = jnp.mean(centered * centered, axis=-1, keepdims=True)
    factor = lax.rsqrt(variance + epsilon)
    return centered * factor, factor


def rotate_lanes(x, cos, sin, sign):
    lane = lax.broadcasted_iota(jnp.int32, x.shape, 1) % HD
    left = pltpu.roll(x, PAIR - ROT // 2, 1)
    right = pltpu.roll(x, ROT // 2, 1)
    return x * cos + jnp.where(lane < ROT // 2, -sign * left, sign * right) * sin


def columns(index, width):
    return pl.ds(pl.multiple_of(index * width, width), width)


def project_kernel(
    ids, x, gain, shift, w0, w1, w2, w3, bias, cos, sin, q0, q1, kv0, kv1, n1
):
    normal, _ = norm_rows(x[...].astype(f32))
    n1[...] = (normal * gain[...] + shift[...]).astype(bf16)
    weights = (w0, w1, w2, w3)
    width = w0.shape[1]
    depth = w0.shape[0] // 3
    outs = ((q0, q1), (kv0, kv1))
    for part in range(3):
        total = bias[part : part + 1, :] + jnp.zeros((n1.shape[0], width), f32)
        for piece in range(4):
            total += dot(n1[:, columns(ids[piece], depth)], weights[piece][part * depth : (part + 1) * depth, :], NN)
        for pair in range(2):
            half = total[:, pair * PAIR : (pair + 1) * PAIR]
            if part < 2:
                half = rotate_lanes(half, cos[...], sin[...], 1.0)
            if part == 0:
                outs[0][pair][...] = half.astype(bf16)
            else:
                outs[1][pair][:, (part - 1) * PAIR : part * PAIR] = half.astype(bf16)


def project(ids, x, gain, shift, weights, bias, tables, tile=256):
    rows, wide = x.shape
    row = lambda w: pl.BlockSpec((tile, w), lambda i: (i, 0))
    s = jax.ShapeDtypeStruct
    return pl.pallas_call(
        project_kernel,
        grid=(rows // tile,),
        in_specs=[smem, row(wide)]
        + [whole(v.shape) for v in (gain, shift, *weights, bias)]
        + [row(PAIR)] * 2,
        out_specs=[row(PAIR)] * 2 + [row(2 * PAIR)] * 2 + [row(wide)],
        out_shape=[s((rows, PAIR), bf16)] * 2
        + [s((rows, 2 * PAIR), bf16)] * 2
        + [s((rows, wide), bf16)],
        compiler_params=params(18),
        cost_estimate=cost(4.3),
        name="project",
    )(ids, x, gain, shift, *weights, bias, *tables)


def head_lanes(shape, head):
    return lax.broadcasted_iota(jnp.int32, shape, 1) // HD == head


def load_keys(kvs, kv_scr):
    start = 0
    for part in kvs:
        count = part.shape[0] // BLK
        for block in range(count):
            kv_scr[start + block] = part[block * BLK : (block + 1) * BLK, :]
        start += count


def attend_forward_kernel(maxk, low, count, first, last, ids, q, kv, *refs):
    if first:
        ins, refs = None, refs
    else:
        ins, refs = refs[:2], refs[2:]
    outs, (turned, state, acc) = refs[:2], refs[2:]
    for slot in range(count):
        turned[slot] = kv[slot * BLK : (slot + 1) * BLK, PAIR:].T
    if not first:
        state[...] = ins[0][...]
        acc[...] = ins[1][...]
    for block in range(q.shape[0] // BLK):
        own = ids[0] + block
        for head in range(2):
            rows = slice(block * PAIR + head * HD, block * PAIR + (head + 1) * HD)
            part = slice(head * HD, (head + 1) * HD)
            line = block * 2 + head
            tops, sums = slice(line, line + 1), slice(8 + line, 9 + line)
            query = q[block * BLK : (block + 1) * BLK, :]
            query = jnp.where(head_lanes(query.shape, head), query, jnp.zeros_like(query))

            if first:
                at = pl.ds(pl.multiple_of((own - low) * BLK, BLK), BLK)
                scores = dot(kv[at, :PAIR], query, NT) * scale2
                keep = lax.broadcasted_iota(jnp.int32, scores.shape, 0) <= lax.broadcasted_iota(
                    jnp.int32, scores.shape, 1
                )
                scores = jnp.where(keep, scores, masked)
                top = jnp.max(scores, axis=0, keepdims=True)
                weight = jnp.exp2(scores - top)
                state[tops, :] = top
                state[sums, :] = jnp.sum(weight, axis=0, keepdims=True)
                acc[rows, :] = dot(turned[own - low][part, :], weight.astype(bf16), NN)

            def entry(step, unused):
                slot = ids[2 + block * maxk + step]

                @pl.when((slot >= low) & (slot < low + count) & (slot != own))
                def _():
                    at = pl.ds(pl.multiple_of((slot - low) * BLK, BLK), BLK)
                    scores = dot(kv[at, :PAIR], query, NT) * scale2
                    old = state[tops, :]
                    top = jnp.maximum(old, jnp.max(scores, axis=0, keepdims=True))
                    weight = jnp.exp2(scores - top)
                    shrink = jnp.exp2(old - top)
                    state[tops, :] = top
                    state[sums, :] = state[sums, :] * shrink + jnp.sum(
                        weight, axis=0, keepdims=True
                    )
                    acc[rows, :] = acc[rows, :] * shrink + dot(
                        turned[slot - low][part, :], weight.astype(bf16), NN
                    )

                return unused

            lax.fori_loop(0, maxk, entry, 0)
            if last:
                outs[1][line : line + 1, :] = state[tops, :] + jnp.log2(state[sums, :])
                acc[rows, :] = acc[rows, :] * (1.0 / state[sums, :])
        if last:
            outs[0][block * BLK : (block + 1) * BLK, :] = acc[
                block * PAIR : (block + 1) * PAIR, :
            ].T
    if not last:
        outs[0][...] = state[...]
        outs[1][...] = acc[...]


def attend_forward(ids, maxk, q, kv, low, carried, last, micros=0):
    count = kv.shape[0] // BLK
    rows = q.shape[0]
    tall = rows // BLK * PAIR
    vmem = pl.BlockSpec(memory_space=pltpu.VMEM)
    s = jax.ShapeDtypeStruct
    shapes = [s((rows, PAIR), f32), s((8, BLK), f32)] if last else [
        s((16, BLK), f32), s((tall, BLK), f32)
    ]
    return pl.pallas_call(
        partial(attend_forward_kernel, maxk, low, count, carried is None, last),
        in_specs=[smem] + [vmem] * (2 + len(carried or ())),
        out_specs=[vmem] * 2,
        out_shape=shapes,
        scratch_shapes=[
            pltpu.VMEM((count, PAIR, BLK), bf16),
            pltpu.VMEM((16, BLK), f32),
            pltpu.VMEM((tall, BLK), f32),
        ],
        compiler_params=params(8 + 2 * count),
        cost_estimate=cost(micros),
        name="attend_forward",
    )(ids, q, kv, *(carried or ()))


def attend_backward_kernel(slots, maxk, split, ids, q, g, o, lse, cos, sin, *refs):
    outs = 2 if split else 1
    parts = refs[: -5 - outs]
    grads = refs[-5 - outs : -5]
    qg, kv, turned, acc, total = refs[-5:]
    load_keys(parts, kv)
    for slot in range(slots):
        turned[slot] = kv[slot][:, :PAIR].T
    total[...] = jnp.zeros_like(total)
    pick = (
        lax.broadcasted_iota(jnp.int32, (8, PAIR), 1) // HD
        == lax.broadcasted_iota(jnp.int32, (8, PAIR), 0)
    ).astype(f32)
    for block in range(q.shape[0] // BLK):
        own = ids[0] + block
        span = slice(block * BLK, (block + 1) * BLK)
        deltas = lax.dot_general(
            pick,
            o[span, :] * g[span, :].astype(f32),
            NT,
            preferred_element_type=f32,
            precision=lax.Precision.HIGHEST,
        )
        for head in range(2):
            rows = slice(head * HD, (head + 1) * HD)
            lanes = head_lanes((BLK, PAIR), head)
            query = q[span, :]
            query = jnp.where(lanes, query, jnp.zeros_like(query))
            grad = g[span, :]
            grad = jnp.where(lanes, grad, jnp.zeros_like(grad))
            line = block * 2 + head
            log_sum = lse[line : line + 1, :]
            delta = deltas[head : head + 1, :]

            def tile(slot, keep):
                scores = dot(kv[slot][:, :PAIR], query, NT) * scale2
                prob = jnp.exp2(scores - log_sum)
                if keep is not None:
                    prob = jnp.where(keep, prob, 0.0)
                prob_grad = dot(kv[slot][:, PAIR:], grad, NT)
                score_grad = (prob * (prob_grad - delta)).astype(bf16)
                total[slot, :, PAIR:] += dot(prob.astype(bf16), grad, NN)
                total[slot, :, :PAIR] += dot(score_grad, query, NN)
                return dot(turned[slot][rows, :], score_grad, NN)

            keep = lax.broadcasted_iota(jnp.int32, (BLK, BLK), 0) <= lax.broadcasted_iota(
                jnp.int32, (BLK, BLK), 1
            )
            acc[rows, :] = tile(own, keep)

            def entry(step, unused):
                slot = ids[2 + block * maxk + step]

                @pl.when((slot >= 0) & (slot != own))
                def _():
                    acc[rows, :] += tile(slot, None)

                return unused

            lax.fori_loop(0, maxk, entry, 0)
        grad_q = acc[...].T * (HD ** (-0.5))
        qg[span, :] = rotate_lanes(
            grad_q, cos[span, :], sin[span, :], -1.0
        ).astype(bf16)
    start = 0
    for out in grads:
        count = out.shape[0] // BLK
        for block in range(count):
            out[block * BLK : (block + 1) * BLK, :] = total[start + block].astype(out.dtype)
        start += count


def attend_backward(ids, maxk, q, g, o, lse, tables, kvs):
    slots = sum(part.shape[0] for part in kvs) // BLK
    rows = q.shape[0]
    split = len(kvs) == 2
    shapes = [jax.ShapeDtypeStruct(kvs[0].shape, bf16)]
    if split:
        shapes.append(jax.ShapeDtypeStruct(kvs[1].shape, bf16))
    shapes.append(jax.ShapeDtypeStruct((rows, PAIR), bf16))
    vmem = pl.BlockSpec(memory_space=pltpu.VMEM)
    return pl.pallas_call(
        partial(attend_backward_kernel, slots, maxk, split),
        grid=(),
        in_specs=[smem] + [vmem] * (6 + len(kvs)),
        out_specs=[vmem] * len(shapes),
        out_shape=shapes,
        scratch_shapes=[
            pltpu.VMEM((slots, BLK, 2 * PAIR), bf16),
            pltpu.VMEM((slots, PAIR, BLK), bf16),
            pltpu.VMEM((PAIR, BLK), f32),
            pltpu.VMEM((slots, BLK, 2 * PAIR), f32),
        ],
        compiler_params=params(14 + slots),
        cost_estimate=cost(0),
        name="attend_backward",
    )(ids, q, g, o, lse, *tables, *kvs)


def unpack(ids, pieces, units, up, down, dense):
    for i, piece in enumerate(pieces):
        where = columns(ids[i], SHARD)
        down[:, where] = piece[:units, :]
        for n in range(units // SHARD):
            up[where, n * SHARD : (n + 1) * SHARD] = piece[
                units + n * SHARD : units + (n + 1) * SHARD, :
            ]
        if dense is not None:
            dense[:, where] = piece[2 * units :, :]


def store_part(outs, sizes, value):
    tile = value.shape[0]
    step = pl.program_id(0)
    start = 0
    for out, size in zip(outs, sizes):
        count = size // tile

        @pl.when((step >= start) & (step < start + count))
        def _():
            out[pl.ds(pl.multiple_of((step - start) * tile, tile), tile), :] = value

        start += count


def mlp_forward_kernel(
    rows, ids, x, cot, gain, shift, up_bias, p0, p1, p2, p3, o0, o1,
    keep, send, n2, act, slope, ctx, g0, g1, up, down, dense,
):
    units = act.shape[1]

    @pl.when(pl.program_id(0) == 0)
    def _():
        unpack(ids, (p0, p1, p2, p3), units, up, down, dense)

    normal, _ = norm_rows(x[...].astype(f32))
    normed = (normal * gain[...] + shift[...]).astype(bf16)
    n2[...] = normed
    hidden = dot(normed, up[...], NN) + up_bias[...]
    cdf = 0.5 + 0.5 * lax.erf(hidden * (2.0 ** -0.5))
    pdf = jnp.exp(hidden * hidden * -0.5) * 0.3989422804014327
    low = (hidden * cdf).astype(bf16)
    act[...] = low
    slope[...] = (cdf + hidden * pdf).astype(bf16)
    context_grad = dot(cot[...], dense[...], NT)
    g0[...] = context_grad[:, :PAIR].astype(bf16)
    g1[...] = context_grad[:, PAIR:].astype(bf16)
    ctx[:, :PAIR] = o0[...].astype(bf16)
    ctx[:, PAIR:] = o1[...].astype(bf16)
    value = dot(ctx[...], dense[...], NN) + dot(low, down[...], NN)
    store_part((keep, send), (rows // 2, rows // 2), value.astype(bf16))


def mlp_forward(ids, x, cot, gain, shift, up_bias, pieces, o0, o1, tile=256):
    rows, width = x.shape
    units = up_bias.shape[1]
    row = lambda w: pl.BlockSpec((tile, w), lambda i: (i, 0))
    s = jax.ShapeDtypeStruct
    return pl.pallas_call(
        partial(mlp_forward_kernel, rows),
        grid=(rows // tile,),
        in_specs=[smem, row(width), row(width)]
        + [whole(a.shape) for a in (gain, shift, up_bias, *pieces)]
        + [row(PAIR), row(PAIR)],
        out_specs=[whole((rows // 2, width))] * 2
        + [row(width), row(units), row(units), row(2 * PAIR), row(PAIR), row(PAIR)],
        out_shape=[s((rows // 2, width), bf16)] * 2
        + [
            s((rows, width), bf16), s((rows, units), bf16), s((rows, units), bf16),
            s((rows, 2 * PAIR), bf16), s((rows, PAIR), bf16), s((rows, PAIR), bf16),
        ],
        scratch_shapes=[
            pltpu.VMEM((width, units), bf16),
            pltpu.VMEM((units, width), bf16),
            pltpu.VMEM((2 * PAIR, width), bf16),
        ],
        compiler_params=params(28),
        cost_estimate=cost(1),
        name="mlp_forward",
    )(ids, x, cot, gain, shift, up_bias, *pieces, o0, o1)


def mlp_backward_kernel(
    ids, x, cot, gain, slope, p0, p1, p2, p3, hid, e2, sums, up, down
):
    units = hid.shape[1]

    @pl.when(pl.program_id(0) == 0)
    def _():
        sums[...] = jnp.zeros_like(sums)
        unpack(ids, (p0, p1, p2, p3), units, up, down, None)

    low = (dot(cot[...], down[...], NT) * slope[...].astype(f32)).astype(bf16)
    hid[...] = low
    grad = dot(low, up[...], NT)
    normal, _ = norm_rows(x[...].astype(f32))
    sums[0:1, :] += jnp.sum(grad * normal, axis=0, keepdims=True)
    sums[1:2, :] += jnp.sum(grad, axis=0, keepdims=True)
    sums[2:3, :] += jnp.sum(low.astype(f32), axis=0, keepdims=True)
    sums[3:4, :] += jnp.sum(cot[...].astype(f32), axis=0, keepdims=True)
    e2[...] = (grad * gain[...]).astype(bf16)


def mlp_backward(ids, x, cot, gain, slope, pieces, tile=256):
    rows, width = x.shape
    units = slope.shape[1]
    row = lambda w: pl.BlockSpec((tile, w), lambda i: (i, 0))
    s = jax.ShapeDtypeStruct
    return pl.pallas_call(
        mlp_backward_kernel,
        grid=(rows // tile,),
        in_specs=[smem, row(width), row(width), whole(gain.shape), row(units)]
        + [whole(a.shape) for a in pieces],
        out_specs=[row(units), row(width), whole((8, width))],
        out_shape=[s((rows, units), bf16), s((rows, width), bf16), s((8, width), f32)],
        scratch_shapes=[
            pltpu.VMEM((width, units), bf16),
            pltpu.VMEM((units, width), bf16),
        ],
        compiler_params=params(26),
        cost_estimate=cost(1),
        name="mlp_backward",
    )(ids, x, cot, gain, slope, *pieces)


def mlp_weights_kernel(ids, act, cot, n2, hid, keep, near, far):
    units = act.shape[1]
    step = pl.program_id(0)
    index = ids[step]
    for out, when in ((near, step == 0), (far, step == 1), (keep, step >= 2)):

        @pl.when(when)
        def _():
            out[0, :units, :] = dot(act[...], cot[:, columns(index, SHARD)], TN).astype(bf16)
            lhs = n2[:, columns(index, SHARD)]
            for n in range(units // SHARD):
                at = slice(n * SHARD, (n + 1) * SHARD)
                out[0, units + n * SHARD : units + (n + 1) * SHARD, :] = dot(
                    lhs, hid[:, at], TN
                ).astype(bf16)


def rest_weights_kernel(ids, ctx, cot, n1, pg, keep, near, far):
    width = ctx.shape[1]
    step = pl.program_id(0)
    index = ids[step]
    for out, when in ((near, step == 0), (far, step == 1), (keep, step >= 2)):

        @pl.when(when)
        def _():
            out[0, :width, :] = dot(ctx[...], cot[:, columns(index, SHARD)], TN).astype(bf16)
            lhs = n1[:, columns(index, SHARD)]
            for n in range(3):
                at = slice(n * SHARD, (n + 1) * SHARD)
                out[0, width + n * SHARD : width + (n + 1) * SHARD, :] = dot(
                    lhs, pg[:, at], TN
                ).astype(bf16)


def weight_parts(kernel, name, ids, tall, *args):
    s = lambda n: jax.ShapeDtypeStruct((n, tall, SHARD), bf16)
    return pl.pallas_call(
        kernel,
        grid=(4,),
        in_specs=[smem] + [whole(a.shape) for a in args],
        out_specs=[
            pl.BlockSpec((1, tall, SHARD), lambda i: (jnp.maximum(i - 2, 0), 0, 0)),
            whole((1, tall, SHARD)),
            whole((1, tall, SHARD)),
        ],
        out_shape=[s(2), s(1), s(1)],
        compiler_params=params(20),
        cost_estimate=cost(0),
        name=name,
    )(ids, *args)


def input_grad_kernel(
    split, sizes, ids, x, e2, gain, sums_two, qg0, qg1, cos, sin, w0, w1, w2, w3, *refs
):
    count = 4 if split else 2
    grads, es, (pg, sums, first) = refs[:count], refs[count:-3], refs[-3:]
    weights = (w0, w1, w2, w3)
    depth = w0.shape[0] // 3
    width = w0.shape[1]

    @pl.when(pl.program_id(0) == 0)
    def _():
        sums[...] = sums_two[...]

    pg[:, 0:PAIR] = qg0[...]
    pg[:, PAIR : 2 * PAIR] = qg1[...]
    for pair in range(2):
        if split:
            own, other = grads[2 * pair : 2 * pair + 2]
            grad = own[...].astype(f32) + other[...].astype(f32)
        else:
            grad = grads[pair][...].astype(f32)
        key = rotate_lanes(
            grad[:, :PAIR] * (HD ** (-0.5)), cos[...], sin[...], -1.0
        )
        at = width + pair * PAIR
        pg[:, at : at + PAIR] = key.astype(bf16)
        pg[:, at + width : at + width + PAIR] = grad[:, PAIR:].astype(bf16)
    sums[6:7, : 3 * width] += jnp.sum(pg[...].astype(f32), axis=0, keepdims=True)
    normal, _ = norm_rows(x[...].astype(f32))
    for piece in range(4):
        where = columns(ids[piece], depth)
        total = dot(pg[:, :width], weights[piece][:depth, :], NT)
        total += dot(pg[:, width : 2 * width], weights[piece][depth : 2 * depth, :], NT)
        total += dot(pg[:, 2 * width :], weights[piece][2 * depth :, :], NT)
        first[:, where] = total
    grad = first[...]
    store_part(es, sizes, (grad * gain[...] + e2[...].astype(f32)).astype(bf16))
    sums[4:5, :] += jnp.sum(grad * normal, axis=0, keepdims=True)
    sums[5:6, :] += jnp.sum(grad, axis=0, keepdims=True)

    @pl.when(pl.program_id(0) == pl.num_programs(0) - 1)
    def _():
        terms = split_terms(jnp.concatenate([sums[0:2, :], sums[4:6, :]], axis=0))
        es[0][sizes[0] :, :] = terms


def input_grad(ids, x, e2, gain, sums, qgs, tables, weights, grads, split, tile=256):
    rows, width = x.shape
    row = lambda w: pl.BlockSpec((tile, w), lambda i: (i, 0))
    s = jax.ShapeDtypeStruct
    units = 3 * weights[0].shape[1]
    sizes = (rows // 2,) * 2
    parts = [(sizes[0] + EXTRA, width), *[(size, width) for size in sizes[1:]]]
    return pl.pallas_call(
        partial(input_grad_kernel, split, sizes),
        grid=(rows // tile,),
        in_specs=[smem, row(width), row(width), whole(gain.shape), whole(sums.shape)]
        + [row(PAIR), row(PAIR)]
        + [row(PAIR)] * 2
        + [whole(w.shape) for w in weights]
        + [row(2 * PAIR)] * len(grads),
        out_specs=[whole(part) for part in parts] + [row(units), whole((8, width))],
        out_shape=[s(part, bf16) for part in parts]
        + [s((rows, units), bf16), s((8, width), f32)],
        scratch_shapes=[pltpu.VMEM((tile, width), f32)],
        compiler_params=params(24),
        cost_estimate=cost(0),
        name="input_grad",
    )(ids, x, e2, gain, sums, *qgs, *tables, *weights, *grads)


def call(kernel, name, args, shapes, grid=1, in_specs=None, out_specs=None, aliases=None, mib=16):
    s = jax.ShapeDtypeStruct
    many = isinstance(shapes, list)
    shapes = [s(*shape) for shape in (shapes if many else [shapes])]
    out = pl.pallas_call(
        kernel,
        grid=(grid,),
        in_specs=in_specs or [whole(a.shape) for a in args],
        out_specs=out_specs or [whole(shape.shape) for shape in shapes],
        out_shape=shapes,
        input_output_aliases=aliases or {},
        compiler_params=params(mib),
        cost_estimate=cost(0),
        name=name,
    )(*args)
    return out if many else out[0]


def add_kernel(a, b, out):
    out[...] = (a[...].astype(f32) + b[...].astype(f32)).astype(out.dtype)


def add(a, b, dtype=bf16, grid=2):
    grid = grid if a.shape[0] > 8 else 1
    row = pl.BlockSpec((a.shape[0] // grid, a.shape[1]), lambda i: (i, 0))
    return call(add_kernel, "add", (a, b), (a.shape, dtype), grid, [row, row], [row])


def split_terms(value):
    high = value.astype(bf16)
    rest = value - high.astype(f32)
    middle = rest.astype(bf16)
    low = (rest - middle.astype(f32)).astype(bf16)
    return jnp.concatenate([high, middle, low, jnp.zeros_like(low)], axis=0)


def join_terms(terms):
    terms = terms.astype(f32)
    return terms[0:4] + terms[4:8] + terms[8:12]


def add_extra_kernel(a, b, out):
    rows = a.shape[0] - EXTRA
    out[:rows, :] = (a[:rows, :].astype(f32) + b[:rows, :].astype(f32)).astype(out.dtype)
    out[rows:, :] = split_terms(join_terms(a[rows:, :]) + join_terms(b[rows:, :]))


def add_extra(a, b):
    return call(add_extra_kernel, "add_extra", (a, b), (a.shape, a.dtype))


def finish_out_kernel(a, b, x, dense_bias, down_bias, out):
    total = a[...].astype(f32) + b[...].astype(f32)
    out[...] = (x[...].astype(f32) + total + (dense_bias[...] + down_bias[...])).astype(bf16)


def finish_in_kernel(rows, a, b, x, upstream, out):
    tile = 128
    for at in range(0, rows, tile):
        here = slice(at, at + tile)
        total = a[here, :].astype(f32) + b[here, :].astype(f32)
        normal, factor = norm_rows(x[here, :].astype(f32))
        mean_e = jnp.mean(total, axis=-1, keepdims=True)
        mean_en = jnp.mean(total * normal, axis=-1, keepdims=True)
        result = upstream[here, :].astype(f32) + factor * (total - mean_e - normal * mean_en)
        out[here, :] = result.astype(bf16)
    if a.shape[0] > rows:
        out[rows:, :] = split_terms(join_terms(a[rows:, :]) + join_terms(b[rows:, :]))


def finish(kernel, name, start, rows, of_rows, arrays, a, b):
    block = pl.BlockSpec((rows, a.shape[1]), lambda i: (start // rows, 0))
    specs = [whole(a.shape)] * 2 + [
        block if i < of_rows else whole(v.shape) for i, v in enumerate(arrays)
    ]
    return call(kernel, name, (a, b, *arrays), (a.shape, bf16), 1, specs)


def choose_kernel(sizes, flag, *refs):
    out, count = refs[-1], len(sizes)
    for parts, when in ((refs[:count], flag[0] > 0), (refs[count : 2 * count], flag[0] <= 0)):

        @pl.when(when)
        def _():
            start = 0
            for part, size in zip(parts, sizes):
                out[start : start + size, :] = part[:size, :]
                start += size


def choose(flag, ours, theirs, sizes, start=0, total=None, before=None):
    rows, width = sum(sizes), ours[0].shape[1]
    args = (flag, *ours, *theirs)
    specs, aliases = [smem] + [whole(v.shape) for v in args[1:]], {}
    if before is not None:
        aliases = {len(args): 0}
        args, specs = args + (before,), specs + [pl.BlockSpec(memory_space=pl.ANY)]
    return call(
        partial(choose_kernel, sizes), "choose", args, ((total or rows, width), bf16), 1, specs,
        [pl.BlockSpec((rows, width), lambda i: (start // rows, 0))], aliases,
    )


def decode_kernel(flag, ours, theirs, out):
    out[0:4, :] = jnp.where(flag[0] > 0, join_terms(ours[...]), join_terms(theirs[...]))
    out[4:8, :] = jnp.zeros((4, out.shape[1]), f32)


def decode(flag, ours, theirs):
    at = ours.shape[0] // EXTRA - 1
    block = pl.BlockSpec((EXTRA, ours.shape[1]), lambda i: (at, 0))
    return call(
        decode_kernel, "decode", (flag, ours, theirs), ((8, ours.shape[1]), f32), 1,
        [smem, block, block],
    )


def halves_kernel(keep, near, far, here, there):
    here[...] = keep[0].astype(f32) + near[0].astype(f32)
    there[...] = (keep[1].astype(f32) + far[0].astype(f32)).astype(bf16)


def halves(keep, got, grid=2):
    tall, width = keep.shape[1:]
    block = lambda n: pl.BlockSpec((n, tall // grid, width), lambda i: (0, i, 0))
    row = pl.BlockSpec((tall // grid, width), lambda i: (i, 0))
    return call(
        halves_kernel, "halves", (keep, *got), [((tall, width), f32), ((tall, width), bf16)],
        grid, [block(2), block(1), block(1)], [row, row],
    )


def mlp_last_kernel(a, b, down, up):
    units = down.shape[0]
    down[...] = a[:units, :].astype(f32) + b[:units, :].astype(f32)
    for n in range(units // SHARD):
        at = slice(units + n * SHARD, units + (n + 1) * SHARD)
        up[:, n * SHARD : (n + 1) * SHARD] = a[at, :].astype(f32) + b[at, :].astype(f32)


def rest_last_kernel(a, b, dense, project):
    dense[...] = a[:SHARD, :].astype(f32) + b[:SHARD, :].astype(f32)
    for n in range(3):
        at = slice((n + 1) * SHARD, (n + 2) * SHARD)
        project[n] = a[at, :].astype(f32) + b[at, :].astype(f32)


def swap(values, axis, size, bit):
    pairs = [(i, i ^ bit) for i in range(size)]
    return jax.tree.map(lambda v: lax.ppermute(v, axis, pairs), values)


def after(values, *others):
    return lax.optimization_barrier((values, others))[0]


class LineSum:
    def __init__(self, parts, finishes):
        place = lax.axis_index("tensor")
        self.flag = ((place == 1) | (place == 2)).astype(jnp.int32)[None]
        self.parts, self.finishes = parts, finishes
        self.first = [lax.ppermute(part, "tensor", [(0, 1), (3, 2)]) for part in parts]
        self.sums, self.second, self.finals, self.third = {}, {}, {}, {}

    def add(self, i, mark):
        part, got = self.parts[i], after(self.first[i], mark)
        self.sums[i] = add_extra(part, got) if part.shape[0] % 128 else add(part, got)
        self.second[i] = lax.ppermute(self.sums[i], "tensor", [(1, 2), (2, 1)])
        return self.sums[i]

    def end(self, i, mark):
        self.finals[i] = self.finishes[i](self.sums[i], after(self.second[i], mark))
        self.third[i] = lax.ppermute(self.finals[i], "tensor", [(1, 0), (2, 3)])
        return self.finals[i]

    def arrive(self, i, mark):
        self.third[i] = after(self.third[i], mark)
        return self.third[i]

    def result(self, indices, mark, **place):
        theirs = after([self.third[i] for i in indices], mark)
        sizes = tuple(self.finals[i].shape[0] // 128 * 128 for i in indices)
        return choose(self.flag, [self.finals[i] for i in indices], theirs, sizes, **place)

    def decode(self, mark):
        self.third[0] = after(self.third[0], mark)
        return decode(self.flag, self.finals[0], self.third[0])


def rotation_tables(positions):
    lane = jnp.arange(PAIR, dtype=jnp.int32) % HD
    half = ROT // 2
    frequency = jnp.exp(
        -jnp.log(10000.0) * (lane % half).astype(f32) * 2.0 / ROT
    )
    angle = positions.astype(f32)[:, None] * frequency[None, :]
    rotated = lane < ROT
    return jnp.where(rotated, jnp.cos(angle), 1.0), jnp.where(rotated, jnp.sin(angle), 0.0)


def body(
    contexts,
    tokens,
    cotangent,
    segments,
    positions,
    parents,
    block_lists,
    project_weight,
    project_bias,
    dense_weight,
    dense_bias,
    up_weight,
    up_bias,
    down_weight,
    down_bias,
    first_gain,
    first_shift,
    second_gain,
    second_shift,
):
    rows, width = tokens.shape
    blocks = rows // BLK
    maxk = block_lists.shape[1]
    me = lax.axis_index("fsdp")
    place = lax.axis_index("context")
    order = jnp.stack([me, me ^ 1, me ^ 2, me ^ 3]).astype(jnp.int32)
    send_order = jnp.stack([me ^ 1, me ^ 3, me, me ^ 2]).astype(jnp.int32)
    split = contexts == 2
    slots = contexts * blocks
    first_slot = place * blocks
    if split:
        lists = jnp.where(block_lists >= 0, (block_lists - first_slot) % slots, -1)
        base = jnp.zeros((), jnp.int32)
    else:
        lists, base = block_lists, first_slot
    ids = jnp.concatenate(
        [jnp.stack([base, base]).astype(jnp.int32), lists.reshape(-1).astype(jnp.int32)]
    )

    blocks_of = lambda w: w.reshape(SHARD, -1, SHARD).transpose(1, 0, 2).reshape(-1, SHARD)
    units = up_bias.shape[0]
    wp = blocks_of(project_weight)
    wp1, wp2 = swap(wp, "fsdp", 4, 1), swap(wp, "fsdp", 4, 2)
    wr = jnp.concatenate([down_weight, blocks_of(up_weight), dense_weight], axis=0)
    wr = after(wr, wp)
    wr1, wr2 = swap(wr, "fsdp", 4, 1), swap(wr, "fsdp", 4, 2)

    tables = rotation_tables(positions)
    wp2 = after(wp2, tables, ids, send_order)
    wp3 = swap(wp2, "fsdp", 4, 1)
    projects = (wp, wp1, wp2, wp3)
    q0, q1, kv0, kv1, normed_one = project(
        order, tokens, first_gain[None], first_shift[None], projects, project_bias, tables
    )
    if split:
        other0, other1 = swap(kv0, "context", 2, 1), swap(kv1, "context", 2, 1)
        keys = ((kv0, other0), (kv1, other1))
        state0 = attend_forward(ids, maxk, q0, kv0, 0, None, False)
        state1 = attend_forward(ids, maxk, after(q1, state0), kv1, 0, None, False)
        o0, lse0 = attend_forward(
            ids, maxk, after(q0, state1), other0, blocks, state0, True
        )
        wr2 = after(wr2, o0)
        wr3 = swap(wr2, "fsdp", 4, 1)
        o1, lse1 = attend_forward(
            ids, maxk, after(q1, o0), other1, blocks, state1, True, 10
        )
    else:
        keys = [(lax.all_gather(kv, "context", axis=0, tiled=True),) for kv in (kv0, kv1)]
        wr3 = swap(wr2, "fsdp", 4, 1)
        o0, lse0 = attend_forward(ids, maxk, q0, keys[0][0], 0, None, True)
        o1, lse1 = attend_forward(ids, maxk, q1, keys[1][0], 0, None, True)

    made = mlp_forward(
        order, tokens, cotangent, second_gain[None], second_shift[None], up_bias[None],
        (wr, wr1, wr2, wr3), o0, o1,
    )
    normed_two, activated, slope, context_low, g0, g1 = made[2:]
    half = rows // 2

    out = LineSum(
        made[:2],
        [
            partial(
                finish, finish_out_kernel, "finish_out", start, half, 1,
                (tokens, dense_bias[None], down_bias[None]),
            )
            for start in (0, half)
        ],
    )
    back0 = attend_backward(ids, maxk, q0, g0, o0, lse0, tables, keys[0])
    back1 = attend_backward(ids, maxk, q1, after(g1, back0), o1, lse1, tables, keys[1])
    if split:
        grads = []
        for own, other, _ in (back0, back1):
            grads += [own, swap(other, "context", 2, 1)]
    else:
        grads = [
            lax.psum_scatter(whole_grad, "context", scatter_dimension=0, tiled=True)
            for whole_grad, _ in (back0, back1)
        ]
    mark = out.add(0, (back1, grads[1]) if split else back1)
    hidden_grad, e2, sums = mlp_backward(
        order, tokens, after(cotangent, mark),
        second_gain[None], slope, (wr, wr1, wr2, wr3),
    )
    made = input_grad(
        order, tokens, e2, first_gain[None], sums, (back0[-1], back1[-1]),
        tables, projects, grads, split,
    )
    projected_grad, sums = made[2:]
    line = LineSum(
        made[:2],
        [
            partial(
                finish, partial(finish_in_kernel, half), "finish_in", start, half, 2,
                (tokens, cotangent),
            )
            for start in (0, half)
        ],
    )
    mark = out.add(1, made[0])
    mlp_keep, *mlp_send = weight_parts(
        mlp_weights_kernel, "mlp_weights", send_order, 2 * units,
        activated, cotangent, normed_two, after(hidden_grad, mark),
    )
    mlp_got = swap(mlp_send, "fsdp", 4, 1)
    mark = out.end(0, mlp_keep)
    rest_keep, *rest_send = weight_parts(
        rest_weights_kernel, "rest_weights", send_order, 4 * SHARD,
        context_low, cotangent, normed_one, after(projected_grad, mark),
    )
    rest_got = swap(rest_send, "fsdp", 4, 1)
    mark = line.add(0, rest_keep)
    mark = out.end(1, mark)
    mark = out.arrive(0, mark)
    mlp_here, mlp_there = halves(mlp_keep, after(mlp_got, mark))
    mlp_got = swap(mlp_there, "fsdp", 4, 2)
    rest_here, rest_there = halves(rest_keep, after(rest_got, mlp_here))
    rest_got = swap(rest_there, "fsdp", 4, 2)
    mark = out.arrive(1, rest_here)
    mark = line.add(1, mark)
    mark = line.end(0, mark)
    mlp_part = add(mlp_here, after(mlp_got, mark))
    if split:
        mlp_got = swap(mlp_part, "context", 2, 1)
    rest_part = add(rest_here, after(rest_got, mlp_part))
    if split:
        rest_got = swap(rest_part, "context", 2, 1)
    mark = line.end(1, rest_part)
    norms = line.decode(mark)
    sums = jnp.concatenate([norms[0:2], sums[2:4], norms[2:4], sums[6:8]], axis=0)
    mark = sums
    for step in [("fsdp", 4, 1), ("fsdp", 4, 2)]:
        sums = mark = add(sums, swap(after(sums, mark), *step), f32)
    hop = swap(sums, "context", contexts, 1)
    layer_out = mark = out.result([0, 1], mark)
    tokens_grad = mark = line.result([0], mark, total=rows)
    if split:
        down_grad, up_grad = call(
            mlp_last_kernel, "mlp_last", (mlp_part, after(mlp_got, mark)),
            [((units, SHARD), f32), ((SHARD, units), f32)],
        )
        dense_grad, project_grad = call(
            rest_last_kernel, "rest_last", (rest_part, after(rest_got, down_grad)),
            [((SHARD, SHARD), f32), ((3, SHARD, SHARD), f32)],
        )
        mark = dense_grad
        project_grad = project_grad.transpose(1, 0, 2)
    else:
        mlp_part, rest_part = lax.psum(
            (mlp_part.astype(f32), rest_part.astype(f32)), "context"
        )
        back_blocks = lambda g: g.reshape(-1, SHARD, SHARD).transpose(1, 0, 2)
        down_grad = mlp_part[:units]
        up_grad = back_blocks(mlp_part[units:]).reshape(SHARD, units)
        dense_grad = rest_part[:SHARD]
        project_grad = back_blocks(rest_part[SHARD:])
    sums = mark = add(sums, after(hop, mark), f32)
    for i in range(1, contexts.bit_length() - 1):
        sums = mark = add(sums, swap(after(sums, mark), "context", contexts, 1 << i), f32)
    tokens_grad = line.result([1], mark, start=half, total=rows, before=tokens_grad)
    norms = sums
    up_total, bias_sum = sums[2], sums[3]
    project_total = sums[6, : project_bias.size]
    return (
        layer_out,
        tokens_grad,
        project_grad,
        project_total.reshape(3, -1),
        dense_grad,
        bias_sum,
        up_grad,
        up_total,
        down_grad,
        bias_sum,
        norms[4],
        norms[5],
        norms[0],
        norms[1],
    )


def solution(mesh):
    tokens = P(("fsdp", "context"), None)
    line = P(("fsdp", "context"))
    in_specs = (
        tokens, tokens, line, line, P("fsdp", None), tokens,
        P("fsdp", None, "tensor"), P(None, "tensor"), P("tensor", "fsdp"), P(),
        P("fsdp", "tensor"), P("tensor"), P("tensor", "fsdp"), P(), P(), P(), P(), P(),
    )
    out_specs = (
        tokens, tokens, P("fsdp", None, "tensor"), P(None, "tensor"), P("tensor", "fsdp"), P(),
        P("fsdp", "tensor"), P("tensor"), P("tensor", "fsdp"), P(), P(), P(), P(), P(),
    )
    run = partial(body, mesh.shape["context"])
    return jax.shard_map(run, mesh=mesh, in_specs=in_specs, out_specs=out_specs, check_vma=False)
```

```python
from functools import partial

import jax
import jax.numpy as jnp
from jax import lax
from jax.experimental import pallas as pl
from jax.experimental.pallas import tpu as pltpu
from jax.sharding import PartitionSpec as P

HD = 64
ROT = 16
BLK = 512
HALF = 256
PAIR = 2 * HD
SHARD = 256
EXTRA = 16

epsilon = 1e-05
masked = -1e30
bf16 = jnp.bfloat16
f32 = jnp.float32
scale2 = HD ** (-0.5) * 1.4426950408889634
NT = (((1,), (1,)), ((), ()))
NN = (((1,), (0,)), ((), ()))
TN = (((0,), (0,)), ((), ()))


def dot(a, b, dims):
    return lax.dot_general(a, b, dims, preferred_element_type=f32)


def params(mib):
    return pltpu.CompilerParams(vmem_limit_bytes=mib * 1024 * 1024)


SCALE = 1.0


def cost(micros):
    return pl.CostEstimate(
        flops=int(1.15e9 * micros * SCALE), bytes_accessed=int(3.7e6 * micros * SCALE), transcendentals=0
    )


def whole(shape):
    return pl.BlockSpec(shape, lambda *_: (0,) * len(shape))


smem = pl.BlockSpec(memory_space=pltpu.SMEM)


def norm_rows(x):
    mean = jnp.mean(x, axis=-1, keepdims=True)
    centered = x - mean
    variance = jnp.mean(centered * centered, axis=-1, keepdims=True)
    factor = lax.rsqrt(variance + epsilon)
    return centered * factor, factor


def rotate_lanes(x, cos, sin, sign):
    lane = lax.broadcasted_iota(jnp.int32, x.shape, 1) % HD
    left = pltpu.roll(x, PAIR - ROT // 2, 1)
    right = pltpu.roll(x, ROT // 2, 1)
    return x * cos + jnp.where(lane < ROT // 2, -sign * left, sign * right) * sin


def columns(index, width):
    return pl.ds(pl.multiple_of(index * width, width), width)


def norm_kernel(x, gain, shift, out):
    normal, _ = norm_rows(x[...].astype(f32))
    out[...] = (normal * gain[...] + shift[...]).astype(bf16)


def norm(x, gain, shift, tile=256):
    row = pl.BlockSpec((tile, x.shape[1]), lambda i: (i, 0))
    return call(
        norm_kernel, "norm", (x, gain, shift), (x.shape, bf16), x.shape[0] // tile,
        [row, whole(gain.shape), whole(shift.shape)], [row],
    )


def project_kernel(ids, n1, w0, w1, w2, w3, bias, cos, sin, q0, q1, kv0, kv1, weight):
    depth, width = w0.shape[0] // 3, w0.shape[1]

    @pl.when(pl.program_id(0) == 0)
    def _():
        for i, piece in enumerate((w0, w1, w2, w3)):
            for part in range(3):
                weight[part, columns(ids[i], depth), :] = piece[
                    part * depth : (part + 1) * depth, :
                ]

    for part in range(3):
        total = dot(n1[...], weight[part], NN) + bias[part : part + 1, :]
        for pair, (q, kv) in enumerate(((q0, kv0), (q1, kv1))):
            half = total[:, pair * PAIR : (pair + 1) * PAIR]
            if part < 2:
                half = rotate_lanes(half, cos[...], sin[...], 1.0)
            if part == 0:
                q[...] = half.astype(bf16)
            else:
                kv[:, (part - 1) * PAIR : part * PAIR] = half.astype(bf16)


def project(ids, n1, weights, bias, tables, tile=256):
    rows, wide = n1.shape
    row = lambda w: pl.BlockSpec((tile, w), lambda i: (i, 0))
    s = jax.ShapeDtypeStruct
    return pl.pallas_call(
        project_kernel,
        grid=(rows // tile,),
        in_specs=[smem, row(wide)]
        + [whole(v.shape) for v in (*weights, bias)]
        + [row(PAIR)] * 2,
        out_specs=[row(PAIR)] * 2 + [row(2 * PAIR)] * 2,
        out_shape=[s((rows, PAIR), bf16)] * 2 + [s((rows, 2 * PAIR), bf16)] * 2,
        scratch_shapes=[pltpu.VMEM((3, wide, weights[0].shape[1]), bf16)],
        compiler_params=params(16),
        cost_estimate=cost(4.3),
        name="project",
    )(ids, n1, *weights, bias, *tables)


def head_lanes(shape, head):
    return lax.broadcasted_iota(jnp.int32, shape, 1) // HD == head


def sublanes(index, size):
    return pl.ds(pl.multiple_of(index * size, size), size)


def triangle(rows, cols):
    return lax.broadcasted_iota(jnp.int32, (rows, cols), 0) <= lax.broadcasted_iota(
        jnp.int32, (rows, cols), 1
    )


def slot_of(ids, lists, slots, block, step):
    entry = lists[block, step]
    return jnp.where(entry < 0, entry, lax.rem(entry - ids[9] + slots, slots))


def head_of(ref, block, head):
    value = ref[sublanes(block, BLK), :]
    return jnp.where(head_lanes(value.shape, head), value, jnp.zeros_like(value))


def attend_forward_kernel(slots, low, count, first, last, ids, lists, q, kv, *refs):
    if not first:
        ins, refs = refs[:2], refs[2:]
    outs, (turned, state, acc) = refs[:2], refs[2:]
    blocks = q.shape[0] // BLK

    def turn(slot, unused):
        turned[slot] = kv[sublanes(slot, BLK), PAIR:].T
        return unused

    lax.fori_loop(0, count, turn, 0)
    if not first:
        state[...] = ins[0][...]
        acc[...] = ins[1][...]

    def one(line, unused):
        block, head = lax.div(line, 2), lax.rem(line, 2)
        own = ids[8] + block
        rows, part = sublanes(line, HD), sublanes(head, HD)
        tops, sums = pl.ds(line, 1), pl.ds(8 + line, 1)
        query = head_of(q, block, head)

        if first:
            upper, lower = sublanes(2 * (own - low), HALF), sublanes(2 * (own - low) + 1, HALF)
            scores = dot(kv[upper, :PAIR], query, NT) * scale2
            scores = jnp.where(triangle(HALF, BLK), scores, masked)
            late = dot(kv[lower, :PAIR], query[HALF:, :], NT) * scale2
            late = jnp.where(triangle(HALF, HALF), late, masked)
            state[tops, :] = jnp.max(scores, axis=0, keepdims=True)
            state[tops, HALF:] = jnp.maximum(
                state[tops, HALF:], jnp.max(late, axis=0, keepdims=True)
            )
            weight = jnp.exp2(scores - state[tops, :])
            late = jnp.exp2(late - state[tops, HALF:])
            state[sums, :] = jnp.sum(weight, axis=0, keepdims=True)
            state[sums, HALF:] += jnp.sum(late, axis=0, keepdims=True)
            acc[rows, :] = dot(turned[own - low, part, :HALF], weight.astype(bf16), NN)
            acc[rows, HALF:] += dot(turned[own - low, part, HALF:], late.astype(bf16), NN)

        def entry(step, unused):
            slot = slot_of(ids, lists, slots, block, step)

            @pl.when((slot >= low) & (slot < low + count) & (slot != own))
            def _():
                scores = dot(kv[sublanes(slot - low, BLK), :PAIR], query, NT) * scale2
                old = state[tops, :]
                top = jnp.maximum(old, jnp.max(scores, axis=0, keepdims=True))
                weight = jnp.exp2(scores - top)
                shrink = jnp.exp2(old - top)
                state[tops, :] = top
                state[sums, :] = state[sums, :] * shrink + jnp.sum(weight, axis=0, keepdims=True)
                acc[rows, :] = acc[rows, :] * shrink + dot(
                    turned[slot - low, part, :], weight.astype(bf16), NN
                )

            return unused

        lax.fori_loop(0, lists.shape[1], entry, 0)
        if last:
            outs[1][pl.ds(line, 1), :] = state[tops, :] + jnp.log2(state[sums, :])
            acc[rows, :] = acc[rows, :] * (1.0 / state[sums, :])
        return unused

    lax.fori_loop(0, 2 * blocks, one, 0)
    if last:

        def give(block, unused):
            outs[0][sublanes(block, BLK), :] = acc[sublanes(block, PAIR), :].T
            return unused

        lax.fori_loop(0, blocks, give, 0)
    else:
        outs[0][...] = state[...]
        outs[1][...] = acc[...]


def attend_forward(ids, lists, slots, q, kv, low, carried, last, micros=0):
    count = kv.shape[0] // BLK
    rows = q.shape[0]
    tall = rows // BLK * PAIR
    vmem = pl.BlockSpec(memory_space=pltpu.VMEM)
    s = jax.ShapeDtypeStruct
    shapes = [s((rows, PAIR), f32), s((8, BLK), f32)] if last else [
        s((16, BLK), f32), s((tall, BLK), f32)
    ]
    return pl.pallas_call(
        partial(attend_forward_kernel, slots, low, count, carried is None, last),
        in_specs=[smem, smem] + [vmem] * (2 + len(carried or ())),
        out_specs=[vmem] * 2,
        out_shape=shapes,
        scratch_shapes=[
            pltpu.VMEM((count, PAIR, BLK), bf16),
            pltpu.VMEM((16, BLK), f32),
            pltpu.VMEM((tall, BLK), f32),
        ],
        compiler_params=params(8 + 2 * count),
        cost_estimate=cost(micros),
        name="attend_forward",
    )(ids, lists, q, kv, *(carried or ()))


def attend_backward_kernel(slots, split, ids, lists, q, g, o, lse, cos, sin, *refs):
    outs = 2 if split else 1
    parts = refs[: -6 - outs]
    grads = refs[-6 - outs : -6]
    qg, kv, turned, acc, total, deltas = refs[-6:]
    blocks = q.shape[0] // BLK
    start = 0
    for part in parts:
        kv[start : start + part.shape[0], :] = part[...]
        start += part.shape[0]

    def prepare(slot, unused):
        turned[slot] = kv[sublanes(slot, BLK), :PAIR].T
        total[sublanes(slot, BLK), :] = jnp.zeros((BLK, 2 * PAIR), f32)
        return unused

    lax.fori_loop(0, slots, prepare, 0)
    pick = (
        lax.broadcasted_iota(jnp.int32, (8, PAIR), 1) // HD
        == lax.broadcasted_iota(jnp.int32, (8, PAIR), 0)
    ).astype(f32)

    def delta_of(block, unused):
        span = sublanes(block, BLK)
        deltas[sublanes(block, 8), :] = lax.dot_general(
            pick,
            o[span, :] * g[span, :].astype(f32),
            NT,
            preferred_element_type=f32,
            precision=lax.Precision.HIGHEST,
        )
        return unused

    lax.fori_loop(0, blocks, delta_of, 0)

    def one(line, unused):
        block, head = lax.div(line, 2), lax.rem(line, 2)
        own = ids[8] + block
        rows, part = sublanes(line, HD), sublanes(head, HD)
        query, grad = head_of(q, block, head), head_of(g, block, head)
        log_sum = lse[pl.ds(line, 1), :]
        delta = deltas[pl.ds(block * 8 + head, 1), :]

        def tile(here, keys, skip=0, keep=None):
            scores = dot(kv[here, :PAIR], query[skip:, :], NT) * scale2
            prob = jnp.exp2(scores - log_sum[:, skip:])
            if keep is not None:
                prob = jnp.where(keep, prob, 0.0)
            prob_grad = dot(kv[here, PAIR:], grad[skip:, :], NT)
            score_grad = (prob * (prob_grad - delta[:, skip:])).astype(bf16)
            total[here, PAIR:] += dot(prob.astype(bf16), grad[skip:, :], NN)
            total[here, :PAIR] += dot(score_grad, query[skip:, :], NN)
            return dot(keys, score_grad, NN)

        acc[rows, :] = tile(
            sublanes(2 * own, HALF), turned[own, part, :HALF], 0, triangle(HALF, BLK)
        )
        acc[rows, HALF:] += tile(
            sublanes(2 * own + 1, HALF), turned[own, part, HALF:], HALF, triangle(HALF, HALF)
        )

        def entry(step, unused):
            slot = slot_of(ids, lists, slots, block, step)

            @pl.when((slot >= 0) & (slot != own))
            def _():
                acc[rows, :] += tile(sublanes(slot, BLK), turned[slot, part, :])

            return unused

        lax.fori_loop(0, lists.shape[1], entry, 0)
        return unused

    lax.fori_loop(0, 2 * blocks, one, 0)

    def give(block, unused):
        span = sublanes(block, BLK)
        grad_q = acc[sublanes(block, PAIR), :].T * (HD ** (-0.5))
        qg[span, :] = rotate_lanes(grad_q, cos[span, :], sin[span, :], -1.0).astype(bf16)
        return unused

    lax.fori_loop(0, blocks, give, 0)
    start = 0
    for out in grads:
        out[...] = total[start : start + out.shape[0], :].astype(out.dtype)
        start += out.shape[0]


def attend_backward(ids, lists, q, g, o, lse, tables, kvs):
    slots = sum(part.shape[0] for part in kvs) // BLK
    rows = q.shape[0]
    split = len(kvs) == 2
    shapes = [jax.ShapeDtypeStruct(kvs[0].shape, bf16)]
    if split:
        shapes.append(jax.ShapeDtypeStruct(kvs[1].shape, bf16))
    shapes.append(jax.ShapeDtypeStruct((rows, PAIR), bf16))
    vmem = pl.BlockSpec(memory_space=pltpu.VMEM)
    return pl.pallas_call(
        partial(attend_backward_kernel, slots, split),
        grid=(),
        in_specs=[smem, smem] + [vmem] * (6 + len(kvs)),
        out_specs=[vmem] * len(shapes),
        out_shape=shapes,
        scratch_shapes=[
            pltpu.VMEM((slots * BLK, 2 * PAIR), bf16),
            pltpu.VMEM((slots, PAIR, BLK), bf16),
            pltpu.VMEM((rows // BLK * PAIR, BLK), f32),
            pltpu.VMEM((slots * BLK, 2 * PAIR), f32),
            pltpu.VMEM((rows // BLK * 8, BLK), f32),
        ],
        compiler_params=params(14 + slots),
        cost_estimate=cost(0),
        name="attend_backward",
    )(ids, lists, q, g, o, lse, *tables, *kvs)


def unpack_up(ids, pieces, up):
    for i, piece in enumerate(pieces):
        for n in range(up.shape[1] // SHARD):
            up[columns(ids[i], SHARD), n * SHARD : (n + 1) * SHARD] = piece[
                n * SHARD : (n + 1) * SHARD, :
            ]


def unpack_down(ids, pieces, down, dense):
    units = down.shape[0]
    for i, piece in enumerate(pieces):
        where = columns(ids[i], SHARD)
        down[:, where] = piece[:units, :]
        if dense is not None:
            dense[:, where] = piece[units:, :]


def mlp_up_kernel(ids, x, gain, shift, up_bias, p0, p1, p2, p3, n2, act, slope, up):
    @pl.when(pl.program_id(0) == 0)
    def _():
        unpack_up(ids, (p0, p1, p2, p3), up)

    normal, _ = norm_rows(x[...].astype(f32))
    normed = (normal * gain[...] + shift[...]).astype(bf16)
    n2[...] = normed
    hidden = dot(normed, up[...], NN) + up_bias[...]
    cdf = 0.5 + 0.5 * lax.erf(hidden * (2.0 ** -0.5))
    pdf = jnp.exp(hidden * hidden * -0.5) * 0.3989422804014327
    act[...] = (hidden * cdf).astype(bf16)
    slope[...] = (cdf + hidden * pdf).astype(bf16)


def mlp_up(ids, x, gain, shift, up_bias, pieces, tile=256):
    rows, width = x.shape
    units = up_bias.shape[1]
    row = lambda w: pl.BlockSpec((tile, w), lambda i: (i, 0))
    s = jax.ShapeDtypeStruct
    return pl.pallas_call(
        mlp_up_kernel,
        grid=(rows // tile,),
        in_specs=[smem, row(width)] + [whole(a.shape) for a in (gain, shift, up_bias, *pieces)],
        out_specs=[row(width), row(units), row(units)],
        out_shape=[s((rows, width), bf16), s((rows, units), bf16), s((rows, units), bf16)],
        scratch_shapes=[pltpu.VMEM((width, units), bf16)],
        compiler_params=params(24),
        cost_estimate=cost(0),
        name="mlp_up",
    )(ids, x, gain, shift, up_bias, *pieces)


def store_part(outs, sizes, value):
    tile = value.shape[0]
    step = pl.program_id(0)
    start = 0
    for out, size in zip(outs, sizes):
        count = size // tile

        @pl.when((step >= start) & (step < start + count))
        def _():
            out[pl.ds(pl.multiple_of((step - start) * tile, tile), tile), :] = value

        start += count


def mlp_down_kernel(
    rows, ids, act, cot, p0, p1, p2, p3, o0, o1, first, second, ctx, g0, g1, down, dense
):
    @pl.when(pl.program_id(0) == 0)
    def _():
        unpack_down(ids, (p0, p1, p2, p3), down, dense)

    context_grad = dot(cot[...], dense[...], NT)
    g0[...] = context_grad[:, :PAIR].astype(bf16)
    g1[...] = context_grad[:, PAIR:].astype(bf16)
    ctx[:, :PAIR] = o0[...].astype(bf16)
    ctx[:, PAIR:] = o1[...].astype(bf16)
    value = dot(ctx[...], dense[...], NN) + dot(act[...], down[...], NN)
    store_part((first, second), (rows // 2, rows // 2), value.astype(bf16))


def mlp_down(ids, act, cot, pieces, o0, o1, tile=256):
    rows, width = cot.shape
    units = act.shape[1]
    row = lambda w: pl.BlockSpec((tile, w), lambda i: (i, 0))
    s = jax.ShapeDtypeStruct
    return pl.pallas_call(
        partial(mlp_down_kernel, rows),
        grid=(rows // tile,),
        in_specs=[smem, row(units), row(width)]
        + [whole(a.shape) for a in pieces]
        + [row(PAIR), row(PAIR)],
        out_specs=[whole((rows // 2, width))] * 2 + [row(2 * PAIR), row(PAIR), row(PAIR)],
        out_shape=[s((rows // 2, width), bf16)] * 2
        + [s((rows, 2 * PAIR), bf16), s((rows, PAIR), bf16), s((rows, PAIR), bf16)],
        scratch_shapes=[
            pltpu.VMEM((units, width), bf16),
            pltpu.VMEM((2 * PAIR, width), bf16),
        ],
        compiler_params=params(26),
        cost_estimate=cost(1),
        name="mlp_down",
    )(ids, act, cot, *pieces, o0, o1)


def mlp_backward_kernel(
    ids, x, cot, gain, slope, u0, u1, u2, u3, d0, d1, d2, d3, hid, e2, sums, up, down
):
    @pl.when(pl.program_id(0) == 0)
    def _():
        sums[...] = jnp.zeros_like(sums)
        unpack_up(ids, (u0, u1, u2, u3), up)
        unpack_down(ids, (d0, d1, d2, d3), down, None)

    low = (dot(cot[...], down[...], NT) * slope[...].astype(f32)).astype(bf16)
    hid[...] = low
    grad = dot(low, up[...], NT)
    normal, _ = norm_rows(x[...].astype(f32))
    sums[0:1, :] += jnp.sum(grad * normal, axis=0, keepdims=True)
    sums[1:2, :] += jnp.sum(grad, axis=0, keepdims=True)
    sums[2:3, :] += jnp.sum(low.astype(f32), axis=0, keepdims=True)
    sums[3:4, :] += jnp.sum(cot[...].astype(f32), axis=0, keepdims=True)
    e2[...] = (grad * gain[...]).astype(bf16)


def mlp_backward(ids, x, cot, gain, slope, pieces, tile=256):
    rows, width = x.shape
    units = slope.shape[1]
    row = lambda w: pl.BlockSpec((tile, w), lambda i: (i, 0))
    s = jax.ShapeDtypeStruct
    return pl.pallas_call(
        mlp_backward_kernel,
        grid=(rows // tile,),
        in_specs=[smem, row(width), row(width), whole(gain.shape), row(units)]
        + [whole(a.shape) for a in pieces],
        out_specs=[row(units), row(width), whole((8, width))],
        out_shape=[s((rows, units), bf16), s((rows, width), bf16), s((8, width), f32)],
        scratch_shapes=[
            pltpu.VMEM((width, units), bf16),
            pltpu.VMEM((units, width), bf16),
        ],
        compiler_params=params(26),
        cost_estimate=cost(1),
        name="mlp_backward",
    )(ids, x, cot, gain, slope, *pieces)


def mlp_weights_kernel(ids, act, cot, n2, hid, keep, near, far):
    units = act.shape[1]
    step = pl.program_id(0)
    index = ids[4 + step]
    for out, when in ((near, step == 0), (far, step == 1), (keep, step >= 2)):

        @pl.when(when)
        def _():
            out[0, :units, :] = dot(act[...], cot[:, columns(index, SHARD)], TN).astype(bf16)
            lhs = n2[:, columns(index, SHARD)]
            for n in range(units // SHARD):
                at = slice(n * SHARD, (n + 1) * SHARD)
                out[0, units + n * SHARD : units + (n + 1) * SHARD, :] = dot(
                    lhs, hid[:, at], TN
                ).astype(bf16)


def rest_weights_kernel(ids, ctx, cot, n1, pg, keep, near, far):
    width = ctx.shape[1]
    step = pl.program_id(0)
    index = ids[4 + step]
    for out, when in ((near, step == 0), (far, step == 1), (keep, step >= 2)):

        @pl.when(when)
        def _():
            out[0, :width, :] = dot(ctx[...], cot[:, columns(index, SHARD)], TN).astype(bf16)
            lhs = n1[:, columns(index, SHARD)]
            for n in range(3):
                at = slice(n * SHARD, (n + 1) * SHARD)
                out[0, width + n * SHARD : width + (n + 1) * SHARD, :] = dot(
                    lhs, pg[:, at], TN
                ).astype(bf16)


def weight_parts(kernel, name, ids, tall, *args):
    s = lambda n: jax.ShapeDtypeStruct((n, tall, SHARD), bf16)
    return pl.pallas_call(
        kernel,
        grid=(4,),
        in_specs=[smem] + [whole(a.shape) for a in args],
        out_specs=[
            pl.BlockSpec((1, tall, SHARD), lambda i: (jnp.maximum(i - 2, 0), 0, 0)),
            whole((1, tall, SHARD)),
            whole((1, tall, SHARD)),
        ],
        out_shape=[s(2), s(1), s(1)],
        compiler_params=params(20),
        cost_estimate=cost(0),
        name=name,
    )(ids, *args)


def input_grad_kernel(
    split, sizes, ids, x, e2, gain, sums_two, qg0, qg1, cos, sin, *refs
):
    count = 4 if split else 2
    weights, refs = refs[:4], refs[4:]
    grads, es, (pg, sums, first) = refs[:count], refs[count:-3], refs[-3:]
    depth, width = weights[0].shape[0] // 3, 2 * PAIR

    @pl.when(pl.program_id(0) == 0)
    def _():
        sums[...] = sums_two[...]

    pg[:, 0:PAIR] = qg0[...]
    pg[:, PAIR : 2 * PAIR] = qg1[...]
    for pair in range(2):
        if split:
            own, other = grads[2 * pair : 2 * pair + 2]
            grad = own[...].astype(f32) + other[...].astype(f32)
        else:
            grad = grads[pair][...].astype(f32)
        key = rotate_lanes(
            grad[:, :PAIR] * (HD ** (-0.5)), cos[...], sin[...], -1.0
        )
        at = width + pair * PAIR
        pg[:, at : at + PAIR] = key.astype(bf16)
        pg[:, at + width : at + width + PAIR] = grad[:, PAIR:].astype(bf16)
    sums[6:7, : 3 * width] += jnp.sum(pg[...].astype(f32), axis=0, keepdims=True)
    normal, _ = norm_rows(x[...].astype(f32))
    for piece in range(4):
        where = columns(ids[piece], depth)
        total = dot(pg[:, :width], weights[piece][:depth, :], NT)
        total += dot(pg[:, width : 2 * width], weights[piece][depth : 2 * depth, :], NT)
        total += dot(pg[:, 2 * width :], weights[piece][2 * depth :, :], NT)
        first[:, where] = total
    grad = first[...]
    store_part(es, sizes, (grad * gain[...] + e2[...].astype(f32)).astype(bf16))
    sums[4:5, :] += jnp.sum(grad * normal, axis=0, keepdims=True)
    sums[5:6, :] += jnp.sum(grad, axis=0, keepdims=True)

    @pl.when(pl.program_id(0) == pl.num_programs(0) - 1)
    def _():
        terms = split_terms(jnp.concatenate([sums[0:2, :], sums[4:6, :]], axis=0))
        es[0][sizes[0] :, :] = terms


def input_grad(ids, x, e2, gain, sums, qgs, tables, weights, grads, split, tile=256):
    rows, width = x.shape
    row = lambda w: pl.BlockSpec((tile, w), lambda i: (i, 0))
    s = jax.ShapeDtypeStruct
    units = 6 * PAIR
    sizes = (rows // 2,) * 2
    parts = [(sizes[0] + EXTRA, width), *[(size, width) for size in sizes[1:]]]
    return pl.pallas_call(
        partial(input_grad_kernel, split, sizes),
        grid=(rows // tile,),
        in_specs=[smem, row(width), row(width), whole(gain.shape), whole(sums.shape)]
        + [row(PAIR), row(PAIR)]
        + [row(PAIR)] * 2
        + [whole(w.shape) for w in weights]
        + [row(2 * PAIR)] * len(grads),
        out_specs=[whole(part) for part in parts] + [row(units), whole((8, width))],
        out_shape=[s(part, bf16) for part in parts]
        + [s((rows, units), bf16), s((8, width), f32)],
        scratch_shapes=[pltpu.VMEM((tile, width), f32)],
        compiler_params=params(24),
        cost_estimate=cost(0),
        name="input_grad",
    )(ids, x, e2, gain, sums, *qgs, *tables, *weights, *grads)


def call(kernel, name, args, shapes, grid=1, in_specs=None, out_specs=None, aliases=None, mib=16):
    s = jax.ShapeDtypeStruct
    many = isinstance(shapes, list)
    shapes = [s(*shape) for shape in (shapes if many else [shapes])]
    out = pl.pallas_call(
        kernel,
        grid=(grid,),
        in_specs=in_specs or [whole(a.shape) for a in args],
        out_specs=out_specs or [whole(shape.shape) for shape in shapes],
        out_shape=shapes,
        input_output_aliases=aliases or {},
        compiler_params=params(mib),
        cost_estimate=cost(0),
        name=name,
    )(*args)
    return out if many else out[0]


def add_kernel(a, b, out):
    out[...] = (a[...].astype(f32) + b[...].astype(f32)).astype(out.dtype)


def add(a, b, dtype=bf16, grid=2):
    grid = grid if a.shape[0] > 8 else 1
    row = pl.BlockSpec((a.shape[0] // grid, a.shape[1]), lambda i: (i, 0))
    return call(add_kernel, "add", (a, b), (a.shape, dtype), grid, [row, row], [row])


def split_terms(value):
    high = value.astype(bf16)
    rest = value - high.astype(f32)
    middle = rest.astype(bf16)
    low = (rest - middle.astype(f32)).astype(bf16)
    return jnp.concatenate([high, middle, low, jnp.zeros_like(low)], axis=0)


def join_terms(terms):
    terms = terms.astype(f32)
    return terms[0:4] + terms[4:8] + terms[8:12]


def add_extra_kernel(a, b, out):
    rows = a.shape[0] - EXTRA
    out[:rows, :] = (a[:rows, :].astype(f32) + b[:rows, :].astype(f32)).astype(out.dtype)
    out[rows:, :] = split_terms(join_terms(a[rows:, :]) + join_terms(b[rows:, :]))


def add_extra(a, b):
    return call(add_extra_kernel, "add_extra", (a, b), (a.shape, a.dtype))


def finish_out_kernel(a, b, x, dense_bias, down_bias, out):
    total = a[...].astype(f32) + b[...].astype(f32)
    out[...] = (x[...].astype(f32) + total + (dense_bias[...] + down_bias[...])).astype(bf16)


def finish_in_kernel(rows, a, b, x, upstream, out):
    def one(step, unused):
        here = sublanes(step, 128)
        total = a[here, :].astype(f32) + b[here, :].astype(f32)
        normal, factor = norm_rows(x[here, :].astype(f32))
        mean_e = jnp.mean(total, axis=-1, keepdims=True)
        mean_en = jnp.mean(total * normal, axis=-1, keepdims=True)
        result = upstream[here, :].astype(f32) + factor * (total - mean_e - normal * mean_en)
        out[here, :] = result.astype(bf16)
        return unused

    lax.fori_loop(0, rows // 128, one, 0)
    if a.shape[0] > rows:
        out[rows:, :] = split_terms(join_terms(a[rows:, :]) + join_terms(b[rows:, :]))


def finish(kernel, name, start, rows, of_rows, arrays, a, b):
    block = pl.BlockSpec((rows, a.shape[1]), lambda i: (start // rows, 0))
    specs = [whole(a.shape)] * 2 + [
        block if i < of_rows else whole(v.shape) for i, v in enumerate(arrays)
    ]
    return call(kernel, name, (a, b, *arrays), (a.shape, bf16), 1, specs)


def choose_kernel(sizes, flag, *refs):
    out, count = refs[-1], len(sizes)
    for parts, when in ((refs[:count], flag[0] > 0), (refs[count : 2 * count], flag[0] <= 0)):

        @pl.when(when)
        def _():
            start = 0
            for part, size in zip(parts, sizes):
                out[start : start + size, :] = part[:size, :]
                start += size


def choose(flag, ours, theirs, sizes, start=0, total=None, before=None):
    rows, width = sum(sizes), ours[0].shape[1]
    args = (flag, *ours, *theirs)
    specs, aliases = [smem] + [whole(v.shape) for v in args[1:]], {}
    if before is not None:
        aliases = {len(args): 0}
        args, specs = args + (before,), specs + [pl.BlockSpec(memory_space=pl.ANY)]
    return call(
        partial(choose_kernel, sizes), "choose", args, ((total or rows, width), bf16), 1, specs,
        [pl.BlockSpec((rows, width), lambda i: (start // rows, 0))], aliases,
    )


def decode_kernel(flag, ours, theirs, out):
    out[0:4, :] = jnp.where(flag[0] > 0, join_terms(ours[...]), join_terms(theirs[...]))
    out[4:8, :] = jnp.zeros((4, out.shape[1]), f32)


def decode(flag, ours, theirs):
    at = ours.shape[0] // EXTRA - 1
    block = pl.BlockSpec((EXTRA, ours.shape[1]), lambda i: (at, 0))
    return call(
        decode_kernel, "decode", (flag, ours, theirs), ((8, ours.shape[1]), f32), 1,
        [smem, block, block],
    )


def halves_kernel(keep, near, far, here, there):
    here[...] = keep[0].astype(f32) + near[0].astype(f32)
    there[...] = (keep[1].astype(f32) + far[0].astype(f32)).astype(bf16)


def halves(keep, got, grid=2):
    tall, width = keep.shape[1:]
    block = lambda n: pl.BlockSpec((n, tall // grid, width), lambda i: (0, i, 0))
    row = pl.BlockSpec((tall // grid, width), lambda i: (i, 0))
    return call(
        halves_kernel, "halves", (keep, *got), [((tall, width), f32), ((tall, width), bf16)],
        grid, [block(2), block(1), block(1)], [row, row],
    )


def mlp_last_kernel(a, b, down, up):
    units = down.shape[0]
    down[...] = a[:units, :].astype(f32) + b[:units, :].astype(f32)
    for n in range(units // SHARD):
        at = slice(units + n * SHARD, units + (n + 1) * SHARD)
        up[:, n * SHARD : (n + 1) * SHARD] = a[at, :].astype(f32) + b[at, :].astype(f32)


def rest_last_kernel(a, b, dense, project):
    dense[...] = a[:SHARD, :].astype(f32) + b[:SHARD, :].astype(f32)
    for n in range(3):
        at = slice((n + 1) * SHARD, (n + 2) * SHARD)
        project[n] = a[at, :].astype(f32) + b[at, :].astype(f32)


def swap(values, axis, size, bit):
    pairs = [(i, i ^ bit) for i in range(size)]
    return jax.tree.map(lambda v: lax.ppermute(v, axis, pairs), values)


def after(values, *others):
    return lax.optimization_barrier((values, others))[0]


class LineSum:
    def __init__(self, parts, finishes):
        place = lax.axis_index("tensor")
        self.flag = ((place == 1) | (place == 2)).astype(jnp.int32)[None]
        self.parts, self.finishes = parts, finishes
        self.first = [lax.ppermute(part, "tensor", [(0, 1), (3, 2)]) for part in parts]
        self.sums, self.second, self.finals, self.third = {}, {}, {}, {}

    def add(self, i, mark):
        part, got = self.parts[i], after(self.first[i], mark)
        self.sums[i] = add_extra(part, got) if part.shape[0] % 128 else add(part, got)
        self.second[i] = lax.ppermute(self.sums[i], "tensor", [(1, 2), (2, 1)])
        return self.sums[i]

    def end(self, i, mark):
        self.finals[i] = self.finishes[i](self.sums[i], after(self.second[i], mark))
        self.third[i] = lax.ppermute(self.finals[i], "tensor", [(1, 0), (2, 3)])
        return self.finals[i]

    def arrive(self, i, mark):
        self.third[i] = after(self.third[i], mark)
        return self.third[i]

    def result(self, indices, mark, **place):
        theirs = after([self.third[i] for i in indices], mark)
        sizes = tuple(self.finals[i].shape[0] // 128 * 128 for i in indices)
        return choose(self.flag, [self.finals[i] for i in indices], theirs, sizes, **place)

    def decode(self, mark):
        self.third[0] = after(self.third[0], mark)
        return decode(self.flag, self.finals[0], self.third[0])


def rotation_tables(positions):
    half = ROT // 2
    frequency = jnp.exp(
        -jnp.log(10000.0) * jnp.arange(half, dtype=jnp.int32).astype(f32) * 2.0 / ROT
    )
    angle = frequency[:, None] * positions.astype(f32)[None, :]
    lane = lax.broadcasted_iota(jnp.int32, (half, PAIR), 1) % HD
    pick = lax.broadcasted_iota(jnp.int32, (half, PAIR), 0) == lane % half
    pick = (pick & (lane < ROT)).astype(f32)
    spread = lambda v: lax.dot_general(
        v, pick, TN, precision=lax.Precision.HIGHEST, preferred_element_type=f32
    )
    plain = (jnp.arange(PAIR, dtype=jnp.int32) % HD >= ROT).astype(f32)
    return spread(jnp.cos(angle)) + plain, spread(jnp.sin(angle))


def body(
    contexts,
    tokens,
    cotangent,
    segments,
    positions,
    parents,
    block_lists,
    project_weight,
    project_bias,
    dense_weight,
    dense_bias,
    up_weight,
    up_bias,
    down_weight,
    down_bias,
    first_gain,
    first_shift,
    second_gain,
    second_shift,
):
    rows, width = tokens.shape
    blocks = rows // BLK
    me = lax.axis_index("fsdp")
    split = contexts == 2
    slots = contexts * blocks
    first_slot = lax.axis_index("context") * blocks
    step = jnp.arange(10, dtype=jnp.int32)
    flip = jnp.where(step < 4, step, jnp.where(step < 6, 2 * step - 7, 2 * step - 12))
    ids = jnp.where(step < 8, me ^ flip, jnp.where(step == 8 if split else step < 8, 0, first_slot))
    if not split:
        ids = jnp.where(step == 9, 0, ids)
    ids = ids.astype(jnp.int32)

    blocks_of = lambda w: w.reshape(SHARD, -1, SHARD).transpose(1, 0, 2)
    units = up_bias.shape[0]
    near = lambda v: swap(v, "fsdp", 4, 1)
    far = lambda v: swap(v, "fsdp", 4, 2)
    wp = blocks_of(project_weight).reshape(-1, SHARD)
    up = blocks_of(up_weight).reshape(-1, SHARD)
    wp_far, up_far = far(wp), far(up)
    tables = rotation_tables(positions)
    normed_one = norm(tokens, first_gain[None], first_shift[None])
    wp_far = after(wp_far, tables, ids, normed_one, up)
    projects = (wp, near(wp), wp_far, near(wp_far))
    q0, q1, kv0, kv1 = project(ids, normed_one, projects, project_bias, tables)
    down = jnp.concatenate(after([down_weight, dense_weight], kv1), axis=0)
    down_far = far(down)
    if split:
        other0, other1 = swap(kv0, "context", 2, 1), swap(kv1, "context", 2, 1)
        keys = ((kv0, other0), (kv1, other1))
        state0 = attend_forward(ids, block_lists, slots, after(q0, kv1), kv0, 0, None, False)
        state1 = attend_forward(ids, block_lists, slots, after(q1, state0), kv1, 0, None, False)
        up_far = after(up_far, state1)
        ups = (up, near(up), up_far, near(up_far))
        o0, lse0 = attend_forward(
            ids, block_lists, slots, after(q0, up_far), other0, blocks, state0, True
        )
        normed_two, activated, slope = mlp_up(
            ids, after(tokens, o0), second_gain[None], second_shift[None], up_bias[None], ups
        )
        o1, lse1 = attend_forward(
            ids, block_lists, slots, after(q1, activated), other1, blocks, state1, True, 10
        )
        down_far = after(down_far, activated)
    else:
        keys = [(lax.all_gather(kv, "context", axis=0, tiled=True),) for kv in (kv0, kv1)]
        o0, lse0 = attend_forward(ids, block_lists, slots, q0, keys[0][0], 0, None, True)
        o1, lse1 = attend_forward(ids, block_lists, slots, q1, keys[1][0], 0, None, True)
        ups = (up, near(up), up_far, near(up_far))
        normed_two, activated, slope = mlp_up(
            ids, tokens, second_gain[None], second_shift[None], up_bias[None], ups
        )
    downs = (down, near(down), down_far, near(down_far))
    made = mlp_down(ids, activated, cotangent, downs, o0, o1)
    context_low, g0, g1 = made[2:]
    half = rows // 2

    out = LineSum(
        made[:2],
        [
            partial(
                finish, finish_out_kernel, "finish_out", start, half, 1,
                (tokens, dense_bias[None], down_bias[None]),
            )
            for start in (0, half)
        ],
    )
    back0 = attend_backward(ids, block_lists, q0, g0, o0, lse0, tables, keys[0])
    back1 = attend_backward(ids, block_lists, q1, after(g1, back0), o1, lse1, tables, keys[1])
    if split:
        grads = []
        for own, other, _ in (back0, back1):
            grads += [own, swap(other, "context", 2, 1)]
    else:
        grads = [
            lax.psum_scatter(whole_grad, "context", scatter_dimension=0, tiled=True)
            for whole_grad, _ in (back0, back1)
        ]
    mark = out.add(0, (back1, grads[1]) if split else back1)
    hidden_grad, e2, sums = mlp_backward(
        ids, tokens, after(cotangent, mark),
        second_gain[None], slope, ups + downs,
    )
    made = input_grad(
        ids, tokens, e2, first_gain[None], sums, (back0[-1], back1[-1]),
        tables, projects, grads, split,
    )
    projected_grad, sums = made[2:]
    line = LineSum(
        made[:2],
        [
            partial(
                finish, partial(finish_in_kernel, half), "finish_in", start, half, 2,
                (tokens, cotangent),
            )
            for start in (0, half)
        ],
    )
    mark = out.add(1, made[0])
    mlp_keep, *mlp_send = weight_parts(
        mlp_weights_kernel, "mlp_weights", ids, 2 * units,
        activated, cotangent, normed_two, after(hidden_grad, mark),
    )
    mlp_got = swap(mlp_send, "fsdp", 4, 1)
    mark = out.end(0, mlp_keep)
    rest_keep, *rest_send = weight_parts(
        rest_weights_kernel, "rest_weights", ids, 4 * SHARD,
        context_low, cotangent, normed_one, after(projected_grad, mark),
    )
    rest_got = swap(rest_send, "fsdp", 4, 1)
    mark = line.add(0, rest_keep)
    mark = out.end(1, mark)
    mark = out.arrive(0, mark)
    mlp_here, mlp_there = halves(mlp_keep, after(mlp_got, mark))
    mlp_got = swap(mlp_there, "fsdp", 4, 2)
    rest_here, rest_there = halves(rest_keep, after(rest_got, mlp_here))
    rest_got = swap(rest_there, "fsdp", 4, 2)
    mark = out.arrive(1, rest_here)
    mark = line.add(1, mark)
    mark = line.end(0, mark)
    mlp_part = add(mlp_here, after(mlp_got, mark))
    if split:
        mlp_got = swap(mlp_part, "context", 2, 1)
    rest_part = add(rest_here, after(rest_got, mlp_part))
    if split:
        rest_got = swap(rest_part, "context", 2, 1)
    mark = line.end(1, rest_part)
    norms = line.decode(mark)
    sums = jnp.concatenate([norms[0:2], sums[2:4], norms[2:4], sums[6:8]], axis=0)
    mark = sums
    for step in [("fsdp", 4, 1), ("fsdp", 4, 2)]:
        sums = mark = add(sums, swap(after(sums, mark), *step), f32)
    hop = swap(sums, "context", contexts, 1)
    layer_out = mark = out.result([0, 1], mark)
    tokens_grad = mark = line.result([0], mark, total=rows)
    if split:
        down_grad, up_grad = call(
            mlp_last_kernel, "mlp_last", (mlp_part, after(mlp_got, mark)),
            [((units, SHARD), f32), ((SHARD, units), f32)],
        )
        dense_grad, project_grad = call(
            rest_last_kernel, "rest_last", (rest_part, after(rest_got, down_grad)),
            [((SHARD, SHARD), f32), ((3, SHARD, SHARD), f32)],
        )
        mark = dense_grad
        project_grad = project_grad.transpose(1, 0, 2)
    else:
        mlp_part, rest_part = lax.psum(
            (mlp_part.astype(f32), rest_part.astype(f32)), "context"
        )
        back_blocks = lambda g: g.reshape(-1, SHARD, SHARD).transpose(1, 0, 2)
        down_grad = mlp_part[:units]
        up_grad = back_blocks(mlp_part[units:]).reshape(SHARD, units)
        dense_grad = rest_part[:SHARD]
        project_grad = back_blocks(rest_part[SHARD:])
    sums = mark = add(sums, after(hop, mark), f32)
    for i in range(1, contexts.bit_length() - 1):
        sums = mark = add(sums, swap(after(sums, mark), "context", contexts, 1 << i), f32)
    tokens_grad = line.result([1], mark, start=half, total=rows, before=tokens_grad)
    norms = sums
    up_total, bias_sum = sums[2], sums[3]
    project_total = sums[6, : project_bias.size]
    return (
        layer_out,
        tokens_grad,
        project_grad,
        project_total.reshape(3, -1),
        dense_grad,
        bias_sum,
        up_grad,
        up_total,
        down_grad,
        bias_sum,
        norms[4],
        norms[5],
        norms[0],
        norms[1],
    )


def solution(mesh):
    tokens = P(("fsdp", "context"), None)
    line = P(("fsdp", "context"))
    in_specs = (
        tokens, tokens, line, line, P("fsdp", None), tokens,
        P("fsdp", None, "tensor"), P(None, "tensor"), P("tensor", "fsdp"), P(),
        P("fsdp", "tensor"), P("tensor"), P("tensor", "fsdp"), P(), P(), P(), P(), P(),
    )
    out_specs = (
        tokens, tokens, P("fsdp", None, "tensor"), P(None, "tensor"), P("tensor", "fsdp"), P(),
        P("fsdp", "tensor"), P("tensor"), P("tensor", "fsdp"), P(), P(), P(), P(), P(),
    )
    run = partial(body, mesh.shape["context"])
    return jax.shard_map(run, mesh=mesh, in_specs=in_specs, out_specs=out_specs, check_vma=False)
```

```python
from functools import partial

import jax
import jax.numpy as jnp
from jax import lax
from jax.experimental import pallas as pl
from jax.experimental.pallas import tpu as pltpu
from jax.sharding import PartitionSpec as P

HD = 64
ROT = 16
BLK = 512
HALF = 256
PAIR = 2 * HD
SHARD = 256
EXTRA = 16

epsilon = 1e-05
masked = -1e30
bf16 = jnp.bfloat16
f32 = jnp.float32
scale2 = HD ** (-0.5) * 1.4426950408889634
NT = (((1,), (1,)), ((), ()))
NN = (((1,), (0,)), ((), ()))
TN = (((0,), (0,)), ((), ()))


def dot(a, b, dims):
    return lax.dot_general(a, b, dims, preferred_element_type=f32)


def params(mib):
    return pltpu.CompilerParams(vmem_limit_bytes=mib * 1024 * 1024)


def cost(micros):
    return pl.CostEstimate(
        flops=int(1.15e9 * micros), bytes_accessed=int(3.7e6 * micros), transcendentals=0
    )


def whole(shape):
    return pl.BlockSpec(shape, lambda *_: (0,) * len(shape))


smem = pl.BlockSpec(memory_space=pltpu.SMEM)


def norm_rows(x):
    mean = jnp.mean(x, axis=-1, keepdims=True)
    centered = x - mean
    variance = jnp.mean(centered * centered, axis=-1, keepdims=True)
    factor = lax.rsqrt(variance + epsilon)
    return centered * factor, factor


def rotate_lanes(x, cos, sin, sign):
    lane = lax.broadcasted_iota(jnp.int32, x.shape, 1) % HD
    left = pltpu.roll(x, PAIR - ROT // 2, 1)
    right = pltpu.roll(x, ROT // 2, 1)
    return x * cos + jnp.where(lane < ROT // 2, -sign * left, sign * right) * sin


def columns(index, width):
    return pl.ds(pl.multiple_of(index * width, width), width)


def norm_kernel(x, gain, shift, out):
    normal, _ = norm_rows(x[...].astype(f32))
    out[...] = (normal * gain[...] + shift[...]).astype(bf16)


def norm(x, gain, shift, tile=256):
    row = pl.BlockSpec((tile, x.shape[1]), lambda i: (i, 0))
    return call(
        norm_kernel, "norm", (x, gain, shift), (x.shape, bf16), x.shape[0] // tile,
        [row, whole(gain.shape), whole(shift.shape)], [row],
    )


def project_kernel(ids, n1, w0, w1, w2, w3, bias, cos, sin, q0, q1, kv0, kv1, weight):
    depth, width = w0.shape[0] // 3, w0.shape[1]

    @pl.when(pl.program_id(0) == 0)
    def _():
        for i, piece in enumerate((w0, w1, w2, w3)):
            for part in range(3):
                weight[part, columns(ids[i], depth), :] = piece[
                    part * depth : (part + 1) * depth, :
                ]

    for part in range(3):
        total = dot(n1[...], weight[part], NN) + bias[part : part + 1, :]
        for pair, (q, kv) in enumerate(((q0, kv0), (q1, kv1))):
            half = total[:, pair * PAIR : (pair + 1) * PAIR]
            if part < 2:
                half = rotate_lanes(half, cos[...], sin[...], 1.0)
            if part == 0:
                q[...] = half.astype(bf16)
            else:
                kv[:, (part - 1) * PAIR : part * PAIR] = half.astype(bf16)


def project(ids, n1, weights, bias, tables, tile=256):
    rows, wide = n1.shape
    row = lambda w: pl.BlockSpec((tile, w), lambda i: (i, 0))
    s = jax.ShapeDtypeStruct
    return pl.pallas_call(
        project_kernel,
        grid=(rows // tile,),
        in_specs=[smem, row(wide)]
        + [whole(v.shape) for v in (*weights, bias)]
        + [row(PAIR)] * 2,
        out_specs=[row(PAIR)] * 2 + [row(2 * PAIR)] * 2,
        out_shape=[s((rows, PAIR), bf16)] * 2 + [s((rows, 2 * PAIR), bf16)] * 2,
        scratch_shapes=[pltpu.VMEM((3, wide, weights[0].shape[1]), bf16)],
        compiler_params=params(16),
        cost_estimate=cost(4.3),
        name="project",
    )(ids, n1, *weights, bias, *tables)


def head_lanes(shape, head):
    return lax.broadcasted_iota(jnp.int32, shape, 1) // HD == head


def sublanes(index, size):
    return pl.ds(pl.multiple_of(index * size, size), size)


def triangle(rows, cols):
    return lax.broadcasted_iota(jnp.int32, (rows, cols), 0) <= lax.broadcasted_iota(
        jnp.int32, (rows, cols), 1
    )


def slot_of(ids, lists, slots, block, step):
    entry = lists[block, step]
    return jnp.where(entry < 0, entry, lax.rem(entry - ids[9] + slots, slots))


def head_of(ref, block, head):
    value = ref[sublanes(block, BLK), :]
    return jnp.where(head_lanes(value.shape, head), value, jnp.zeros_like(value))


def attend_forward_kernel(slots, low, count, first, last, ids, lists, q, kv, *refs):
    if not first:
        ins, refs = refs[:2], refs[2:]
    outs, (turned, state, acc) = refs[:2], refs[2:]
    blocks = q.shape[0] // BLK

    def turn(slot, unused):
        turned[slot] = kv[sublanes(slot, BLK), PAIR:].T
        return unused

    lax.fori_loop(0, count, turn, 0)
    if not first:
        state[...] = ins[0][...]
        acc[...] = ins[1][...]

    def one(line, unused):
        block, head = lax.div(line, 2), lax.rem(line, 2)
        own = ids[8] + block
        rows, part = sublanes(line, HD), sublanes(head, HD)
        tops, sums = pl.ds(line, 1), pl.ds(8 + line, 1)
        query = head_of(q, block, head)

        if first:
            upper, lower = sublanes(2 * (own - low), HALF), sublanes(2 * (own - low) + 1, HALF)
            scores = dot(kv[upper, :PAIR], query, NT) * scale2
            scores = jnp.where(triangle(HALF, BLK), scores, masked)
            late = dot(kv[lower, :PAIR], query[HALF:, :], NT) * scale2
            late = jnp.where(triangle(HALF, HALF), late, masked)
            state[tops, :] = jnp.max(scores, axis=0, keepdims=True)
            state[tops, HALF:] = jnp.maximum(
                state[tops, HALF:], jnp.max(late, axis=0, keepdims=True)
            )
            weight = jnp.exp2(scores - state[tops, :])
            late = jnp.exp2(late - state[tops, HALF:])
            state[sums, :] = jnp.sum(weight, axis=0, keepdims=True)
            state[sums, HALF:] += jnp.sum(late, axis=0, keepdims=True)
            acc[rows, :] = dot(turned[own - low, part, :HALF], weight.astype(bf16), NN)
            acc[rows, HALF:] += dot(turned[own - low, part, HALF:], late.astype(bf16), NN)

        def entry(step, unused):
            slot = slot_of(ids, lists, slots, block, step)

            @pl.when((slot >= low) & (slot < low + count) & (slot != own))
            def _():
                scores = dot(kv[sublanes(slot - low, BLK), :PAIR], query, NT) * scale2
                old = state[tops, :]
                top = jnp.maximum(old, jnp.max(scores, axis=0, keepdims=True))
                weight = jnp.exp2(scores - top)
                shrink = jnp.exp2(old - top)
                state[tops, :] = top
                state[sums, :] = state[sums, :] * shrink + jnp.sum(weight, axis=0, keepdims=True)
                acc[rows, :] = acc[rows, :] * shrink + dot(
                    turned[slot - low, part, :], weight.astype(bf16), NN
                )

            return unused

        lax.fori_loop(0, lists.shape[1], entry, 0)
        if last:
            outs[1][pl.ds(line, 1), :] = state[tops, :] + jnp.log2(state[sums, :])
            acc[rows, :] = acc[rows, :] * (1.0 / state[sums, :])
        return unused

    lax.fori_loop(0, 2 * blocks, one, 0)
    if last:

        def give(block, unused):
            outs[0][sublanes(block, BLK), :] = acc[sublanes(block, PAIR), :].T
            return unused

        lax.fori_loop(0, blocks, give, 0)
    else:
        outs[0][...] = state[...]
        outs[1][...] = acc[...]


def attend_forward(ids, lists, slots, q, kv, low, carried, last, micros=0):
    count = kv.shape[0] // BLK
    rows = q.shape[0]
    tall = rows // BLK * PAIR
    vmem = pl.BlockSpec(memory_space=pltpu.VMEM)
    s = jax.ShapeDtypeStruct
    shapes = [s((rows, PAIR), f32), s((8, BLK), f32)] if last else [
        s((16, BLK), f32), s((tall, BLK), f32)
    ]
    return pl.pallas_call(
        partial(attend_forward_kernel, slots, low, count, carried is None, last),
        in_specs=[smem, smem] + [vmem] * (2 + len(carried or ())),
        out_specs=[vmem] * 2,
        out_shape=shapes,
        scratch_shapes=[
            pltpu.VMEM((count, PAIR, BLK), bf16),
            pltpu.VMEM((16, BLK), f32),
            pltpu.VMEM((tall, BLK), f32),
        ],
        compiler_params=params(8 + 2 * count),
        cost_estimate=cost(micros),
        name="attend_forward",
    )(ids, lists, q, kv, *(carried or ()))


def attend_backward_kernel(slots, split, ids, lists, q, g, o, lse, cos, sin, *refs):
    outs = 2 if split else 1
    parts = refs[: -6 - outs]
    grads = refs[-6 - outs : -6]
    qg, kv, turned, acc, total, deltas = refs[-6:]
    blocks = q.shape[0] // BLK
    start = 0
    for part in parts:
        kv[start : start + part.shape[0], :] = part[...]
        start += part.shape[0]

    def prepare(slot, unused):
        turned[slot] = kv[sublanes(slot, BLK), :PAIR].T
        total[sublanes(slot, BLK), :] = jnp.zeros((BLK, 2 * PAIR), f32)
        return unused

    lax.fori_loop(0, slots, prepare, 0)
    pick = (
        lax.broadcasted_iota(jnp.int32, (8, PAIR), 1) // HD
        == lax.broadcasted_iota(jnp.int32, (8, PAIR), 0)
    ).astype(f32)

    def delta_of(block, unused):
        span = sublanes(block, BLK)
        deltas[sublanes(block, 8), :] = lax.dot_general(
            pick,
            o[span, :] * g[span, :].astype(f32),
            NT,
            preferred_element_type=f32,
            precision=lax.Precision.HIGHEST,
        )
        return unused

    lax.fori_loop(0, blocks, delta_of, 0)

    def one(line, unused):
        block, head = lax.div(line, 2), lax.rem(line, 2)
        own = ids[8] + block
        rows, part = sublanes(line, HD), sublanes(head, HD)
        query, grad = head_of(q, block, head), head_of(g, block, head)
        log_sum = lse[pl.ds(line, 1), :]
        delta = deltas[pl.ds(block * 8 + head, 1), :]

        def tile(here, keys, skip=0, keep=None):
            scores = dot(kv[here, :PAIR], query[skip:, :], NT) * scale2
            prob = jnp.exp2(scores - log_sum[:, skip:])
            if keep is not None:
                prob = jnp.where(keep, prob, 0.0)
            prob_grad = dot(kv[here, PAIR:], grad[skip:, :], NT)
            score_grad = (prob * (prob_grad - delta[:, skip:])).astype(bf16)
            total[here, PAIR:] += dot(prob.astype(bf16), grad[skip:, :], NN)
            total[here, :PAIR] += dot(score_grad, query[skip:, :], NN)
            return dot(keys, score_grad, NN)

        acc[rows, :] = tile(
            sublanes(2 * own, HALF), turned[own, part, :HALF], 0, triangle(HALF, BLK)
        )
        acc[rows, HALF:] += tile(
            sublanes(2 * own + 1, HALF), turned[own, part, HALF:], HALF, triangle(HALF, HALF)
        )

        def entry(step, unused):
            slot = slot_of(ids, lists, slots, block, step)

            @pl.when((slot >= 0) & (slot != own))
            def _():
                acc[rows, :] += tile(sublanes(slot, BLK), turned[slot, part, :])

            return unused

        lax.fori_loop(0, lists.shape[1], entry, 0)
        return unused

    lax.fori_loop(0, 2 * blocks, one, 0)

    def give(block, unused):
        span = sublanes(block, BLK)
        grad_q = acc[sublanes(block, PAIR), :].T * (HD ** (-0.5))
        qg[span, :] = rotate_lanes(grad_q, cos[span, :], sin[span, :], -1.0).astype(bf16)
        return unused

    lax.fori_loop(0, blocks, give, 0)
    start = 0
    for out in grads:
        out[...] = total[start : start + out.shape[0], :].astype(out.dtype)
        start += out.shape[0]


def attend_backward(ids, lists, q, g, o, lse, tables, kvs):
    slots = sum(part.shape[0] for part in kvs) // BLK
    rows = q.shape[0]
    split = len(kvs) == 2
    shapes = [jax.ShapeDtypeStruct(kvs[0].shape, bf16)]
    if split:
        shapes.append(jax.ShapeDtypeStruct(kvs[1].shape, bf16))
    shapes.append(jax.ShapeDtypeStruct((rows, PAIR), bf16))
    vmem = pl.BlockSpec(memory_space=pltpu.VMEM)
    return pl.pallas_call(
        partial(attend_backward_kernel, slots, split),
        grid=(),
        in_specs=[smem, smem] + [vmem] * (6 + len(kvs)),
        out_specs=[vmem] * len(shapes),
        out_shape=shapes,
        scratch_shapes=[
            pltpu.VMEM((slots * BLK, 2 * PAIR), bf16),
            pltpu.VMEM((slots, PAIR, BLK), bf16),
            pltpu.VMEM((rows // BLK * PAIR, BLK), f32),
            pltpu.VMEM((slots * BLK, 2 * PAIR), f32),
            pltpu.VMEM((rows // BLK * 8, BLK), f32),
        ],
        compiler_params=params(14 + slots),
        cost_estimate=cost(0),
        name="attend_backward",
    )(ids, lists, q, g, o, lse, *tables, *kvs)


def unpack_up(ids, pieces, up):
    for i, piece in enumerate(pieces):
        for n in range(up.shape[1] // SHARD):
            up[columns(ids[i], SHARD), n * SHARD : (n + 1) * SHARD] = piece[
                n * SHARD : (n + 1) * SHARD, :
            ]


def unpack_down(ids, pieces, down, dense):
    units = down.shape[0]
    for i, piece in enumerate(pieces):
        where = columns(ids[i], SHARD)
        down[:, where] = piece[:units, :]
        if dense is not None:
            dense[:, where] = piece[units:, :]


def mlp_up_kernel(ids, x, gain, shift, up_bias, p0, p1, p2, p3, n2, act, slope, up):
    @pl.when(pl.program_id(0) == 0)
    def _():
        unpack_up(ids, (p0, p1, p2, p3), up)

    normal, _ = norm_rows(x[...].astype(f32))
    normed = (normal * gain[...] + shift[...]).astype(bf16)
    n2[...] = normed
    hidden = dot(normed, up[...], NN) + up_bias[...]
    cdf = 0.5 + 0.5 * lax.erf(hidden * (2.0 ** -0.5))
    pdf = jnp.exp(hidden * hidden * -0.5) * 0.3989422804014327
    act[...] = (hidden * cdf).astype(bf16)
    slope[...] = (cdf + hidden * pdf).astype(bf16)


def mlp_up(ids, x, gain, shift, up_bias, pieces, tile=256):
    rows, width = x.shape
    units = up_bias.shape[1]
    row = lambda w: pl.BlockSpec((tile, w), lambda i: (i, 0))
    s = jax.ShapeDtypeStruct
    return pl.pallas_call(
        mlp_up_kernel,
        grid=(rows // tile,),
        in_specs=[smem, row(width)] + [whole(a.shape) for a in (gain, shift, up_bias, *pieces)],
        out_specs=[row(width), row(units), row(units)],
        out_shape=[s((rows, width), bf16), s((rows, units), bf16), s((rows, units), bf16)],
        scratch_shapes=[pltpu.VMEM((width, units), bf16)],
        compiler_params=params(24),
        cost_estimate=cost(0),
        name="mlp_up",
    )(ids, x, gain, shift, up_bias, *pieces)


def store_part(outs, sizes, value):
    tile = value.shape[0]
    step = pl.program_id(0)
    start = 0
    for out, size in zip(outs, sizes):
        count = size // tile

        @pl.when((step >= start) & (step < start + count))
        def _():
            out[pl.ds(pl.multiple_of((step - start) * tile, tile), tile), :] = value

        start += count


def mlp_down_kernel(
    rows, ids, act, cot, p0, p1, p2, p3, o0, o1, first, second, ctx, g0, g1, down, dense
):
    @pl.when(pl.program_id(0) == 0)
    def _():
        unpack_down(ids, (p0, p1, p2, p3), down, dense)

    context_grad = dot(cot[...], dense[...], NT)
    g0[...] = context_grad[:, :PAIR].astype(bf16)
    g1[...] = context_grad[:, PAIR:].astype(bf16)
    ctx[:, :PAIR] = o0[...].astype(bf16)
    ctx[:, PAIR:] = o1[...].astype(bf16)
    value = dot(ctx[...], dense[...], NN) + dot(act[...], down[...], NN)
    store_part((first, second), (rows // 2, rows // 2), value.astype(bf16))


def mlp_down(ids, act, cot, pieces, o0, o1, tile=256):
    rows, width = cot.shape
    units = act.shape[1]
    row = lambda w: pl.BlockSpec((tile, w), lambda i: (i, 0))
    s = jax.ShapeDtypeStruct
    return pl.pallas_call(
        partial(mlp_down_kernel, rows),
        grid=(rows // tile,),
        in_specs=[smem, row(units), row(width)]
        + [whole(a.shape) for a in pieces]
        + [row(PAIR), row(PAIR)],
        out_specs=[whole((rows // 2, width))] * 2 + [row(2 * PAIR), row(PAIR), row(PAIR)],
        out_shape=[s((rows // 2, width), bf16)] * 2
        + [s((rows, 2 * PAIR), bf16), s((rows, PAIR), bf16), s((rows, PAIR), bf16)],
        scratch_shapes=[
            pltpu.VMEM((units, width), bf16),
            pltpu.VMEM((2 * PAIR, width), bf16),
        ],
        compiler_params=params(26),
        cost_estimate=cost(1),
        name="mlp_down",
    )(ids, act, cot, *pieces, o0, o1)


def mlp_backward_kernel(
    ids, x, cot, gain, slope, u0, u1, u2, u3, d0, d1, d2, d3, hid, e2, sums, up, down
):
    @pl.when(pl.program_id(0) == 0)
    def _():
        sums[...] = jnp.zeros_like(sums)
        unpack_up(ids, (u0, u1, u2, u3), up)
        unpack_down(ids, (d0, d1, d2, d3), down, None)

    low = (dot(cot[...], down[...], NT) * slope[...].astype(f32)).astype(bf16)
    hid[...] = low
    grad = dot(low, up[...], NT)
    normal, _ = norm_rows(x[...].astype(f32))
    sums[0:1, :] += jnp.sum(grad * normal, axis=0, keepdims=True)
    sums[1:2, :] += jnp.sum(grad, axis=0, keepdims=True)
    sums[2:3, :] += jnp.sum(low.astype(f32), axis=0, keepdims=True)
    sums[3:4, :] += jnp.sum(cot[...].astype(f32), axis=0, keepdims=True)
    e2[...] = (grad * gain[...]).astype(bf16)


def mlp_backward(ids, x, cot, gain, slope, pieces, tile=256):
    rows, width = x.shape
    units = slope.shape[1]
    row = lambda w: pl.BlockSpec((tile, w), lambda i: (i, 0))
    s = jax.ShapeDtypeStruct
    return pl.pallas_call(
        mlp_backward_kernel,
        grid=(rows // tile,),
        in_specs=[smem, row(width), row(width), whole(gain.shape), row(units)]
        + [whole(a.shape) for a in pieces],
        out_specs=[row(units), row(width), whole((8, width))],
        out_shape=[s((rows, units), bf16), s((rows, width), bf16), s((8, width), f32)],
        scratch_shapes=[
            pltpu.VMEM((width, units), bf16),
            pltpu.VMEM((units, width), bf16),
        ],
        compiler_params=params(26),
        cost_estimate=cost(1),
        name="mlp_backward",
    )(ids, x, cot, gain, slope, *pieces)


def mlp_weights_kernel(ids, act, cot, n2, hid, keep, near, far):
    units = act.shape[1]
    step = pl.program_id(0)
    index = ids[4 + step]
    for out, when in ((near, step == 0), (far, step == 1), (keep, step >= 2)):

        @pl.when(when)
        def _():
            out[0, :units, :] = dot(act[...], cot[:, columns(index, SHARD)], TN).astype(bf16)
            lhs = n2[:, columns(index, SHARD)]
            for n in range(units // SHARD):
                at = slice(n * SHARD, (n + 1) * SHARD)
                out[0, units + n * SHARD : units + (n + 1) * SHARD, :] = dot(
                    lhs, hid[:, at], TN
                ).astype(bf16)


def rest_weights_kernel(ids, ctx, cot, n1, pg, keep, near, far):
    width = ctx.shape[1]
    step = pl.program_id(0)
    index = ids[4 + step]
    for out, when in ((near, step == 0), (far, step == 1), (keep, step >= 2)):

        @pl.when(when)
        def _():
            out[0, :width, :] = dot(ctx[...], cot[:, columns(index, SHARD)], TN).astype(bf16)
            lhs = n1[:, columns(index, SHARD)]
            for n in range(3):
                at = slice(n * SHARD, (n + 1) * SHARD)
                out[0, width + n * SHARD : width + (n + 1) * SHARD, :] = dot(
                    lhs, pg[:, at], TN
                ).astype(bf16)


def weight_parts(kernel, name, ids, tall, *args):
    s = lambda n: jax.ShapeDtypeStruct((n, tall, SHARD), bf16)
    return pl.pallas_call(
        kernel,
        grid=(4,),
        in_specs=[smem] + [whole(a.shape) for a in args],
        out_specs=[
            pl.BlockSpec((1, tall, SHARD), lambda i: (jnp.maximum(i - 2, 0), 0, 0)),
            whole((1, tall, SHARD)),
            whole((1, tall, SHARD)),
        ],
        out_shape=[s(2), s(1), s(1)],
        compiler_params=params(20),
        cost_estimate=cost(0),
        name=name,
    )(ids, *args)


def input_grad_kernel(
    split, sizes, ids, x, e2, gain, sums_two, qg0, qg1, cos, sin, *refs
):
    count = 4 if split else 2
    weights, refs = refs[:4], refs[4:]
    grads, es, (pg, sums, first) = refs[:count], refs[count:-3], refs[-3:]
    depth, width = weights[0].shape[0] // 3, 2 * PAIR

    @pl.when(pl.program_id(0) == 0)
    def _():
        sums[...] = sums_two[...]

    pg[:, 0:PAIR] = qg0[...]
    pg[:, PAIR : 2 * PAIR] = qg1[...]
    for pair in range(2):
        if split:
            own, other = grads[2 * pair : 2 * pair + 2]
            grad = own[...].astype(f32) + other[...].astype(f32)
        else:
            grad = grads[pair][...].astype(f32)
        key = rotate_lanes(
            grad[:, :PAIR] * (HD ** (-0.5)), cos[...], sin[...], -1.0
        )
        at = width + pair * PAIR
        pg[:, at : at + PAIR] = key.astype(bf16)
        pg[:, at + width : at + width + PAIR] = grad[:, PAIR:].astype(bf16)
    sums[6:7, : 3 * width] += jnp.sum(pg[...].astype(f32), axis=0, keepdims=True)
    normal, _ = norm_rows(x[...].astype(f32))
    for piece in range(4):
        where = columns(ids[piece], depth)
        total = dot(pg[:, :width], weights[piece][:depth, :], NT)
        total += dot(pg[:, width : 2 * width], weights[piece][depth : 2 * depth, :], NT)
        total += dot(pg[:, 2 * width :], weights[piece][2 * depth :, :], NT)
        first[:, where] = total
    grad = first[...]
    store_part(es, sizes, (grad * gain[...] + e2[...].astype(f32)).astype(bf16))
    sums[4:5, :] += jnp.sum(grad * normal, axis=0, keepdims=True)
    sums[5:6, :] += jnp.sum(grad, axis=0, keepdims=True)

    @pl.when(pl.program_id(0) == pl.num_programs(0) - 1)
    def _():
        terms = split_terms(jnp.concatenate([sums[0:2, :], sums[4:6, :]], axis=0))
        es[0][sizes[0] :, :] = terms


def input_grad(ids, x, e2, gain, sums, qgs, tables, weights, grads, split, tile=256):
    rows, width = x.shape
    row = lambda w: pl.BlockSpec((tile, w), lambda i: (i, 0))
    s = jax.ShapeDtypeStruct
    units = 6 * PAIR
    sizes = (rows // 2,) * 2
    parts = [(sizes[0] + EXTRA, width), *[(size, width) for size in sizes[1:]]]
    return pl.pallas_call(
        partial(input_grad_kernel, split, sizes),
        grid=(rows // tile,),
        in_specs=[smem, row(width), row(width), whole(gain.shape), whole(sums.shape)]
        + [row(PAIR), row(PAIR)]
        + [row(PAIR)] * 2
        + [whole(w.shape) for w in weights]
        + [row(2 * PAIR)] * len(grads),
        out_specs=[whole(part) for part in parts] + [row(units), whole((8, width))],
        out_shape=[s(part, bf16) for part in parts]
        + [s((rows, units), bf16), s((8, width), f32)],
        scratch_shapes=[pltpu.VMEM((tile, width), f32)],
        compiler_params=params(24),
        cost_estimate=cost(4),
        name="input_grad",
    )(ids, x, e2, gain, sums, *qgs, *tables, *weights, *grads)


def call(kernel, name, args, shapes, grid=1, in_specs=None, out_specs=None, aliases=None, mib=16, micros=0):
    s = jax.ShapeDtypeStruct
    many = isinstance(shapes, list)
    shapes = [s(*shape) for shape in (shapes if many else [shapes])]
    out = pl.pallas_call(
        kernel,
        grid=(grid,),
        in_specs=in_specs or [whole(a.shape) for a in args],
        out_specs=out_specs or [whole(shape.shape) for shape in shapes],
        out_shape=shapes,
        input_output_aliases=aliases or {},
        compiler_params=params(mib),
        cost_estimate=cost(micros),
        name=name,
    )(*args)
    return out if many else out[0]


def add_kernel(a, b, out):
    out[...] = (a[...].astype(f32) + b[...].astype(f32)).astype(out.dtype)


def add(a, b, dtype=bf16, grid=2):
    grid = grid if a.shape[0] > 8 else 1
    row = pl.BlockSpec((a.shape[0] // grid, a.shape[1]), lambda i: (i, 0))
    return call(add_kernel, "add", (a, b), (a.shape, dtype), grid, [row, row], [row])


def split_terms(value):
    high = value.astype(bf16)
    rest = value - high.astype(f32)
    middle = rest.astype(bf16)
    low = (rest - middle.astype(f32)).astype(bf16)
    return jnp.concatenate([high, middle, low, jnp.zeros_like(low)], axis=0)


def join_terms(terms):
    terms = terms.astype(f32)
    return terms[0:4] + terms[4:8] + terms[8:12]


def add_extra_kernel(a, b, out):
    rows = a.shape[0] - EXTRA
    out[:rows, :] = (a[:rows, :].astype(f32) + b[:rows, :].astype(f32)).astype(out.dtype)
    out[rows:, :] = split_terms(join_terms(a[rows:, :]) + join_terms(b[rows:, :]))


def add_extra(a, b):
    return call(add_extra_kernel, "add_extra", (a, b), (a.shape, a.dtype))


def finish_out_kernel(a, b, x, dense_bias, down_bias, out):
    total = a[...].astype(f32) + b[...].astype(f32)
    out[...] = (x[...].astype(f32) + total + (dense_bias[...] + down_bias[...])).astype(bf16)


def finish_in_kernel(rows, a, b, x, upstream, out):
    def one(step, unused):
        here = sublanes(step, 128)
        total = a[here, :].astype(f32) + b[here, :].astype(f32)
        normal, factor = norm_rows(x[here, :].astype(f32))
        mean_e = jnp.mean(total, axis=-1, keepdims=True)
        mean_en = jnp.mean(total * normal, axis=-1, keepdims=True)
        result = upstream[here, :].astype(f32) + factor * (total - mean_e - normal * mean_en)
        out[here, :] = result.astype(bf16)
        return unused

    lax.fori_loop(0, rows // 128, one, 0)
    if a.shape[0] > rows:
        out[rows:, :] = split_terms(join_terms(a[rows:, :]) + join_terms(b[rows:, :]))


def finish(kernel, name, start, rows, of_rows, arrays, a, b):
    block = pl.BlockSpec((rows, a.shape[1]), lambda i: (start // rows, 0))
    specs = [whole(a.shape)] * 2 + [
        block if i < of_rows else whole(v.shape) for i, v in enumerate(arrays)
    ]
    return call(kernel, name, (a, b, *arrays), (a.shape, bf16), 1, specs)


def choose_kernel(sizes, flag, *refs):
    out, count = refs[-1], len(sizes)
    for parts, when in ((refs[:count], flag[0] > 0), (refs[count : 2 * count], flag[0] <= 0)):

        @pl.when(when)
        def _():
            start = 0
            for part, size in zip(parts, sizes):
                out[start : start + size, :] = part[:size, :]
                start += size


def choose(flag, ours, theirs, sizes, start=0, total=None, before=None):
    rows, width = sum(sizes), ours[0].shape[1]
    args = (flag, *ours, *theirs)
    specs, aliases = [smem] + [whole(v.shape) for v in args[1:]], {}
    if before is not None:
        aliases = {len(args): 0}
        args, specs = args + (before,), specs + [pl.BlockSpec(memory_space=pl.ANY)]
    return call(
        partial(choose_kernel, sizes), "choose", args, ((total or rows, width), bf16), 1, specs,
        [pl.BlockSpec((rows, width), lambda i: (start // rows, 0))], aliases,
    )


def decode_kernel(flag, ours, theirs, out):
    out[0:4, :] = jnp.where(flag[0] > 0, join_terms(ours[...]), join_terms(theirs[...]))
    out[4:8, :] = jnp.zeros((4, out.shape[1]), f32)


def decode(flag, ours, theirs):
    at = ours.shape[0] // EXTRA - 1
    block = pl.BlockSpec((EXTRA, ours.shape[1]), lambda i: (at, 0))
    return call(
        decode_kernel, "decode", (flag, ours, theirs), ((8, ours.shape[1]), f32), 1,
        [smem, block, block],
    )


def halves_kernel(keep, near, far, here, there):
    here[...] = keep[0].astype(f32) + near[0].astype(f32)
    there[...] = (keep[1].astype(f32) + far[0].astype(f32)).astype(bf16)


def halves(keep, got, grid=2, micros=0):
    tall, width = keep.shape[1:]
    block = lambda n: pl.BlockSpec((n, tall // grid, width), lambda i: (0, i, 0))
    row = pl.BlockSpec((tall // grid, width), lambda i: (i, 0))
    return call(
        halves_kernel, "halves", (keep, *got), [((tall, width), f32), ((tall, width), bf16)],
        grid, [block(2), block(1), block(1)], [row, row], micros=micros,
    )


def mlp_last_kernel(a, b, down, up):
    units = down.shape[0]
    down[...] = a[:units, :].astype(f32) + b[:units, :].astype(f32)
    for n in range(units // SHARD):
        at = slice(units + n * SHARD, units + (n + 1) * SHARD)
        up[:, n * SHARD : (n + 1) * SHARD] = a[at, :].astype(f32) + b[at, :].astype(f32)


def rest_last_kernel(a, b, dense, project):
    dense[...] = a[:SHARD, :].astype(f32) + b[:SHARD, :].astype(f32)
    for n in range(3):
        at = slice((n + 1) * SHARD, (n + 2) * SHARD)
        project[n] = a[at, :].astype(f32) + b[at, :].astype(f32)


def swap(values, axis, size, bit):
    pairs = [(i, i ^ bit) for i in range(size)]
    return jax.tree.map(lambda v: lax.ppermute(v, axis, pairs), values)


def after(values, *others):
    return lax.optimization_barrier((values, others))[0]


class LineSum:
    def __init__(self, parts, finishes):
        place = lax.axis_index("tensor")
        self.flag = ((place == 1) | (place == 2)).astype(jnp.int32)[None]
        self.parts, self.finishes = parts, finishes
        self.first = [lax.ppermute(part, "tensor", [(0, 1), (3, 2)]) for part in parts]
        self.sums, self.second, self.finals, self.third = {}, {}, {}, {}

    def add(self, i, mark):
        part, got = self.parts[i], after(self.first[i], mark)
        self.sums[i] = add_extra(part, got) if part.shape[0] % 128 else add(part, got)
        self.second[i] = lax.ppermute(self.sums[i], "tensor", [(1, 2), (2, 1)])
        return self.sums[i]

    def end(self, i, mark):
        self.finals[i] = self.finishes[i](self.sums[i], after(self.second[i], mark))
        self.third[i] = lax.ppermute(self.finals[i], "tensor", [(1, 0), (2, 3)])
        return self.finals[i]

    def arrive(self, i, mark):
        self.third[i] = after(self.third[i], mark)
        return self.third[i]

    def result(self, indices, mark, **place):
        theirs = after([self.third[i] for i in indices], mark)
        sizes = tuple(self.finals[i].shape[0] // 128 * 128 for i in indices)
        return choose(self.flag, [self.finals[i] for i in indices], theirs, sizes, **place)

    def decode(self, mark):
        self.third[0] = after(self.third[0], mark)
        return decode(self.flag, self.finals[0], self.third[0])


def rotation_tables(positions):
    half = ROT // 2
    frequency = jnp.exp(
        -jnp.log(10000.0) * jnp.arange(half, dtype=jnp.int32).astype(f32) * 2.0 / ROT
    )
    angle = frequency[:, None] * positions.astype(f32)[None, :]
    lane = lax.broadcasted_iota(jnp.int32, (half, PAIR), 1) % HD
    pick = lax.broadcasted_iota(jnp.int32, (half, PAIR), 0) == lane % half
    pick = (pick & (lane < ROT)).astype(f32)
    spread = lambda v: lax.dot_general(
        v, pick, TN, precision=lax.Precision.HIGHEST, preferred_element_type=f32
    )
    plain = (jnp.arange(PAIR, dtype=jnp.int32) % HD >= ROT).astype(f32)
    return spread(jnp.cos(angle)) + plain, spread(jnp.sin(angle))


def body(
    contexts,
    tokens,
    cotangent,
    segments,
    positions,
    parents,
    block_lists,
    project_weight,
    project_bias,
    dense_weight,
    dense_bias,
    up_weight,
    up_bias,
    down_weight,
    down_bias,
    first_gain,
    first_shift,
    second_gain,
    second_shift,
):
    rows, width = tokens.shape
    blocks = rows // BLK
    me = lax.axis_index("fsdp")
    split = contexts == 2
    slots = contexts * blocks
    first_slot = lax.axis_index("context") * blocks
    step = jnp.arange(10, dtype=jnp.int32)
    flip = jnp.where(step < 4, step, jnp.where(step < 6, 2 * step - 7, 2 * step - 12))
    ids = jnp.where(step < 8, me ^ flip, jnp.where(step == 8 if split else step < 8, 0, first_slot))
    if not split:
        ids = jnp.where(step == 9, 0, ids)
    ids = ids.astype(jnp.int32)

    blocks_of = lambda w: w.reshape(SHARD, -1, SHARD).transpose(1, 0, 2)
    units = up_bias.shape[0]
    near = lambda v: swap(v, "fsdp", 4, 1)
    far = lambda v: swap(v, "fsdp", 4, 2)
    wp = blocks_of(project_weight).reshape(-1, SHARD)
    up = blocks_of(up_weight).reshape(-1, SHARD)
    wp_far, up_far = far(wp), far(up)
    tables = rotation_tables(positions)
    normed_one = norm(tokens, first_gain[None], first_shift[None])
    wp_far = after(wp_far, tables, ids, normed_one, up)
    projects = (wp, near(wp), wp_far, near(wp_far))
    q0, q1, kv0, kv1 = project(ids, normed_one, projects, project_bias, tables)
    down = jnp.concatenate(after([down_weight, dense_weight], kv1), axis=0)
    down_far = far(down)
    if split:
        other0, other1 = swap(kv0, "context", 2, 1), swap(kv1, "context", 2, 1)
        keys = ((kv0, other0), (kv1, other1))
        state0 = attend_forward(ids, block_lists, slots, after(q0, kv1), kv0, 0, None, False)
        state1 = attend_forward(ids, block_lists, slots, after(q1, state0), kv1, 0, None, False)
        up_far = after(up_far, state1)
        ups = (up, near(up), up_far, near(up_far))
        o0, lse0 = attend_forward(
            ids, block_lists, slots, after(q0, up_far), other0, blocks, state0, True
        )
        normed_two, activated, slope = mlp_up(
            ids, after(tokens, o0), second_gain[None], second_shift[None], up_bias[None], ups
        )
        o1, lse1 = attend_forward(
            ids, block_lists, slots, after(q1, activated), other1, blocks, state1, True, 10
        )
        down_far = after(down_far, activated)
    else:
        keys = [(lax.all_gather(kv, "context", axis=0, tiled=True),) for kv in (kv0, kv1)]
        o0, lse0 = attend_forward(ids, block_lists, slots, q0, keys[0][0], 0, None, True)
        o1, lse1 = attend_forward(ids, block_lists, slots, q1, keys[1][0], 0, None, True)
        ups = (up, near(up), up_far, near(up_far))
        normed_two, activated, slope = mlp_up(
            ids, tokens, second_gain[None], second_shift[None], up_bias[None], ups
        )
    downs = (down, near(down), down_far, near(down_far))
    made = mlp_down(ids, activated, cotangent, downs, o0, o1)
    context_low, g0, g1 = made[2:]
    half = rows // 2

    out = LineSum(
        made[:2],
        [
            partial(
                finish, finish_out_kernel, "finish_out", start, half, 1,
                (tokens, dense_bias[None], down_bias[None]),
            )
            for start in (0, half)
        ],
    )
    back0 = attend_backward(ids, block_lists, q0, g0, o0, lse0, tables, keys[0])
    back1 = attend_backward(ids, block_lists, q1, after(g1, back0), o1, lse1, tables, keys[1])
    if split:
        grads = []
        for own, other, _ in (back0, back1):
            grads += [own, swap(other, "context", 2, 1)]
    else:
        grads = [
            lax.psum_scatter(whole_grad, "context", scatter_dimension=0, tiled=True)
            for whole_grad, _ in (back0, back1)
        ]
    mark = out.add(0, (back1, grads[1]) if split else back1)
    hidden_grad, e2, sums = mlp_backward(
        ids, tokens, after(cotangent, mark),
        second_gain[None], slope, ups + downs,
    )
    made = input_grad(
        ids, tokens, e2, first_gain[None], sums, (back0[-1], back1[-1]),
        tables, projects, grads, split,
    )
    projected_grad, sums = made[2:]
    line = LineSum(
        made[:2],
        [
            partial(
                finish, partial(finish_in_kernel, half), "finish_in", start, half, 2,
                (tokens, cotangent),
            )
            for start in (0, half)
        ],
    )
    mark = out.add(1, made[0])
    mark = out.end(0, mark)
    mlp_keep, *mlp_send = weight_parts(
        mlp_weights_kernel, "mlp_weights", ids, 2 * units,
        activated, cotangent, normed_two, after(hidden_grad, mark),
    )
    mark = mlp_keep
    mlp_got = swap(mlp_send, "fsdp", 4, 1)
    mark = line.add(0, mark)
    mark = out.end(1, mark)
    mark = out.arrive(0, mark)
    mlp_here, mlp_there = halves(mlp_keep, after(mlp_got, mark), micros=0)
    mlp_got = swap(mlp_there, "fsdp", 4, 2)
    mark = mlp_here
    rest_keep, *rest_send = weight_parts(
        rest_weights_kernel, "rest_weights", ids, 4 * SHARD,
        context_low, cotangent, normed_one, after(projected_grad, mark),
    )
    rest_got = swap(rest_send, "fsdp", 4, 1)
    mark = rest_keep
    mark = line.add(1, mark)
    mark = line.end(0, mark)
    mark = out.arrive(1, mark)
    mlp_part = add(mlp_here, after(mlp_got, mark))
    if split:
        mlp_got = swap(mlp_part, "context", 2, 1)
    rest_here, rest_there = halves(rest_keep, after(rest_got, mlp_part))
    rest_got = swap(rest_there, "fsdp", 4, 2)
    mark = line.end(1, rest_here)
    rest_part = add(rest_here, after(rest_got, mark))
    if split:
        rest_got = swap(rest_part, "context", 2, 1)
    mark = rest_part
    norms = line.decode(mark)
    sums = jnp.concatenate([norms[0:2], sums[2:4], norms[2:4], sums[6:8]], axis=0)
    mark = sums
    for step in [("fsdp", 4, 1), ("fsdp", 4, 2)]:
        sums = mark = add(sums, swap(after(sums, mark), *step), f32)
    hop = swap(sums, "context", contexts, 1)
    layer_out = mark = out.result([0, 1], mark)
    tokens_grad = mark = line.result([0], mark, total=rows)
    if split:
        down_grad, up_grad = call(
            mlp_last_kernel, "mlp_last", (mlp_part, after(mlp_got, mark)),
            [((units, SHARD), f32), ((SHARD, units), f32)],
        )
        dense_grad, project_grad = call(
            rest_last_kernel, "rest_last", (rest_part, after(rest_got, down_grad)),
            [((SHARD, SHARD), f32), ((3, SHARD, SHARD), f32)],
        )
        mark = dense_grad
        project_grad = project_grad.transpose(1, 0, 2)
    else:
        mlp_part, rest_part = lax.psum(
            (mlp_part.astype(f32), rest_part.astype(f32)), "context"
        )
        back_blocks = lambda g: g.reshape(-1, SHARD, SHARD).transpose(1, 0, 2)
        down_grad = mlp_part[:units]
        up_grad = back_blocks(mlp_part[units:]).reshape(SHARD, units)
        dense_grad = rest_part[:SHARD]
        project_grad = back_blocks(rest_part[SHARD:])
    sums = mark = add(sums, after(hop, mark), f32)
    for i in range(1, contexts.bit_length() - 1):
        sums = mark = add(sums, swap(after(sums, mark), "context", contexts, 1 << i), f32)
    tokens_grad = line.result([1], mark, start=half, total=rows, before=tokens_grad)
    norms = sums
    up_total, bias_sum = sums[2], sums[3]
    project_total = sums[6, : project_bias.size]
    return (
        layer_out,
        tokens_grad,
        project_grad,
        project_total.reshape(3, -1),
        dense_grad,
        bias_sum,
        up_grad,
        up_total,
        down_grad,
        bias_sum,
        norms[4],
        norms[5],
        norms[0],
        norms[1],
    )


def solution(mesh):
    tokens = P(("fsdp", "context"), None)
    line = P(("fsdp", "context"))
    in_specs = (
        tokens, tokens, line, line, P("fsdp", None), tokens,
        P("fsdp", None, "tensor"), P(None, "tensor"), P("tensor", "fsdp"), P(),
        P("fsdp", "tensor"), P("tensor"), P("tensor", "fsdp"), P(), P(), P(), P(), P(),
    )
    out_specs = (
        tokens, tokens, P("fsdp", None, "tensor"), P(None, "tensor"), P("tensor", "fsdp"), P(),
        P("fsdp", "tensor"), P("tensor"), P("tensor", "fsdp"), P(), P(), P(), P(), P(),
    )
    run = partial(body, mesh.shape["context"])
    return jax.shard_map(run, mesh=mesh, in_specs=in_specs, out_specs=out_specs, check_vma=False)
```

```python
from functools import partial

import jax
import jax.numpy as jnp
from jax import lax
from jax.experimental import pallas as pl
from jax.experimental.pallas import tpu as pltpu
from jax.sharding import PartitionSpec as P

HD = 64
ROT = 16
BLK = 512
HALF = 256
PAIR = 2 * HD
SHARD = 256
EXTRA = 16

epsilon = 1e-05
masked = -1e30
bf16 = jnp.bfloat16
f32 = jnp.float32
scale2 = HD ** (-0.5) * 1.4426950408889634
NT = (((1,), (1,)), ((), ()))
NN = (((1,), (0,)), ((), ()))
TN = (((0,), (0,)), ((), ()))


def dot(a, b, dims):
    return lax.dot_general(a, b, dims, preferred_element_type=f32)


def params(mib):
    return pltpu.CompilerParams(vmem_limit_bytes=mib * 1024 * 1024)


def cost(micros):
    return pl.CostEstimate(
        flops=int(1.15e9 * micros), bytes_accessed=int(3.7e6 * micros), transcendentals=0
    )


def whole(shape):
    return pl.BlockSpec(shape, lambda *_: (0,) * len(shape))


smem = pl.BlockSpec(memory_space=pltpu.SMEM)


def norm_rows(x):
    mean = jnp.mean(x, axis=-1, keepdims=True)
    centered = x - mean
    variance = jnp.mean(centered * centered, axis=-1, keepdims=True)
    factor = lax.rsqrt(variance + epsilon)
    return centered * factor, factor


def rotate_lanes(x, cos, sin, sign):
    lane = lax.broadcasted_iota(jnp.int32, x.shape, 1) % HD
    left = pltpu.roll(x, PAIR - ROT // 2, 1)
    right = pltpu.roll(x, ROT // 2, 1)
    return x * cos + jnp.where(lane < ROT // 2, -sign * left, sign * right) * sin


def columns(index, width):
    return pl.ds(pl.multiple_of(index * width, width), width)


def norm_kernel(x, gain, shift, out):
    normal, _ = norm_rows(x[...].astype(f32))
    out[...] = (normal * gain[...] + shift[...]).astype(bf16)


def norm(x, gain, shift, tile=256):
    row = pl.BlockSpec((tile, x.shape[1]), lambda i: (i, 0))
    return call(
        norm_kernel, "norm", (x, gain, shift), (x.shape, bf16), x.shape[0] // tile,
        [row, whole(gain.shape), whole(shift.shape)], [row],
    )


def project_kernel(ids, n1, w0, w1, w2, w3, bias, cos, sin, q0, q1, kv0, kv1, weight):
    depth, width = w0.shape[0] // 3, w0.shape[1]

    @pl.when(pl.program_id(0) == 0)
    def _():
        for i, piece in enumerate((w0, w1, w2, w3)):
            for part in range(3):
                weight[part, columns(ids[i], depth), :] = piece[
                    part * depth : (part + 1) * depth, :
                ]

    for part in range(3):
        total = dot(n1[...], weight[part], NN) + bias[part : part + 1, :]
        for pair, (q, kv) in enumerate(((q0, kv0), (q1, kv1))):
            half = total[:, pair * PAIR : (pair + 1) * PAIR]
            if part < 2:
                half = rotate_lanes(half, cos[...], sin[...], 1.0)
            if part == 0:
                q[...] = half.astype(bf16)
            else:
                kv[:, (part - 1) * PAIR : part * PAIR] = half.astype(bf16)


def project(ids, n1, weights, bias, tables, tile=512):
    rows, wide = n1.shape
    row = lambda w: pl.BlockSpec((tile, w), lambda i: (i, 0))
    s = jax.ShapeDtypeStruct
    return pl.pallas_call(
        project_kernel,
        grid=(rows // tile,),
        in_specs=[smem, row(wide)]
        + [whole(v.shape) for v in (*weights, bias)]
        + [row(PAIR)] * 2,
        out_specs=[row(PAIR)] * 2 + [row(2 * PAIR)] * 2,
        out_shape=[s((rows, PAIR), bf16)] * 2 + [s((rows, 2 * PAIR), bf16)] * 2,
        scratch_shapes=[pltpu.VMEM((3, wide, weights[0].shape[1]), bf16)],
        compiler_params=params(16),
        cost_estimate=cost(4.3),
        name="project",
    )(ids, n1, *weights, bias, *tables)


def head_lanes(shape, head):
    return lax.broadcasted_iota(jnp.int32, shape, 1) // HD == head


def sublanes(index, size):
    return pl.ds(pl.multiple_of(index * size, size), size)


def triangle(rows, cols):
    return lax.broadcasted_iota(jnp.int32, (rows, cols), 0) <= lax.broadcasted_iota(
        jnp.int32, (rows, cols), 1
    )


def slot_of(ids, lists, slots, block, step):
    entry = lists[block, step]
    return jnp.where(entry < 0, entry, lax.rem(entry - ids[9] + slots, slots))


def head_of(ref, block, head):
    value = ref[sublanes(block, BLK), :]
    return jnp.where(head_lanes(value.shape, head), value, jnp.zeros_like(value))


def attend_forward_kernel(slots, low, count, first, last, ids, lists, q, kv, *refs):
    if not first:
        ins, refs = refs[:2], refs[2:]
    outs, (turned, state, acc) = refs[:2], refs[2:]
    blocks = q.shape[0] // BLK

    def turn(slot, unused):
        turned[slot] = kv[sublanes(slot, BLK), PAIR:].T
        return unused

    lax.fori_loop(0, count, turn, 0)
    if not first:
        state[...] = ins[0][...]
        acc[...] = ins[1][...]

    def one(line, unused):
        block, head = lax.div(line, 2), lax.rem(line, 2)
        own = ids[8] + block
        rows, part = sublanes(line, HD), sublanes(head, HD)
        tops, sums = pl.ds(line, 1), pl.ds(8 + line, 1)
        query = head_of(q, block, head)

        if first:
            upper, lower = sublanes(2 * (own - low), HALF), sublanes(2 * (own - low) + 1, HALF)
            scores = dot(kv[upper, :PAIR], query, NT) * scale2
            scores = jnp.where(triangle(HALF, BLK), scores, masked)
            late = dot(kv[lower, :PAIR], query[HALF:, :], NT) * scale2
            late = jnp.where(triangle(HALF, HALF), late, masked)
            state[tops, :] = jnp.max(scores, axis=0, keepdims=True)
            state[tops, HALF:] = jnp.maximum(
                state[tops, HALF:], jnp.max(late, axis=0, keepdims=True)
            )
            weight = jnp.exp2(scores - state[tops, :])
            late = jnp.exp2(late - state[tops, HALF:])
            state[sums, :] = jnp.sum(weight, axis=0, keepdims=True)
            state[sums, HALF:] += jnp.sum(late, axis=0, keepdims=True)
            acc[rows, :] = dot(turned[own - low, part, :HALF], weight.astype(bf16), NN)
            acc[rows, HALF:] += dot(turned[own - low, part, HALF:], late.astype(bf16), NN)

        def entry(step, unused):
            slot = slot_of(ids, lists, slots, block, step)

            @pl.when((slot >= low) & (slot < low + count) & (slot != own))
            def _():
                scores = dot(kv[sublanes(slot - low, BLK), :PAIR], query, NT) * scale2
                old = state[tops, :]
                top = jnp.maximum(old, jnp.max(scores, axis=0, keepdims=True))
                weight = jnp.exp2(scores - top)
                shrink = jnp.exp2(old - top)
                state[tops, :] = top
                state[sums, :] = state[sums, :] * shrink + jnp.sum(weight, axis=0, keepdims=True)
                acc[rows, :] = acc[rows, :] * shrink + dot(
                    turned[slot - low, part, :], weight.astype(bf16), NN
                )

            return unused

        lax.fori_loop(0, lists.shape[1], entry, 0)
        if last:
            outs[1][pl.ds(line, 1), :] = state[tops, :] + jnp.log2(state[sums, :])
            acc[rows, :] = acc[rows, :] * (1.0 / state[sums, :])
        return unused

    lax.fori_loop(0, 2 * blocks, one, 0)
    if last:

        def give(block, unused):
            outs[0][sublanes(block, BLK), :] = acc[sublanes(block, PAIR), :].T
            return unused

        lax.fori_loop(0, blocks, give, 0)
    else:
        outs[0][...] = state[...]
        outs[1][...] = acc[...]


def attend_forward(ids, lists, slots, q, kv, low, carried, last, micros=0):
    count = kv.shape[0] // BLK
    rows = q.shape[0]
    tall = rows // BLK * PAIR
    vmem = pl.BlockSpec(memory_space=pltpu.VMEM)
    s = jax.ShapeDtypeStruct
    shapes = [s((rows, PAIR), f32), s((8, BLK), f32)] if last else [
        s((16, BLK), f32), s((tall, BLK), f32)
    ]
    return pl.pallas_call(
        partial(attend_forward_kernel, slots, low, count, carried is None, last),
        in_specs=[smem, smem] + [vmem] * (2 + len(carried or ())),
        out_specs=[vmem] * 2,
        out_shape=shapes,
        scratch_shapes=[
            pltpu.VMEM((count, PAIR, BLK), bf16),
            pltpu.VMEM((16, BLK), f32),
            pltpu.VMEM((tall, BLK), f32),
        ],
        compiler_params=params(8 + 2 * count),
        cost_estimate=cost(micros),
        name="attend_forward",
    )(ids, lists, q, kv, *(carried or ()))


def attend_backward_kernel(slots, split, ids, lists, q, g, o, lse, cos, sin, *refs):
    outs = 2 if split else 1
    parts = refs[: -6 - outs]
    grads = refs[-6 - outs : -6]
    qg, kv, turned, acc, total, deltas = refs[-6:]
    blocks = q.shape[0] // BLK
    start = 0
    for part in parts:
        kv[start : start + part.shape[0], :] = part[...]
        start += part.shape[0]

    def prepare(slot, unused):
        turned[slot] = kv[sublanes(slot, BLK), :PAIR].T
        total[sublanes(slot, BLK), :] = jnp.zeros((BLK, 2 * PAIR), f32)
        return unused

    lax.fori_loop(0, slots, prepare, 0)
    pick = (
        lax.broadcasted_iota(jnp.int32, (8, PAIR), 1) // HD
        == lax.broadcasted_iota(jnp.int32, (8, PAIR), 0)
    ).astype(f32)

    def delta_of(block, unused):
        span = sublanes(block, BLK)
        deltas[sublanes(block, 8), :] = lax.dot_general(
            pick,
            o[span, :] * g[span, :].astype(f32),
            NT,
            preferred_element_type=f32,
            precision=lax.Precision.HIGHEST,
        )
        return unused

    lax.fori_loop(0, blocks, delta_of, 0)

    def one(line, unused):
        block, head = lax.div(line, 2), lax.rem(line, 2)
        own = ids[8] + block
        rows, part = sublanes(line, HD), sublanes(head, HD)
        query, grad = head_of(q, block, head), head_of(g, block, head)
        log_sum = lse[pl.ds(line, 1), :]
        delta = deltas[pl.ds(block * 8 + head, 1), :]

        def tile(here, keys, skip=0, keep=None):
            scores = dot(kv[here, :PAIR], query[skip:, :], NT) * scale2
            prob = jnp.exp2(scores - log_sum[:, skip:])
            if keep is not None:
                prob = jnp.where(keep, prob, 0.0)
            prob_grad = dot(kv[here, PAIR:], grad[skip:, :], NT)
            score_grad = (prob * (prob_grad - delta[:, skip:])).astype(bf16)
            total[here, PAIR:] += dot(prob.astype(bf16), grad[skip:, :], NN)
            total[here, :PAIR] += dot(score_grad, query[skip:, :], NN)
            return dot(keys, score_grad, NN)

        acc[rows, :] = tile(
            sublanes(2 * own, HALF), turned[own, part, :HALF], 0, triangle(HALF, BLK)
        )
        acc[rows, HALF:] += tile(
            sublanes(2 * own + 1, HALF), turned[own, part, HALF:], HALF, triangle(HALF, HALF)
        )

        def entry(step, unused):
            slot = slot_of(ids, lists, slots, block, step)

            @pl.when((slot >= 0) & (slot != own))
            def _():
                acc[rows, :] += tile(sublanes(slot, BLK), turned[slot, part, :])

            return unused

        lax.fori_loop(0, lists.shape[1], entry, 0)
        return unused

    lax.fori_loop(0, 2 * blocks, one, 0)

    def give(block, unused):
        span = sublanes(block, BLK)
        grad_q = acc[sublanes(block, PAIR), :].T * (HD ** (-0.5))
        qg[span, :] = rotate_lanes(grad_q, cos[span, :], sin[span, :], -1.0).astype(bf16)
        return unused

    lax.fori_loop(0, blocks, give, 0)
    start = 0
    for out in grads:
        out[...] = total[start : start + out.shape[0], :].astype(out.dtype)
        start += out.shape[0]


def attend_backward(ids, lists, q, g, o, lse, tables, kvs):
    slots = sum(part.shape[0] for part in kvs) // BLK
    rows = q.shape[0]
    split = len(kvs) == 2
    shapes = [jax.ShapeDtypeStruct(kvs[0].shape, bf16)]
    if split:
        shapes.append(jax.ShapeDtypeStruct(kvs[1].shape, bf16))
    shapes.append(jax.ShapeDtypeStruct((rows, PAIR), bf16))
    vmem = pl.BlockSpec(memory_space=pltpu.VMEM)
    return pl.pallas_call(
        partial(attend_backward_kernel, slots, split),
        grid=(),
        in_specs=[smem, smem] + [vmem] * (6 + len(kvs)),
        out_specs=[vmem] * len(shapes),
        out_shape=shapes,
        scratch_shapes=[
            pltpu.VMEM((slots * BLK, 2 * PAIR), bf16),
            pltpu.VMEM((slots, PAIR, BLK), bf16),
            pltpu.VMEM((rows // BLK * PAIR, BLK), f32),
            pltpu.VMEM((slots * BLK, 2 * PAIR), f32),
            pltpu.VMEM((rows // BLK * 8, BLK), f32),
        ],
        compiler_params=params(14 + slots),
        cost_estimate=cost(0),
        name="attend_backward",
    )(ids, lists, q, g, o, lse, *tables, *kvs)


def unpack_up(ids, pieces, up):
    for i, piece in enumerate(pieces):
        for n in range(up.shape[1] // SHARD):
            up[columns(ids[i], SHARD), n * SHARD : (n + 1) * SHARD] = piece[
                n * SHARD : (n + 1) * SHARD, :
            ]


def unpack_down(ids, pieces, down, dense):
    units = down.shape[0]
    for i, piece in enumerate(pieces):
        where = columns(ids[i], SHARD)
        down[:, where] = piece[:units, :]
        if dense is not None:
            dense[:, where] = piece[units:, :]


def mlp_up_kernel(ids, x, gain, shift, up_bias, p0, p1, p2, p3, n2, act, slope, up):
    @pl.when(pl.program_id(0) == 0)
    def _():
        unpack_up(ids, (p0, p1, p2, p3), up)

    normal, _ = norm_rows(x[...].astype(f32))
    normed = (normal * gain[...] + shift[...]).astype(bf16)
    n2[...] = normed
    hidden = dot(normed, up[...], NN) + up_bias[...]
    cdf = 0.5 + 0.5 * lax.erf(hidden * (2.0 ** -0.5))
    pdf = jnp.exp(hidden * hidden * -0.5) * 0.3989422804014327
    act[...] = (hidden * cdf).astype(bf16)
    slope[...] = (cdf + hidden * pdf).astype(bf16)


def mlp_up(ids, x, gain, shift, up_bias, pieces, tile=512):
    rows, width = x.shape
    units = up_bias.shape[1]
    row = lambda w: pl.BlockSpec((tile, w), lambda i: (i, 0))
    s = jax.ShapeDtypeStruct
    return pl.pallas_call(
        mlp_up_kernel,
        grid=(rows // tile,),
        in_specs=[smem, row(width)] + [whole(a.shape) for a in (gain, shift, up_bias, *pieces)],
        out_specs=[row(width), row(units), row(units)],
        out_shape=[s((rows, width), bf16), s((rows, units), bf16), s((rows, units), bf16)],
        scratch_shapes=[pltpu.VMEM((width, units), bf16)],
        compiler_params=params(24),
        cost_estimate=cost(0),
        name="mlp_up",
    )(ids, x, gain, shift, up_bias, *pieces)


def store_part(outs, sizes, value):
    tile = value.shape[0]
    step = pl.program_id(0)
    start = 0
    for out, size in zip(outs, sizes):
        count = size // tile

        @pl.when((step >= start) & (step < start + count))
        def _():
            out[pl.ds(pl.multiple_of((step - start) * tile, tile), tile), :] = value

        start += count


def mlp_down_kernel(
    rows, ids, act, cot, p0, p1, p2, p3, o0, o1, first, second, ctx, g0, g1, down, dense
):
    @pl.when(pl.program_id(0) == 0)
    def _():
        unpack_down(ids, (p0, p1, p2, p3), down, dense)

    context_grad = dot(cot[...], dense[...], NT)
    g0[...] = context_grad[:, :PAIR].astype(bf16)
    g1[...] = context_grad[:, PAIR:].astype(bf16)
    ctx[:, :PAIR] = o0[...].astype(bf16)
    ctx[:, PAIR:] = o1[...].astype(bf16)
    value = dot(ctx[...], dense[...], NN) + dot(act[...], down[...], NN)
    store_part((first, second), (rows // 2, rows // 2), value.astype(bf16))


def mlp_down(ids, act, cot, pieces, o0, o1, tile=512):
    rows, width = cot.shape
    units = act.shape[1]
    row = lambda w: pl.BlockSpec((tile, w), lambda i: (i, 0))
    s = jax.ShapeDtypeStruct
    return pl.pallas_call(
        partial(mlp_down_kernel, rows),
        grid=(rows // tile,),
        in_specs=[smem, row(units), row(width)]
        + [whole(a.shape) for a in pieces]
        + [row(PAIR), row(PAIR)],
        out_specs=[whole((rows // 2, width))] * 2 + [row(2 * PAIR), row(PAIR), row(PAIR)],
        out_shape=[s((rows // 2, width), bf16)] * 2
        + [s((rows, 2 * PAIR), bf16), s((rows, PAIR), bf16), s((rows, PAIR), bf16)],
        scratch_shapes=[
            pltpu.VMEM((units, width), bf16),
            pltpu.VMEM((2 * PAIR, width), bf16),
        ],
        compiler_params=params(26),
        cost_estimate=cost(1),
        name="mlp_down",
    )(ids, act, cot, *pieces, o0, o1)


def mlp_backward_kernel(
    ids, x, cot, gain, slope, u0, u1, u2, u3, d0, d1, d2, d3, hid, e2, sums, up, down
):
    @pl.when(pl.program_id(0) == 0)
    def _():
        sums[...] = jnp.zeros_like(sums)
        unpack_up(ids, (u0, u1, u2, u3), up)
        unpack_down(ids, (d0, d1, d2, d3), down, None)

    low = (dot(cot[...], down[...], NT) * slope[...].astype(f32)).astype(bf16)
    hid[...] = low
    grad = dot(low, up[...], NT)
    normal, _ = norm_rows(x[...].astype(f32))
    sums[0:1, :] += jnp.sum(grad * normal, axis=0, keepdims=True)
    sums[1:2, :] += jnp.sum(grad, axis=0, keepdims=True)
    sums[2:3, :] += jnp.sum(low.astype(f32), axis=0, keepdims=True)
    sums[3:4, :] += jnp.sum(cot[...].astype(f32), axis=0, keepdims=True)
    e2[...] = (grad * gain[...]).astype(bf16)


def mlp_backward(ids, x, cot, gain, slope, pieces, tile=256):
    rows, width = x.shape
    units = slope.shape[1]
    row = lambda w: pl.BlockSpec((tile, w), lambda i: (i, 0))
    s = jax.ShapeDtypeStruct
    return pl.pallas_call(
        mlp_backward_kernel,
        grid=(rows // tile,),
        in_specs=[smem, row(width), row(width), whole(gain.shape), row(units)]
        + [whole(a.shape) for a in pieces],
        out_specs=[row(units), row(width), whole((8, width))],
        out_shape=[s((rows, units), bf16), s((rows, width), bf16), s((8, width), f32)],
        scratch_shapes=[
            pltpu.VMEM((width, units), bf16),
            pltpu.VMEM((units, width), bf16),
        ],
        compiler_params=params(26),
        cost_estimate=cost(1),
        name="mlp_backward",
    )(ids, x, cot, gain, slope, *pieces)


def mlp_weights_kernel(ids, act, cot, n2, hid, keep, near, far):
    units = act.shape[1]
    step = pl.program_id(0)
    index = ids[4 + step]
    for out, when in ((near, step == 0), (far, step == 1), (keep, step >= 2)):

        @pl.when(when)
        def _():
            out[0, :units, :] = dot(act[...], cot[:, columns(index, SHARD)], TN).astype(bf16)
            lhs = n2[:, columns(index, SHARD)]
            for n in range(units // SHARD):
                at = slice(n * SHARD, (n + 1) * SHARD)
                out[0, units + n * SHARD : units + (n + 1) * SHARD, :] = dot(
                    lhs, hid[:, at], TN
                ).astype(bf16)


def rest_weights_kernel(ids, ctx, cot, n1, pg, keep, near, far):
    width = ctx.shape[1]
    step = pl.program_id(0)
    index = ids[4 + step]
    for out, when in ((near, step == 0), (far, step == 1), (keep, step >= 2)):

        @pl.when(when)
        def _():
            out[0, :width, :] = dot(ctx[...], cot[:, columns(index, SHARD)], TN).astype(bf16)
            lhs = n1[:, columns(index, SHARD)]
            for n in range(3):
                at = slice(n * SHARD, (n + 1) * SHARD)
                out[0, width + n * SHARD : width + (n + 1) * SHARD, :] = dot(
                    lhs, pg[:, at], TN
                ).astype(bf16)


def weight_parts(kernel, name, ids, tall, *args):
    s = lambda n: jax.ShapeDtypeStruct((n, tall, SHARD), bf16)
    return pl.pallas_call(
        kernel,
        grid=(4,),
        in_specs=[smem] + [whole(a.shape) for a in args],
        out_specs=[
            pl.BlockSpec((1, tall, SHARD), lambda i: (jnp.maximum(i - 2, 0), 0, 0)),
            whole((1, tall, SHARD)),
            whole((1, tall, SHARD)),
        ],
        out_shape=[s(2), s(1), s(1)],
        compiler_params=params(20),
        cost_estimate=cost(0),
        name=name,
    )(ids, *args)


def input_grad_kernel(
    split, sizes, ids, x, e2, gain, sums_two, qg0, qg1, cos, sin, *refs
):
    count = 4 if split else 2
    weights, refs = refs[:4], refs[4:]
    grads, es, (pg, sums, first) = refs[:count], refs[count:-3], refs[-3:]
    depth, width = weights[0].shape[0] // 3, 2 * PAIR

    @pl.when(pl.program_id(0) == 0)
    def _():
        sums[...] = sums_two[...]

    pg[:, 0:PAIR] = qg0[...]
    pg[:, PAIR : 2 * PAIR] = qg1[...]
    for pair in range(2):
        if split:
            own, other = grads[2 * pair : 2 * pair + 2]
            grad = own[...].astype(f32) + other[...].astype(f32)
        else:
            grad = grads[pair][...].astype(f32)
        key = rotate_lanes(
            grad[:, :PAIR] * (HD ** (-0.5)), cos[...], sin[...], -1.0
        )
        at = width + pair * PAIR
        pg[:, at : at + PAIR] = key.astype(bf16)
        pg[:, at + width : at + width + PAIR] = grad[:, PAIR:].astype(bf16)
    sums[6:7, : 3 * width] += jnp.sum(pg[...].astype(f32), axis=0, keepdims=True)
    normal, _ = norm_rows(x[...].astype(f32))
    for piece in range(4):
        where = columns(ids[piece], depth)
        total = dot(pg[:, :width], weights[piece][:depth, :], NT)
        total += dot(pg[:, width : 2 * width], weights[piece][depth : 2 * depth, :], NT)
        total += dot(pg[:, 2 * width :], weights[piece][2 * depth :, :], NT)
        first[:, where] = total
    grad = first[...]
    store_part(es, sizes, (grad * gain[...] + e2[...].astype(f32)).astype(bf16))
    sums[4:5, :] += jnp.sum(grad * normal, axis=0, keepdims=True)
    sums[5:6, :] += jnp.sum(grad, axis=0, keepdims=True)

    @pl.when(pl.program_id(0) == pl.num_programs(0) - 1)
    def _():
        terms = split_terms(jnp.concatenate([sums[0:2, :], sums[4:6, :]], axis=0))
        es[0][sizes[0] :, :] = terms


def input_grad(ids, x, e2, gain, sums, qgs, tables, weights, grads, split, tile=256):
    rows, width = x.shape
    row = lambda w: pl.BlockSpec((tile, w), lambda i: (i, 0))
    s = jax.ShapeDtypeStruct
    units = 6 * PAIR
    sizes = (rows // 2,) * 2
    parts = [(sizes[0] + EXTRA, width), *[(size, width) for size in sizes[1:]]]
    return pl.pallas_call(
        partial(input_grad_kernel, split, sizes),
        grid=(rows // tile,),
        in_specs=[smem, row(width), row(width), whole(gain.shape), whole(sums.shape)]
        + [row(PAIR), row(PAIR)]
        + [row(PAIR)] * 2
        + [whole(w.shape) for w in weights]
        + [row(2 * PAIR)] * len(grads),
        out_specs=[whole(part) for part in parts] + [row(units), whole((8, width))],
        out_shape=[s(part, bf16) for part in parts]
        + [s((rows, units), bf16), s((8, width), f32)],
        scratch_shapes=[pltpu.VMEM((tile, width), f32)],
        compiler_params=params(24),
        cost_estimate=cost(4),
        name="input_grad",
    )(ids, x, e2, gain, sums, *qgs, *tables, *weights, *grads)


def call(kernel, name, args, shapes, grid=1, in_specs=None, out_specs=None, aliases=None, mib=16, micros=0):
    s = jax.ShapeDtypeStruct
    many = isinstance(shapes, list)
    shapes = [s(*shape) for shape in (shapes if many else [shapes])]
    out = pl.pallas_call(
        kernel,
        grid=(grid,),
        in_specs=in_specs or [whole(a.shape) for a in args],
        out_specs=out_specs or [whole(shape.shape) for shape in shapes],
        out_shape=shapes,
        input_output_aliases=aliases or {},
        compiler_params=params(mib),
        cost_estimate=cost(micros),
        name=name,
    )(*args)
    return out if many else out[0]


def add_kernel(a, b, out):
    out[...] = (a[...].astype(f32) + b[...].astype(f32)).astype(out.dtype)


def add(a, b, dtype=bf16, grid=2):
    grid = grid if a.shape[0] > 8 else 1
    row = pl.BlockSpec((a.shape[0] // grid, a.shape[1]), lambda i: (i, 0))
    return call(add_kernel, "add", (a, b), (a.shape, dtype), grid, [row, row], [row])


def split_terms(value):
    high = value.astype(bf16)
    rest = value - high.astype(f32)
    middle = rest.astype(bf16)
    low = (rest - middle.astype(f32)).astype(bf16)
    return jnp.concatenate([high, middle, low, jnp.zeros_like(low)], axis=0)


def join_terms(terms):
    terms = terms.astype(f32)
    return terms[0:4] + terms[4:8] + terms[8:12]


def add_extra_kernel(a, b, out):
    rows = a.shape[0] - EXTRA
    out[:rows, :] = (a[:rows, :].astype(f32) + b[:rows, :].astype(f32)).astype(out.dtype)
    out[rows:, :] = split_terms(join_terms(a[rows:, :]) + join_terms(b[rows:, :]))


def add_extra(a, b):
    return call(add_extra_kernel, "add_extra", (a, b), (a.shape, a.dtype))


def finish_out_kernel(a, b, x, dense_bias, down_bias, out):
    total = a[...].astype(f32) + b[...].astype(f32)
    out[...] = (x[...].astype(f32) + total + (dense_bias[...] + down_bias[...])).astype(bf16)


def finish_in_kernel(rows, a, b, x, upstream, out):
    def one(step, unused):
        here = sublanes(step, 128)
        total = a[here, :].astype(f32) + b[here, :].astype(f32)
        normal, factor = norm_rows(x[here, :].astype(f32))
        mean_e = jnp.mean(total, axis=-1, keepdims=True)
        mean_en = jnp.mean(total * normal, axis=-1, keepdims=True)
        result = upstream[here, :].astype(f32) + factor * (total - mean_e - normal * mean_en)
        out[here, :] = result.astype(bf16)
        return unused

    lax.fori_loop(0, rows // 128, one, 0)
    if a.shape[0] > rows:
        out[rows:, :] = split_terms(join_terms(a[rows:, :]) + join_terms(b[rows:, :]))


def finish(kernel, name, start, rows, of_rows, arrays, a, b):
    block = pl.BlockSpec((rows, a.shape[1]), lambda i: (start // rows, 0))
    specs = [whole(a.shape)] * 2 + [
        block if i < of_rows else whole(v.shape) for i, v in enumerate(arrays)
    ]
    return call(kernel, name, (a, b, *arrays), (a.shape, bf16), 1, specs)


def choose_kernel(sizes, flag, *refs):
    out, count = refs[-1], len(sizes)
    for parts, when in ((refs[:count], flag[0] > 0), (refs[count : 2 * count], flag[0] <= 0)):

        @pl.when(when)
        def _():
            start = 0
            for part, size in zip(parts, sizes):
                out[start : start + size, :] = part[:size, :]
                start += size


def choose(flag, ours, theirs, sizes, start=0, total=None, before=None):
    rows, width = sum(sizes), ours[0].shape[1]
    args = (flag, *ours, *theirs)
    specs, aliases = [smem] + [whole(v.shape) for v in args[1:]], {}
    if before is not None:
        aliases = {len(args): 0}
        args, specs = args + (before,), specs + [pl.BlockSpec(memory_space=pl.ANY)]
    return call(
        partial(choose_kernel, sizes), "choose", args, ((total or rows, width), bf16), 1, specs,
        [pl.BlockSpec((rows, width), lambda i: (start // rows, 0))], aliases,
    )


def decode_kernel(flag, ours, theirs, out):
    out[0:4, :] = jnp.where(flag[0] > 0, join_terms(ours[...]), join_terms(theirs[...]))
    out[4:8, :] = jnp.zeros((4, out.shape[1]), f32)


def decode(flag, ours, theirs):
    at = ours.shape[0] // EXTRA - 1
    block = pl.BlockSpec((EXTRA, ours.shape[1]), lambda i: (at, 0))
    return call(
        decode_kernel, "decode", (flag, ours, theirs), ((8, ours.shape[1]), f32), 1,
        [smem, block, block],
    )


def halves_kernel(keep, near, far, here, there):
    here[...] = keep[0].astype(f32) + near[0].astype(f32)
    there[...] = (keep[1].astype(f32) + far[0].astype(f32)).astype(bf16)


def halves(keep, got, grid=2, micros=0):
    tall, width = keep.shape[1:]
    block = lambda n: pl.BlockSpec((n, tall // grid, width), lambda i: (0, i, 0))
    row = pl.BlockSpec((tall // grid, width), lambda i: (i, 0))
    return call(
        halves_kernel, "halves", (keep, *got), [((tall, width), f32), ((tall, width), bf16)],
        grid, [block(2), block(1), block(1)], [row, row], micros=micros,
    )


def mlp_last_kernel(a, b, down, up):
    units = down.shape[0]
    down[...] = a[:units, :].astype(f32) + b[:units, :].astype(f32)
    for n in range(units // SHARD):
        at = slice(units + n * SHARD, units + (n + 1) * SHARD)
        up[:, n * SHARD : (n + 1) * SHARD] = a[at, :].astype(f32) + b[at, :].astype(f32)


def rest_last_kernel(a, b, dense, project):
    dense[...] = a[:SHARD, :].astype(f32) + b[:SHARD, :].astype(f32)
    for n in range(3):
        at = slice((n + 1) * SHARD, (n + 2) * SHARD)
        project[n] = a[at, :].astype(f32) + b[at, :].astype(f32)


def swap(values, axis, size, bit):
    pairs = [(i, i ^ bit) for i in range(size)]
    return jax.tree.map(lambda v: lax.ppermute(v, axis, pairs), values)


def after(values, *others):
    return lax.optimization_barrier((values, others))[0]


class LineSum:
    def __init__(self, parts, finishes):
        place = lax.axis_index("tensor")
        self.flag = ((place == 1) | (place == 2)).astype(jnp.int32)[None]
        self.parts, self.finishes = parts, finishes
        self.first = [lax.ppermute(part, "tensor", [(0, 1), (3, 2)]) for part in parts]
        self.sums, self.second, self.finals, self.third = {}, {}, {}, {}

    def add(self, i, mark):
        part, got = self.parts[i], after(self.first[i], mark)
        self.sums[i] = add_extra(part, got) if part.shape[0] % 128 else add(part, got)
        self.second[i] = lax.ppermute(self.sums[i], "tensor", [(1, 2), (2, 1)])
        return self.sums[i]

    def end(self, i, mark):
        self.finals[i] = self.finishes[i](self.sums[i], after(self.second[i], mark))
        self.third[i] = lax.ppermute(self.finals[i], "tensor", [(1, 0), (2, 3)])
        return self.finals[i]

    def arrive(self, i, mark):
        self.third[i] = after(self.third[i], mark)
        return self.third[i]

    def result(self, indices, mark, **place):
        theirs = after([self.third[i] for i in indices], mark)
        sizes = tuple(self.finals[i].shape[0] // 128 * 128 for i in indices)
        return choose(self.flag, [self.finals[i] for i in indices], theirs, sizes, **place)

    def decode(self, mark):
        self.third[0] = after(self.third[0], mark)
        return decode(self.flag, self.finals[0], self.third[0])


def rotation_tables(positions):
    half = ROT // 2
    frequency = jnp.exp(
        -jnp.log(10000.0) * jnp.arange(half, dtype=jnp.int32).astype(f32) * 2.0 / ROT
    )
    angle = frequency[:, None] * positions.astype(f32)[None, :]
    lane = lax.broadcasted_iota(jnp.int32, (half, PAIR), 1) % HD
    pick = lax.broadcasted_iota(jnp.int32, (half, PAIR), 0) == lane % half
    pick = (pick & (lane < ROT)).astype(f32)
    spread = lambda v: lax.dot_general(
        v, pick, TN, precision=lax.Precision.HIGHEST, preferred_element_type=f32
    )
    plain = (jnp.arange(PAIR, dtype=jnp.int32) % HD >= ROT).astype(f32)
    return spread(jnp.cos(angle)) + plain, spread(jnp.sin(angle))


def body(
    contexts,
    tokens,
    cotangent,
    segments,
    positions,
    parents,
    block_lists,
    project_weight,
    project_bias,
    dense_weight,
    dense_bias,
    up_weight,
    up_bias,
    down_weight,
    down_bias,
    first_gain,
    first_shift,
    second_gain,
    second_shift,
):
    rows, width = tokens.shape
    blocks = rows // BLK
    me = lax.axis_index("fsdp")
    split = contexts == 2
    slots = contexts * blocks
    first_slot = lax.axis_index("context") * blocks
    step = jnp.arange(10, dtype=jnp.int32)
    flip = jnp.where(step < 4, step, jnp.where(step < 6, 2 * step - 7, 2 * step - 12))
    ids = jnp.where(step < 8, me ^ flip, jnp.where(step == 8 if split else step < 8, 0, first_slot))
    if not split:
        ids = jnp.where(step == 9, 0, ids)
    ids = ids.astype(jnp.int32)

    blocks_of = lambda w: w.reshape(SHARD, -1, SHARD).transpose(1, 0, 2)
    units = up_bias.shape[0]
    near = lambda v: swap(v, "fsdp", 4, 1)
    far = lambda v: swap(v, "fsdp", 4, 2)
    wp = blocks_of(project_weight).reshape(-1, SHARD)
    up = blocks_of(up_weight).reshape(-1, SHARD)
    wp_far, up_far = far(wp), far(up)
    tables = rotation_tables(positions)
    normed_one = norm(tokens, first_gain[None], first_shift[None])
    wp_far = after(wp_far, tables, ids, normed_one, up)
    projects = (wp, near(wp), wp_far, near(wp_far))
    q0, q1, kv0, kv1 = project(ids, normed_one, projects, project_bias, tables)
    down = jnp.concatenate(after([down_weight, dense_weight], kv1), axis=0)
    down_far = far(down)
    if split:
        other0, other1 = swap(kv0, "context", 2, 1), swap(kv1, "context", 2, 1)
        keys = ((kv0, other0), (kv1, other1))
        state0 = attend_forward(ids, block_lists, slots, after(q0, kv1), kv0, 0, None, False)
        state1 = attend_forward(ids, block_lists, slots, after(q1, state0), kv1, 0, None, False)
        up_far = after(up_far, state1)
        ups = (up, near(up), up_far, near(up_far))
        o0, lse0 = attend_forward(
            ids, block_lists, slots, after(q0, up_far), other0, blocks, state0, True
        )
        normed_two, activated, slope = mlp_up(
            ids, after(tokens, o0), second_gain[None], second_shift[None], up_bias[None], ups
        )
        o1, lse1 = attend_forward(
            ids, block_lists, slots, after(q1, activated), other1, blocks, state1, True, 10
        )
        down_far = after(down_far, activated)
    else:
        keys = [(lax.all_gather(kv, "context", axis=0, tiled=True),) for kv in (kv0, kv1)]
        o0, lse0 = attend_forward(ids, block_lists, slots, q0, keys[0][0], 0, None, True)
        o1, lse1 = attend_forward(ids, block_lists, slots, q1, keys[1][0], 0, None, True)
        ups = (up, near(up), up_far, near(up_far))
        normed_two, activated, slope = mlp_up(
            ids, tokens, second_gain[None], second_shift[None], up_bias[None], ups
        )
    downs = (down, near(down), down_far, near(down_far))
    made = mlp_down(ids, activated, cotangent, downs, o0, o1)
    context_low, g0, g1 = made[2:]
    half = rows // 2

    out = LineSum(
        made[:2],
        [
            partial(
                finish, finish_out_kernel, "finish_out", start, half, 1,
                (tokens, dense_bias[None], down_bias[None]),
            )
            for start in (0, half)
        ],
    )
    back0 = attend_backward(ids, block_lists, q0, g0, o0, lse0, tables, keys[0])
    back1 = attend_backward(ids, block_lists, q1, after(g1, back0), o1, lse1, tables, keys[1])
    if split:
        grads = []
        for own, other, _ in (back0, back1):
            grads += [own, swap(other, "context", 2, 1)]
    else:
        grads = [
            lax.psum_scatter(whole_grad, "context", scatter_dimension=0, tiled=True)
            for whole_grad, _ in (back0, back1)
        ]
    mark = out.add(0, (back1, grads[1]) if split else back1)
    hidden_grad, e2, sums = mlp_backward(
        ids, tokens, after(cotangent, mark),
        second_gain[None], slope, ups + downs,
    )
    made = input_grad(
        ids, tokens, e2, first_gain[None], sums, (back0[-1], back1[-1]),
        tables, projects, grads, split,
    )
    projected_grad, sums = made[2:]
    line = LineSum(
        made[:2],
        [
            partial(
                finish, partial(finish_in_kernel, half), "finish_in", start, half, 2,
                (tokens, cotangent),
            )
            for start in (0, half)
        ],
    )
    mark = out.add(1, made[0])
    mark = out.end(0, mark)
    mlp_keep, *mlp_send = weight_parts(
        mlp_weights_kernel, "mlp_weights", ids, 2 * units,
        activated, cotangent, normed_two, after(hidden_grad, mark),
    )
    mark = mlp_keep
    mlp_got = swap(mlp_send, "fsdp", 4, 1)
    mark = line.add(0, mark)
    mark = out.end(1, mark)
    mark = out.arrive(0, mark)
    mlp_here, mlp_there = halves(mlp_keep, after(mlp_got, mark), micros=0)
    mlp_got = swap(mlp_there, "fsdp", 4, 2)
    mark = mlp_here
    rest_keep, *rest_send = weight_parts(
        rest_weights_kernel, "rest_weights", ids, 4 * SHARD,
        context_low, cotangent, normed_one, after(projected_grad, mark),
    )
    rest_got = swap(rest_send, "fsdp", 4, 1)
    mark = rest_keep
    mark = line.add(1, mark)
    mark = line.end(0, mark)
    mark = out.arrive(1, mark)
    mlp_part = add(mlp_here, after(mlp_got, mark))
    if split:
        mlp_got = swap(mlp_part, "context", 2, 1)
    rest_here, rest_there = halves(rest_keep, after(rest_got, mlp_part))
    rest_got = swap(rest_there, "fsdp", 4, 2)
    mark = line.end(1, rest_here)
    rest_part = add(rest_here, after(rest_got, mark))
    if split:
        rest_got = swap(rest_part, "context", 2, 1)
    mark = rest_part
    norms = line.decode(mark)
    sums = jnp.concatenate([norms[0:2], sums[2:4], norms[2:4], sums[6:8]], axis=0)
    mark = sums
    for step in [("fsdp", 4, 1), ("fsdp", 4, 2)]:
        sums = mark = add(sums, swap(after(sums, mark), *step), f32)
    hop = swap(sums, "context", contexts, 1)
    layer_out = mark = out.result([0, 1], mark)
    tokens_grad = mark = line.result([0], mark, total=rows)
    if split:
        down_grad, up_grad = call(
            mlp_last_kernel, "mlp_last", (mlp_part, after(mlp_got, mark)),
            [((units, SHARD), f32), ((SHARD, units), f32)],
        )
        dense_grad, project_grad = call(
            rest_last_kernel, "rest_last", (rest_part, after(rest_got, down_grad)),
            [((SHARD, SHARD), f32), ((3, SHARD, SHARD), f32)],
        )
        mark = dense_grad
        project_grad = project_grad.transpose(1, 0, 2)
    else:
        mlp_part, rest_part = lax.psum(
            (mlp_part.astype(f32), rest_part.astype(f32)), "context"
        )
        back_blocks = lambda g: g.reshape(-1, SHARD, SHARD).transpose(1, 0, 2)
        down_grad = mlp_part[:units]
        up_grad = back_blocks(mlp_part[units:]).reshape(SHARD, units)
        dense_grad = rest_part[:SHARD]
        project_grad = back_blocks(rest_part[SHARD:])
    sums = mark = add(sums, after(hop, mark), f32)
    for i in range(1, contexts.bit_length() - 1):
        sums = mark = add(sums, swap(after(sums, mark), "context", contexts, 1 << i), f32)
    tokens_grad = line.result([1], mark, start=half, total=rows, before=tokens_grad)
    norms = sums
    up_total, bias_sum = sums[2], sums[3]
    project_total = sums[6, : project_bias.size]
    return (
        layer_out,
        tokens_grad,
        project_grad,
        project_total.reshape(3, -1),
        dense_grad,
        bias_sum,
        up_grad,
        up_total,
        down_grad,
        bias_sum,
        norms[4],
        norms[5],
        norms[0],
        norms[1],
    )


def solution(mesh):
    tokens = P(("fsdp", "context"), None)
    line = P(("fsdp", "context"))
    in_specs = (
        tokens, tokens, line, line, P("fsdp", None), tokens,
        P("fsdp", None, "tensor"), P(None, "tensor"), P("tensor", "fsdp"), P(),
        P("fsdp", "tensor"), P("tensor"), P("tensor", "fsdp"), P(), P(), P(), P(), P(),
    )
    out_specs = (
        tokens, tokens, P("fsdp", None, "tensor"), P(None, "tensor"), P("tensor", "fsdp"), P(),
        P("fsdp", "tensor"), P("tensor"), P("tensor", "fsdp"), P(), P(), P(), P(), P(),
    )
    run = partial(body, mesh.shape["context"])
    return jax.shard_map(run, mesh=mesh, in_specs=in_specs, out_specs=out_specs, check_vma=False)
```
